32 devices in a mesh: branch: 8 (over z, x), group: 4 (over y, core).
Axes of the slice: x: 2, y: 2, z: 4, core: 2. Of those that a mesh axis runs over, the one named last changes fastest.
Arguments:
- basis: float32 [2, 32768, 256], P(None, ('branch', 'group')), may hold values from -8 to 8
- spread_owner: int32 [32768, 2], P(('branch', 'group')), may hold values from 0 to 31, all different within a row; in each aligned block of 1024 rows (0 to 1023, 1024 to 2047, ...) at most 128 rows name the same one
- spread_row: int32 [32768, 2], P(('branch', 'group')), may hold values from 0 to 1023
- spread_weight: float32 [32768, 2], P(('branch', 'group')), may hold values from 0.2 to 1
- gram_term: bfloat16 [64, 512, 512], P(('branch', 'group')), may hold values from -0.25 to 0.25
- near_block: bfloat16 [64, 8, 512, 512], P(('branch', 'group')), may hold values from -0.09375 to 0.09375
- near_list: int32 [64, 8], P(('branch', 'group')), may hold values from 0 to 1
- leaf_basis: bfloat16 [64, 64, 512], P(('branch', 'group')), may hold values from -0.25 to 0.25
- far_block: bfloat16 [64, 16, 64, 64], P(('branch', 'group')), may hold values from -0.1875 to 0.1875
- far_list: int32 [64, 16], P(('branch', 'group')), may hold values from 0 to 15
- ascend: bfloat16 [64, 64, 64], P(('branch', 'group')), may hold values from -0.1875 to 0.1875
- descend: bfloat16 [64, 64, 64], P(('branch', 'group')), may hold values from -0.75 to 0.75
- top_block: bfloat16 [256, 256], P('group'), may hold values from -0.375 to 0.375
Outputs:
- next_vector: float32 [32768, 256], P(('branch', 'group'))
- hessenberg: float32 [3, 256], replicated
The draws below stay inside these ranges and needn't reach their ends.
Inputs may be any that keep to these rules, and one draw needn't show every extreme that they name: `spread_owner`: within the rows of one device no owner is named by more than 128 entries, and one row never names an owner twice.
All inputs are finite; a program needn't handle non-finite values.
Results may differ from the reference program's by a relative error of at most 0.0035.
Values may be sent and summed in bfloat16 or wider, within the bound.
No kernel may reach another device: no remote copies, remote signals or barrier semaphores. Data moves between devices by JAX's collectives and lax.ppermute only.
A program may use at most 64 MiB of HBM per device.

```python
import math
import jax
import jax.numpy as jnp
import numpy as np
from jax import lax

LEAF = 512
RANK = 64
C = 256
NEAR = 8
KFAR = 16
KRY = 2
SPREAD = 2
LEAVES = 2
ROWS_DEV = 1024
ROWS = 32768
LEAVES_ALL = 64
MOST = 128
GROUPS = 4
N_BRANCH = 8
N_GROUP = 4
DEVICES = 32


def draw_basis(key, part):
    shared_key, own_key = jax.random.split(jax.random.fold_in(key, 7), 2)
    full_shape = (KRY, ROWS, C)
    shared = jax.random.normal(shared_key, (1, ROWS, C), jnp.float32)
    own_part = jax.random.normal(own_key, full_shape, jnp.float32)
    values = 0.6 * shared + 0.8 * own_part
    return jnp.clip(values, -8.0, 8.0).astype(jnp.float32)


def touch_ends(array, key, least, top_value):
    longest = array.shape.index(max(array.shape))
    spots = []
    for shift in (0, 1):
        where = [jax.random.randint(jax.random.fold_in(key, axis), (), 0, length) for axis, length in enumerate(array.shape)]
        where[longest] = (where[longest] + shift) % array.shape[longest]
        spots.append(tuple(where))
    return array.at[spots[0]].set(least).at[spots[1]].set(top_value)


def level_of(stream_key, extent, cuts, low, top_value):
    gain = 1.0
    for axis_at, parts in cuts:
        heights = jax.random.uniform(jax.random.fold_in(jax.random.fold_in(stream_key, 6), axis_at), (parts,), jnp.float32, low / len(cuts), top_value / len(cuts))
        gain = gain * jnp.repeat(jnp.exp(heights), extent[axis_at] // parts).reshape((-1,) + (1,) * (len(extent) - 1 - axis_at))
    return gain


def routed_block(key, own, number, rows, number_of, top, reach, slope):
    order = jax.random.permutation(key, number_of)
    packed, usual = portions_of(number_of, rows * top, reach, slope, True), portions_of(number_of, rows * top, reach, slope, False)
    places = jnp.arange(number_of)

    def named(lengths, rotation):
        used = int((lengths > 0).sum())
        fixed = max(1, used // 4)
        moved = fixed + (places - fixed + rotation * (used - fixed)) % max(1, number_of - fixed)
        return jnp.zeros((number_of,), jnp.int32).at[order[jnp.where(places < fixed, places, moved)]].set(jnp.asarray(lengths, jnp.int32))

    lengths = jnp.where(number % 4 == 0, named(packed, number // 4), named(usual, number - number // 4 - 1))
    mixed = jax.random.permutation(jax.random.fold_in(own, 3), number_of)
    donor, taker = mixed[0:number_of // 2 * 2:2], mixed[1:number_of // 2 * 2:2]
    margin = jnp.minimum(lengths[donor] - 1, reach - lengths[taker]) // 2
    margin = jnp.where((donor == order[0]) | (taker == order[0]) | (lengths[taker] == 0), 0, jnp.maximum(margin, 0))
    moved = jax.random.randint(jax.random.fold_in(own, 4), (number_of // 2,), 0, 1 << 20) % (margin + 1)
    lengths = lengths.at[donor].add(-moved).at[taker].add(moved)
    items = jnp.searchsorted(jnp.cumsum(lengths), jnp.arange(rows * top), side="right").astype(jnp.int32)
    listing = items.reshape(top, rows).T
    listing = listing[jax.random.permutation(jax.random.fold_in(own, 1), rows)]
    rotation = jax.random.randint(jax.random.fold_in(own, 2), (rows, 1), 0, top)
    return jnp.take_along_axis(listing, (jnp.arange(top)[None, :] + rotation) % top, axis=1)


def portions_of(number_of, total, most, slope, full):
    portions = [(1 << 20) // math.isqrt(standing ** slope) + 1 for standing in range(1, number_of + 1)]
    largest = most if full else min(most, max(-(-total // number_of), total * portions[0] // sum(portions)))
    least = 1 if total - largest >= number_of - 1 else 0
    given, surplus = [largest] + [least] * (number_of - 1), total - largest - least * (number_of - 1)
    while surplus > 0:
        movable = [i for i in range(1, number_of) if given[i] < largest] or [i for i in range(1, number_of) if given[i] < most]
        mass, budget = sum([portions[i] for i in movable]), surplus
        for i in movable:
            more = min(most - given[i], max(1, budget * portions[i] // mass), surplus)
            given[i] = given[i] + more
            surplus = surplus - more
    return np.array(given)


def gaussian(rng, shape, scale, limit, pieces=(), held_as=jnp.bfloat16):
    drawn = scale * jax.random.normal(rng, shape, jnp.float32)
    if pieces:
        drawn = drawn * level_of(rng, shape, pieces, -0.22, 0.18)
    return jnp.clip(drawn, -limit, limit).astype(held_as)


def setup_inputs(seed: int = 0) -> dict:
    key_list = jax.random.split(jax.random.key(seed), 14)
    basis = draw_basis(jax.random.fold_in(key_list[13], 71), 0)
    spread_owner_keys = jax.random.split(jax.random.fold_in(key_list[1], 1), ROWS // ROWS_DEV)
    spread_owner_turns = jax.random.permutation(jax.random.fold_in(key_list[1], 3), ROWS // ROWS_DEV)
    spread_owner = jax.vmap(lambda own, number: routed_block(jax.random.fold_in(key_list[1], 2), own, number, ROWS_DEV, DEVICES, SPREAD, MOST, 2))(spread_owner_keys, spread_owner_turns).reshape((ROWS, SPREAD))
    spread_row = touch_ends(jax.random.randint(key_list[2], (ROWS, SPREAD), 0, ROWS_DEV), jax.random.fold_in(key_list[2], 1), 0, ROWS_DEV - 1).astype(jnp.int32)
    spread_weight = jnp.clip(0.2 + 0.8 * jax.random.uniform(key_list[3], (ROWS, SPREAD), jnp.float32) ** level_of(key_list[3], (ROWS, SPREAD), ((0, 32),), -0.2, 0.2), 0.2, 1.0)
    gram_term = gaussian(key_list[4], (LEAVES_ALL, LEAF, LEAF), LEAF ** -0.5, 0.25, ((0, 32),))
    near_block = gaussian(key_list[5], (LEAVES_ALL, NEAR, LEAF, LEAF), (LEAF * NEAR) ** -0.5, 0.09375, ((0, 32),))
    near_list = touch_ends(jax.random.randint(key_list[6], (LEAVES_ALL, NEAR), 0, LEAVES), jax.random.fold_in(key_list[6], 1), 0, LEAVES - 1).astype(jnp.int32)
    leaf_basis = gaussian(key_list[7], (LEAVES_ALL, RANK, LEAF), LEAF ** -0.5, 0.25, ((0, 32),))
    far_block = gaussian(key_list[8], (LEAVES_ALL, KFAR, RANK, RANK), (RANK * KFAR) ** -0.5, 0.1875, ((0, 32),))
    far_list = touch_ends(jax.random.randint(key_list[9], (LEAVES_ALL, KFAR), 0, N_BRANCH * LEAVES), jax.random.fold_in(key_list[9], 1), 0, (N_BRANCH * LEAVES) - 1).astype(jnp.int32)
    ascend = gaussian(key_list[10], (LEAVES_ALL, RANK, RANK), (RANK * LEAVES * N_BRANCH) ** -0.5, 0.1875, ((0, 32),))
    descend = gaussian(key_list[11], (LEAVES_ALL, RANK, RANK), RANK ** -0.5, 0.75, ((0, 32),))
    top_block = gaussian(key_list[12], (GROUPS * RANK, GROUPS * RANK), (GROUPS * RANK) ** -0.5, 0.375, ((0, 4),))
    return dict(basis=basis, spread_owner=spread_owner, spread_row=spread_row, spread_weight=spread_weight, gram_term=gram_term, near_block=near_block, near_list=near_list, leaf_basis=leaf_basis, far_block=far_block, far_list=far_list, ascend=ascend, descend=descend, top_block=top_block)


HIGHEST_PRECISION = lax.Precision.HIGHEST

def product(pattern, first_op, second_op):
    return jnp.einsum(pattern, first_op.astype(jnp.float32), second_op.astype(jnp.float32), precision=HIGHEST_PRECISION)

def reference(basis, spread_owner, spread_row, spread_weight, gram_term, near_block, near_list, leaf_basis, far_block, far_list, ascend, descend, top_block):
    devices = N_BRANCH * N_GROUP
    rows_dev = LEAVES * LEAF
    columns = basis.shape[2]
    vector = basis[KRY - 1]
    target = spread_owner * rows_dev + spread_row
    dual_in = jnp.zeros((devices * rows_dev, columns), jnp.float32)
    for spread_at in range(SPREAD):
        dual_in = dual_in.at[target[:, spread_at]].add(spread_weight[:, spread_at, None] * vector)
    dual_low = dual_in.astype(jnp.bfloat16).reshape(devices, LEAVES, LEAF, columns)
    dual_split = dual_in.reshape(devices, LEAVES, LEAF, columns)
    gram_split = gram_term.reshape(devices, LEAVES, LEAF, LEAF)
    near_split = near_block.reshape(devices, LEAVES, NEAR, LEAF, LEAF)
    near_index = near_list.reshape(devices, LEAVES, NEAR)
    basis_split = leaf_basis.reshape(devices, LEAVES, RANK, LEAF)

    def upward(operands):
        dual_dev, low_dev, gram_dev, near_dev, index_dev, base_dev = operands
        first_pass = dual_dev + product('lji,ljc->lic', gram_dev, low_dev)
        first_low = first_pass.astype(jnp.bfloat16)
        near_sum = product('lkij,lkjc->lic', near_dev, first_low[index_dev])
        leaf_coeff = product('lri,lic->lrc', base_dev, first_low)
        return (first_pass, near_sum, leaf_coeff)
    first_pass, near_sum, leaf_coeff = lax.map(upward, (dual_split, dual_low, gram_split, near_split, near_index, basis_split))
    coeff_low = leaf_coeff.astype(jnp.bfloat16).reshape(N_BRANCH, N_GROUP, LEAVES, RANK, columns)
    ascend_split = ascend.reshape(N_BRANCH, N_GROUP, LEAVES, RANK, RANK)
    parent = product('bglrs,bglsc->grc', ascend_split, coeff_low)
    parent_low = parent.astype(jnp.bfloat16).reshape(N_GROUP * RANK, columns)
    top_field = jnp.dot(top_block, parent_low, preferred_element_type=jnp.float32)
    field_low = top_field.astype(jnp.bfloat16).reshape(N_GROUP, RANK, columns)
    by_group = jnp.transpose(coeff_low, (1, 0, 2, 3, 4)).reshape(N_GROUP, N_BRANCH * LEAVES, RANK, columns)
    far_split = far_block.reshape(devices, LEAVES, KFAR, RANK, RANK)
    far_index = far_list.reshape(devices, LEAVES, KFAR)
    descend_split = descend.reshape(devices, LEAVES, RANK, RANK)
    group_ids = (jnp.arange(devices, dtype=jnp.int32) % N_GROUP).astype(jnp.int32)

    def downward(operands):
        first_dev, near_dev, gram_dev, base_dev, far_dev, index_dev, desc_dev, group_id = operands
        sources = by_group[group_id][index_dev]
        far_sum = product('lkrs,lksc->lrc', far_dev, sources)
        descent = far_sum + product('lrs,sc->lrc', desc_dev, field_low[group_id])
        dual_image = first_dev + near_dev + product('lri,lrc->lic', base_dev, descent.astype(jnp.bfloat16))
        return dual_image + product('lij,ljc->lic', gram_dev, dual_image.astype(jnp.bfloat16))
    dual_out = lax.map(downward, (first_pass, near_sum, gram_split, basis_split, far_split, far_index, descend_split, group_ids))
    dual_out = dual_out.reshape(devices * rows_dev, columns)
    image_primal = jnp.zeros((devices * rows_dev, columns), jnp.float32)
    for spread_at in range(SPREAD):
        image_primal = image_primal + spread_weight[:, spread_at, None] * dual_out[target[:, spread_at]]
    total_rows = devices * rows_dev
    projection = lax.optimization_barrier(jnp.sum(basis * image_primal[None], axis=1)) / total_rows
    remainder = image_primal - lax.optimization_barrier(jnp.sum(projection[:, None, :] * basis, axis=0))
    square = lax.optimization_barrier(jnp.sum(remainder * remainder, axis=0)) / total_rows
    norm_scale = jnp.sqrt(square + 1e-06)
    return (remainder / norm_scale, jnp.concatenate([projection, norm_scale[None]], axis=0))
```

```python
import functools

import jax
import jax.numpy as jnp
from jax import lax
from jax.experimental import pallas as pl
from jax.experimental.pallas import tpu as pltpu
from jax.sharding import PartitionSpec as P

F32 = jnp.float32
LOW = jnp.bfloat16
CODE = jnp.int16
TOP = 32767.0
REST = 65534.0
LOG2 = 0.6931471805599453
BLOCK = 512
VMEM_LIMIT = 24 << 20


def rounded(values):
    return values.astype(LOW)


def contract(pattern, first_op, second_op):
    return jnp.einsum(pattern, first_op, second_op, preferred_element_type=F32)


def dot(lhs, rhs, lhs_dim=1, rhs_dim=0):
    return lax.dot_general(
        lhs, rhs, (((lhs_dim,), (rhs_dim,)), ((), ())), preferred_element_type=F32
    )


def params(semantics=None):
    return pltpu.CompilerParams(dimension_semantics=semantics, vmem_limit_bytes=VMEM_LIMIT)


def whole(shape):
    zeros = (0,) * len(shape)
    return pl.BlockSpec(shape, lambda *_: zeros)


def cost(flops, nbytes):
    return pl.CostEstimate(flops=int(flops), bytes_accessed=int(nbytes), transcendentals=0)


def column(row):
    size = row.shape[1]
    same = lax.broadcasted_iota(jnp.int32, (size, size), 0) == lax.broadcasted_iota(
        jnp.int32, (size, size), 1
    )
    return jnp.sum(jnp.where(same, row, 0.0), axis=1, keepdims=True)


def split(code):
    high = jnp.round(code * (1.0 / 256.0))
    return high, code - 256.0 * high


def route_kernel(slots, owner_ref, row_ref, weight_ref, rank_ref, side_ref, place_ref):
    devices, rows_dev = rank_ref.shape
    spread = owner_ref.shape[0]
    width = side_ref.shape[2]
    ids = lax.broadcasted_iota(jnp.int32, (devices, rows_dev), 0)
    named = [owner_ref[s : s + 1, :] == ids for s in range(spread)]
    chosen = functools.reduce(jnp.logical_or, named)
    flag = jnp.where(chosen, 1.0, 0.0)
    lane = 128
    upper = jnp.where(
        lax.broadcasted_iota(jnp.int32, (lane, lane), 0)
        <= lax.broadcasted_iota(jnp.int32, (lane, lane), 1),
        1.0,
        0.0,
    ).astype(LOW)
    before = jnp.zeros((devices, 1), F32)
    pieces = []
    for start in range(0, rows_dev, lane):
        part = flag[:, start : start + lane]
        upto = dot(part.astype(LOW), upper)
        pieces.append(upto - part + before)
        before = before + upto[:, lane - 1 : lane]
    rank = jnp.concatenate(pieces, axis=1)
    rank_ref[...] = jnp.where(chosen, rank, -1.0)
    slot_ids = lax.broadcasted_iota(jnp.int32, (width, rows_dev), 0).astype(F32)
    place_ref[...] = jnp.zeros_like(place_ref)
    total = jnp.zeros((6 * devices, width), F32)
    for s in range(spread):
        slot = jnp.sum(jnp.where(named[s], rank, 0.0), axis=0, keepdims=True)
        place_ref[s : s + 1, :] = owner_ref[s : s + 1, :].astype(F32) * slots + slot
        weight = weight_ref[s : s + 1, :]
        place_ref[spread + s : spread + s + 1, :] = weight
        code = weight * TOP
        whole_code = jnp.round(code)
        rest_code = jnp.round((code - whole_code) * REST)
        fields = split(row_ref[s : s + 1, :].astype(F32)) + split(whole_code) + split(rest_code)
        lhs = jnp.concatenate([jnp.where(named[s], f, 0.0) for f in fields], axis=0).astype(LOW)
        total = total + dot(lhs, jnp.where(slot_ids == slot, 1.0, 0.0).astype(LOW), 1, 1)
    for i in range(3):
        high = total[2 * i * devices : (2 * i + 1) * devices]
        low = total[(2 * i + 1) * devices : (2 * i + 2) * devices]
        side_ref[i] = 256.0 * high + low


def route(owner_t, row_t, weight_t, devices, slots, width):
    rows_dev = owner_t.shape[1]
    return pl.pallas_call(
        functools.partial(route_kernel, slots),
        out_shape=(
            jax.ShapeDtypeStruct((devices, rows_dev), F32),
            jax.ShapeDtypeStruct((3, devices, width), F32),
            jax.ShapeDtypeStruct((8, rows_dev), F32),
        ),
        compiler_params=params(),
        cost_estimate=cost(1e8, 1 << 19),
        name="route",
    )(owner_t, row_t, weight_t)


def spread_kernel(slots, vector_ref, rank_ref, side_ref, *refs):
    outs, (code_ref, level_ref, pick_ref) = refs[:-3], refs[-3:]
    step = pl.program_id(0)
    columns = vector_ref.shape[2]

    @pl.when(step == 0)
    def _():
        vector = vector_ref[0]
        peak = jnp.maximum(jnp.max(jnp.abs(vector), axis=0, keepdims=True), 1e-30)
        level = jnp.floor(jnp.log(peak) * (1.0 / LOG2)) + 1.0
        level_ref[...] = level
        code = jnp.clip(jnp.round(vector * (TOP / jnp.exp(level * LOG2))), -TOP, TOP)
        high, low = split(code)
        code_ref[:, :columns] = high.astype(LOW)
        code_ref[:, columns:] = low.astype(LOW)

    rows_dev = rank_ref.shape[1]
    owners = BLOCK // slots
    slot_ids = lax.broadcasted_iota(jnp.int32, (slots, rows_dev), 0).astype(F32)
    for j in range(owners):
        rank = rank_ref[pl.ds(step * owners + j, 1), :]
        pick_ref[j * slots : (j + 1) * slots, :] = jnp.where(slot_ids == rank, 1.0, 0.0).astype(LOW)
    picked = dot(pick_ref[...], code_ref[...])
    codes = (256.0 * picked[:, :columns] + picked[:, columns:]).astype(jnp.int32).astype(CODE)
    for i, out_ref in enumerate(outs):
        width = out_ref.shape[2]
        at = slice(i * width, (i + 1) * width)
        line = lax.broadcasted_iota(jnp.int32, (8, width), 0)
        for j in range(owners):
            extra = jnp.where(line == 3, level_ref[:, at], 0.0)
            for k in range(3):
                extra = jnp.where(line == k, side_ref[k, pl.ds(step * owners + j, 1), :], extra)
            out_ref[j, :slots, :] = codes[j * slots : (j + 1) * slots, at]
            out_ref[j, slots:, :] = extra.astype(jnp.int32).astype(CODE)


def spread_out(basis, rank, side, slots, chunks):
    devices, rows_dev = rank.shape
    last, columns = basis.shape[0] - 1, basis.shape[2]
    owners = BLOCK // slots
    width = columns // chunks
    shape = (devices, slots + 8, width)
    return pl.pallas_call(
        functools.partial(spread_kernel, slots),
        grid=(devices // owners,),
        in_specs=[
            pl.BlockSpec((1, rows_dev, columns), lambda i: (last, 0, 0)),
            whole(rank.shape),
            whole(side.shape),
        ],
        out_specs=[pl.BlockSpec((owners,) + shape[1:], lambda i: (i, 0, 0))] * chunks,
        out_shape=[jax.ShapeDtypeStruct(shape, CODE)] * chunks,
        scratch_shapes=[
            pltpu.VMEM((rows_dev, 2 * columns), LOW),
            pltpu.VMEM((1, columns), F32),
            pltpu.VMEM((BLOCK, rows_dev), LOW),
        ],
        compiler_params=params(("arbitrary",)),
        cost_estimate=cost(4 * devices * slots * rows_dev * columns, 4 << 20),
        name="spread_out",
    )(basis, rank, side)


def collect_kernel(
    slots, got_ref, gram_ref, base_ref, first_ref, low_ref, coeff_ref, rows_ref, sum_ref, pick_ref, term_ref
):
    step = pl.program_id(0)
    rows_dev, width = first_ref.shape
    owners = got_ref.shape[0]
    ids = lax.broadcasted_iota(jnp.int32, (rows_dev, slots), 0).astype(F32)
    for j in range(owners):
        at = slice(j * slots, (j + 1) * slots)
        extra = got_ref[j, slots:, :].astype(jnp.int32).astype(F32)
        row = extra[0:1, :slots]
        weight = (extra[1:2, :slots] + extra[2:3, :slots] * (1.0 / REST)) * (1.0 / TOP)
        scale = jnp.exp(extra[3:4, :] * LOG2) * (1.0 / TOP)
        rows_ref[pl.ds(step * owners + j, 1), :] = extra[0:1, :]
        values = got_ref[j, :slots, :].astype(jnp.int32).astype(F32) * column(weight) * scale
        high = values.astype(LOW)
        term_ref[at, :width] = high
        term_ref[at, width:] = (values - high.astype(F32)).astype(LOW)
        pick_ref[:, at] = jnp.where(ids == row, 1.0, 0.0).astype(LOW)
    added = dot(pick_ref[...], term_ref[...])

    @pl.when(step == 0)
    def _():
        sum_ref[...] = added

    @pl.when(step > 0)
    def _():
        sum_ref[...] += added

    @pl.when(step == pl.num_programs(0) - 1)
    def _():
        leaves, leaf = gram_ref.shape[:2]
        rank = base_ref.shape[1]
        for l in range(leaves):
            at = slice(l * leaf, (l + 1) * leaf)
            dual = sum_ref[at, :width] + sum_ref[at, width:]
            first = dual + dot(gram_ref[l], dual.astype(LOW), 0, 0)
            low = first.astype(LOW)
            first_ref[at, :] = first
            low_ref[l] = low
            coeff_ref[l * rank : (l + 1) * rank, :] = dot(base_ref[l], low).astype(LOW)


def collect(got, gram, base):
    devices, slots, width = got.shape[0], got.shape[1] - 8, got.shape[2]
    leaves, leaf = gram.shape[:2]
    rank = base.shape[1]
    rows_dev = leaves * leaf
    owners = BLOCK // slots
    return pl.pallas_call(
        functools.partial(collect_kernel, slots),
        grid=(devices // owners,),
        in_specs=[
            pl.BlockSpec((owners,) + got.shape[1:], lambda i: (i, 0, 0)),
            whole(gram.shape),
            whole(base.shape),
        ],
        out_specs=(
            whole((rows_dev, width)),
            whole((leaves, leaf, width)),
            whole((leaves * rank, width)),
            whole((devices, width)),
        ),
        out_shape=(
            jax.ShapeDtypeStruct((rows_dev, width), F32),
            jax.ShapeDtypeStruct((leaves, leaf, width), LOW),
            jax.ShapeDtypeStruct((leaves * rank, width), LOW),
            jax.ShapeDtypeStruct((devices, width), F32),
        ),
        scratch_shapes=[
            pltpu.VMEM((rows_dev, 2 * width), F32),
            pltpu.VMEM((rows_dev, BLOCK), LOW),
            pltpu.VMEM((BLOCK, 2 * width), LOW),
        ],
        compiler_params=params(("arbitrary",)),
        cost_estimate=cost(4 * devices * slots * rows_dev * width, 4 << 20),
        name="collect",
    )(got, gram, base)


def near_kernel(list_ref, block_ref, low_ref, first_ref, out_ref):
    leaf, item = pl.program_id(0), pl.program_id(1)
    count = block_ref.shape[1]
    term = dot(block_ref[0, 0], low_ref[list_ref[leaf, item * count]])
    for k in range(1, count):
        term = term + dot(block_ref[0, k], low_ref[list_ref[leaf, item * count + k]])

    @pl.when(item == 0)
    def _():
        out_ref[...] = first_ref[...] + term

    @pl.when(item > 0)
    def _():
        out_ref[...] += term


def near_field(near_list, near_block, low, first):
    leaves, items, leaf = near_block.shape[:3]
    width = low.shape[2]
    count = 4 if items % 4 == 0 else 1
    return pl.pallas_call(
        near_kernel,
        grid_spec=pltpu.PrefetchScalarGridSpec(
            num_scalar_prefetch=1,
            grid=(leaves, items // count),
            in_specs=[
                pl.BlockSpec((1, count, leaf, leaf), lambda l, k, _: (l, k, 0, 0)),
                whole(low.shape),
                pl.BlockSpec((leaf, width), lambda l, k, _: (l, 0)),
            ],
            out_specs=pl.BlockSpec((leaf, width), lambda l, k, _: (l, 0)),
        ),
        out_shape=jax.ShapeDtypeStruct(first.shape, F32),
        compiler_params=params(("arbitrary", "arbitrary")),
        cost_estimate=cost(2 * near_block.size * width, 2 * near_block.size),
        name="near_field",
    )(near_list, near_block, low, first)


def reply_kernel(
    slots,
    image_ref,
    far_ref,
    top_ref,
    parents_ref,
    descend_ref,
    base_ref,
    gram_ref,
    rows_ref,
    out_ref,
    dual_ref,
    pick_ref,
):
    step = pl.program_id(0)

    @pl.when(step == 0)
    def _():
        leaves, leaf = gram_ref.shape[:2]
        field = dot(top_ref[...], parents_ref[...]).astype(LOW)
        for l in range(leaves):
            at = slice(l * leaf, (l + 1) * leaf)
            descent = far_ref[l] + dot(descend_ref[l], field)
            image = image_ref[at, :] + dot(base_ref[l], descent.astype(LOW), 0, 0)
            dual_ref[at, :] = (image + dot(gram_ref[l], image.astype(LOW))).astype(LOW)

    rows_dev = dual_ref.shape[0]
    owners = BLOCK // slots
    ids = lax.broadcasted_iota(jnp.int32, (slots, rows_dev), 1).astype(F32)
    for j in range(owners):
        row = column(rows_ref[pl.ds(step * owners + j, 1), :][:, :slots])
        pick_ref[j * slots : (j + 1) * slots, :] = jnp.where(ids == row, 1.0, 0.0).astype(LOW)
    out_ref[...] = dot(pick_ref[...], dual_ref[...]).astype(LOW)


def reply(image, far, top, parents, descend, base, gram, rows, slots):
    rows_dev, width = image.shape
    steps = rows.shape[0] * slots // BLOCK
    args = (image, far, top, parents, descend, base, gram, rows)
    return pl.pallas_call(
        functools.partial(reply_kernel, slots),
        grid=(steps,),
        in_specs=[whole(a.shape) for a in args],
        out_specs=pl.BlockSpec((BLOCK, width), lambda i: (i, 0)),
        out_shape=jax.ShapeDtypeStruct((steps * BLOCK, width), LOW),
        scratch_shapes=[pltpu.VMEM((rows_dev, width), LOW), pltpu.VMEM((BLOCK, rows_dev), LOW)],
        compiler_params=params(("arbitrary",)),
        cost_estimate=cost(2 * steps * BLOCK * rows_dev * width, 4 << 20),
        name="reply",
    )(*args)


def gather_kernel(spread, ret_ref, place_ref, basis_ref, image_ref, sums_ref):
    step = pl.program_id(0)
    rows = place_ref.shape[0]
    total = ret_ref.shape[0]
    ids = lax.broadcasted_iota(jnp.int32, (rows, total), 1).astype(F32)
    image = jnp.zeros(image_ref.shape, F32)
    for s in range(spread):
        pick = jnp.where(ids == place_ref[:, s : s + 1], 1.0, 0.0).astype(LOW)
        image = image + place_ref[:, spread + s : spread + s + 1] * dot(pick, ret_ref[...])
    image_ref[...] = image
    krylov = basis_ref.shape[0]
    parts = [jnp.sum(basis_ref[k] * image, axis=0, keepdims=True) for k in range(krylov)]
    parts.append(jnp.sum(image * image, axis=0, keepdims=True))
    parts.append(jnp.zeros((sums_ref.shape[0] - krylov - 1, image.shape[1]), F32))
    added = jnp.concatenate(parts, axis=0)

    @pl.when(step == 0)
    def _():
        sums_ref[...] = added

    @pl.when(step > 0)
    def _():
        sums_ref[...] += added


def gather_back(ret, place_col, basis, spread):
    total, width = ret.shape
    krylov, rows_dev = basis.shape[:2]
    rows = 256
    return pl.pallas_call(
        functools.partial(gather_kernel, spread),
        grid=(rows_dev // rows,),
        in_specs=[
            whole(ret.shape),
            pl.BlockSpec((rows, place_col.shape[1]), lambda i: (i, 0)),
            pl.BlockSpec((krylov, rows, width), lambda i: (0, i, 0)),
        ],
        out_specs=(pl.BlockSpec((rows, width), lambda i: (i, 0)), whole((8, width))),
        out_shape=(
            jax.ShapeDtypeStruct((rows_dev, width), F32),
            jax.ShapeDtypeStruct((8, width), F32),
        ),
        compiler_params=params(("arbitrary",)),
        cost_estimate=cost(2 * spread * total * rows_dev * width, 6 << 20),
        name="gather_back",
    )(ret, place_col, basis)


AXES = ("branch", "group")


def exchange(values, axes=AXES):
    return lax.all_to_all(values, axes, split_axis=0, concat_axis=0, tiled=True)


def to_all(values, axes, size):
    return exchange(jnp.broadcast_to(values[None], (size,) + values.shape), axes)


def body(
    basis,
    spread_owner,
    spread_row,
    spread_weight,
    gram_term,
    near_block,
    near_list,
    leaf_basis,
    far_block,
    far_list,
    ascend,
    descend,
    top_block,
):
    branches = lax.axis_size("branch")
    groups = lax.axis_size("group")
    devices = branches * groups
    rows_dev, columns = basis.shape[1:]
    krylov = basis.shape[0]
    spread = spread_owner.shape[1]
    slots = 2 * spread * rows_dev // devices
    total = devices * slots
    leaves, rank = leaf_basis.shape[:2]
    rank_of, side, place = route(
        spread_owner.T, spread_row.T, spread_weight.T, devices, slots, columns
    )
    sent = spread_out(basis, rank_of, side, slots, 1)[0]
    got = exchange(sent)
    ascend_all = to_all(ascend, "branch", branches).reshape((branches * leaves,) + ascend.shape[1:])

    first, low, coeff, rows = collect(got, gram_term, leaf_basis)
    coeff_all = to_all(coeff, "branch", branches).reshape(branches * leaves, rank, columns)
    image = near_field(near_list, near_block, low, first)
    parent = rounded(contract("lrs,lsc->rc", ascend_all, coeff_all))
    parents = lax.all_gather(parent, "group", axis=0, tiled=True)
    far = contract("lkrs,lksc->lrc", far_block, coeff_all[far_list])
    replies = reply(image, far, top_block, parents, descend, leaf_basis, gram_term, rows, slots)
    returned = exchange(replies.reshape(devices, slots, columns)).reshape(total, columns)
    primal, sums = gather_back(returned, place.T, basis, spread)
    pairs = [(i, j) for i in range(krylov) for j in range(i, krylov)]
    mutual = jnp.stack([jnp.sum(basis[i] * basis[j], axis=0) for i, j in pairs])
    sums = jnp.concatenate([sums[: krylov + 1], mutual], axis=0)
    sums = jnp.sum(to_all(sums, AXES, devices), axis=0)
    mutual = sums[krylov + 1 :]

    total_rows = rows_dev * devices
    projection = sums[:krylov] / total_rows
    remainder = primal - jnp.sum(projection[:, None, :] * basis, axis=0)
    square = sums[krylov] / total_rows - 2.0 * jnp.sum(projection * projection, axis=0)
    for at, (i, j) in enumerate(pairs):
        times = 1.0 if i == j else 2.0
        square = square + times * projection[i] * projection[j] * mutual[at] / total_rows
    norm_scale = jnp.sqrt(jnp.maximum(square, 0.0) + 1e-06)
    return (remainder / norm_scale, jnp.concatenate([projection, norm_scale[None]], axis=0))


def solution(mesh):
    both = ("branch", "group")
    return jax.shard_map(
        body,
        mesh=mesh,
        in_specs=(
            P(None, both, None),
            P(both, None),
            P(both, None),
            P(both, None),
            P(both, None, None),
            P(both, None, None, None),
            P(both, None),
            P(both, None, None),
            P(both, None, None, None),
            P(both, None),
            P(both, None, None),
            P(both, None, None),
            P("group", None),
        ),
        out_specs=(P(both, None), P()),
        check_vma=False,
    )
```

```python
import functools

import jax
import jax.numpy as jnp
from jax import lax
from jax.experimental import pallas as pl
from jax.experimental.pallas import tpu as pltpu
from jax.sharding import PartitionSpec as P

F32 = jnp.float32
LOW = jnp.bfloat16
CODE = jnp.int16
TOP = 32767.0
REST = 65534.0
LOG2 = 0.6931471805599453
SPREAD_BLOCK = 1024
COLLECT_BLOCK = 2048
REPLY_BLOCK = 2048
LANES = 128
VMEM_LIMIT = 24 << 20


def rounded(values):
    return values.astype(LOW)


def contract(pattern, first_op, second_op):
    return jnp.einsum(pattern, first_op, second_op, preferred_element_type=F32)


def dot(lhs, rhs, lhs_dim=1, rhs_dim=0):
    return lax.dot_general(
        lhs, rhs, (((lhs_dim,), (rhs_dim,)), ((), ())), preferred_element_type=F32
    )


def params(semantics=None):
    return pltpu.CompilerParams(dimension_semantics=semantics, vmem_limit_bytes=VMEM_LIMIT)


def whole(shape):
    zeros = (0,) * len(shape)
    return pl.BlockSpec(shape, lambda *_: zeros)


def in_hbm(shape, dtype):
    return pltpu.HBM(shape, dtype)


def in_vmem(shape, dtype):
    return pltpu.VMEM(shape, dtype)


def kept(values):
    return pltpu.with_memory_space_constraint(values, pltpu.HBM)


def cost(flops, nbytes):
    return pl.CostEstimate(flops=int(flops), bytes_accessed=int(nbytes), transcendentals=0)


def column(row):
    size = row.shape[1]
    same = lax.broadcasted_iota(jnp.int32, (size, size), 0) == lax.broadcasted_iota(
        jnp.int32, (size, size), 1
    )
    return jnp.sum(jnp.where(same, row, 0.0), axis=1, keepdims=True)


def split(code):
    high = jnp.round(code * (1.0 / 256.0))
    return high, code - 256.0 * high


def route_kernel(slots, owner_ref, row_ref, weight_ref, rank_ref, side_ref, place_ref):
    devices, rows_dev = rank_ref.shape
    spread = owner_ref.shape[0]
    width = side_ref.shape[2]
    ids = lax.broadcasted_iota(jnp.int32, (devices, rows_dev), 0)
    named = [owner_ref[s : s + 1, :] == ids for s in range(spread)]
    chosen = functools.reduce(jnp.logical_or, named)
    flag = jnp.where(chosen, 1.0, 0.0)
    lane = 128
    upper = jnp.where(
        lax.broadcasted_iota(jnp.int32, (lane, lane), 0)
        <= lax.broadcasted_iota(jnp.int32, (lane, lane), 1),
        1.0,
        0.0,
    ).astype(LOW)
    before = jnp.zeros((devices, 1), F32)
    pieces = []
    for start in range(0, rows_dev, lane):
        part = flag[:, start : start + lane]
        upto = dot(part.astype(LOW), upper)
        pieces.append(upto - part + before)
        before = before + upto[:, lane - 1 : lane]
    rank = jnp.concatenate(pieces, axis=1)
    rank_ref[...] = jnp.where(chosen, rank, -1.0)
    slot_ids = lax.broadcasted_iota(jnp.int32, (width, rows_dev), 0).astype(F32)
    place_ref[...] = jnp.zeros_like(place_ref)
    total = jnp.zeros((6 * devices, width), F32)
    for s in range(spread):
        slot = jnp.sum(jnp.where(named[s], rank, 0.0), axis=0, keepdims=True)
        place_ref[s : s + 1, :] = owner_ref[s : s + 1, :].astype(F32) * slots + slot
        weight = weight_ref[s : s + 1, :]
        place_ref[spread + s : spread + s + 1, :] = weight
        code = weight * TOP
        whole_code = jnp.round(code)
        rest_code = jnp.round((code - whole_code) * REST)
        fields = split(row_ref[s : s + 1, :].astype(F32)) + split(whole_code) + split(rest_code)
        lhs = jnp.concatenate([jnp.where(named[s], f, 0.0) for f in fields], axis=0).astype(LOW)
        total = total + dot(lhs, jnp.where(slot_ids == slot, 1.0, 0.0).astype(LOW), 1, 1)
    for i in range(3):
        high = total[2 * i * devices : (2 * i + 1) * devices]
        low = total[(2 * i + 1) * devices : (2 * i + 2) * devices]
        side_ref[i] = 256.0 * high + low


def route(owner_t, row_t, weight_t, devices, slots, width):
    rows_dev = owner_t.shape[1]
    return pl.pallas_call(
        functools.partial(route_kernel, slots),
        out_shape=(
            jax.ShapeDtypeStruct((devices, rows_dev), F32),
            jax.ShapeDtypeStruct((3, devices, width), F32),
            jax.ShapeDtypeStruct((8, rows_dev), F32),
        ),
        compiler_params=params(),
        cost_estimate=cost(1e8, 1 << 19),
        name="route",
    )(owner_t, row_t, weight_t)


def spread_kernel(
    slots, vector_ref, rank_ref, side_ref, out_ref, code_ref, level_ref, pick_ref
):
    step = pl.program_id(0)
    columns = vector_ref.shape[2]

    @pl.when(step == 0)
    def _():
        vector = vector_ref[0]
        peak = jnp.maximum(jnp.max(jnp.abs(vector), axis=0, keepdims=True), 1e-30)
        level = jnp.floor(jnp.log(peak) * (1.0 / LOG2)) + 1.0
        level_ref[...] = level
        code = jnp.clip(jnp.round(vector * (TOP / jnp.exp(level * LOG2))), -TOP, TOP)
        high, low = split(code)
        code_ref[:, :columns] = high.astype(LOW)
        code_ref[:, columns:] = low.astype(LOW)

    rows_dev = rank_ref.shape[1]
    owners = SPREAD_BLOCK // slots
    slot_ids = lax.broadcasted_iota(jnp.int32, (slots, rows_dev), 0).astype(F32)
    for j in range(owners):
        rank = rank_ref[pl.ds(step * owners + j, 1), :]
        pick_ref[j * slots : (j + 1) * slots, :] = jnp.where(slot_ids == rank, 1.0, 0.0).astype(LOW)
    picked = dot(pick_ref[...], code_ref[...])
    codes = (256.0 * picked[:, :columns] + picked[:, columns:]).astype(jnp.int32).astype(CODE)
    line = lax.broadcasted_iota(jnp.int32, (8, LANES), 0)
    parts = columns // LANES
    for j in range(owners):
        extra = jnp.zeros((8, LANES), F32)
        for k in range(3):
            extra = jnp.where(line == k, side_ref[k, pl.ds(step * owners + j, 1), :], extra)
        for h in range(parts):
            at = slice(h * LANES, (h + 1) * LANES)
            extra = jnp.where(line == 3 + h, level_ref[:, at], extra)
            out_ref[j, h * slots : (h + 1) * slots, :] = codes[j * slots : (j + 1) * slots, at]
        out_ref[j, parts * slots :, :] = extra.astype(jnp.int32).astype(CODE)


def spread_out(basis, rank, side, slots):
    devices, rows_dev = rank.shape
    last, columns = basis.shape[0] - 1, basis.shape[2]
    owners = SPREAD_BLOCK // slots
    shape = (devices, columns // LANES * slots + 8, LANES)
    return pl.pallas_call(
        functools.partial(spread_kernel, slots),
        grid=(devices // owners,),
        in_specs=[
            pl.BlockSpec((1, rows_dev, columns), lambda i: (last, 0, 0)),
            whole(rank.shape),
            whole(side.shape),
        ],
        out_specs=pl.BlockSpec((owners,) + shape[1:], lambda i: (i, 0, 0)),
        out_shape=in_hbm(shape, CODE),
        scratch_shapes=[
            pltpu.VMEM((rows_dev, 2 * columns), LOW),
            pltpu.VMEM((1, columns), F32),
            pltpu.VMEM((SPREAD_BLOCK, rows_dev), LOW),
        ],
        compiler_params=params(("arbitrary",)),
        cost_estimate=cost(4 * devices * slots * rows_dev * columns, 4 << 20),
        name="spread_out",
    )(basis, rank, side)


def collect_kernel(
    slots,
    got_ref,
    gram_hbm,
    base_ref,
    ascend_ref,
    first_ref,
    coeff_ref,
    rows_ref,
    sum_ref,
    pick_ref,
    term_ref,
    gram_ref,
    gram_sem,
):
    step = pl.program_id(0)
    rows_dev, width = first_ref.shape
    owners = got_ref.shape[0]
    parts = width // LANES
    gram_copy = pltpu.make_async_copy(gram_hbm, gram_ref, gram_sem)

    @pl.when(step == 0)
    def _():
        gram_copy.start()

    ids = lax.broadcasted_iota(jnp.int32, (rows_dev, slots), 0).astype(F32)
    for j in range(owners):
        at = slice(j * slots, (j + 1) * slots)
        extra = got_ref[j, parts * slots :, :].astype(jnp.int32).astype(F32)
        row = extra[0:1, :slots]
        weight = (extra[1:2, :slots] + extra[2:3, :slots] * (1.0 / REST)) * (1.0 / TOP)
        weight = column(weight)
        rows_ref[pl.ds(step * owners + j, 1), :] = extra[0:1, :]
        for h in range(parts):
            scale = jnp.exp(extra[3 + h : 4 + h, :] * LOG2) * (1.0 / TOP)
            codes = got_ref[j, h * slots : (h + 1) * slots, :].astype(jnp.int32).astype(F32)
            values = codes * weight * scale
            high = values.astype(LOW)
            term_ref[at, h * LANES : (h + 1) * LANES] = high
            rest = (values - high.astype(F32)).astype(LOW)
            term_ref[at, width + h * LANES : width + (h + 1) * LANES] = rest
        pick_ref[:, at] = jnp.where(ids == row, 1.0, 0.0).astype(LOW)
    added = dot(pick_ref[...], term_ref[...])

    @pl.when(step == 0)
    def _():
        sum_ref[...] = added

    @pl.when(step > 0)
    def _():
        sum_ref[...] += added

    @pl.when(step == pl.num_programs(0) - 1)
    def _():
        gram_copy.wait()
        leaves, leaf = gram_ref.shape[:2]
        rank = base_ref.shape[1]
        for l in range(leaves):
            at = slice(l * leaf, (l + 1) * leaf)
            dual = sum_ref[at, :width] + sum_ref[at, width:]
            first = dual + dot(gram_ref[l], dual.astype(LOW), 0, 0)
            low = first.astype(LOW)
            first_ref[at, :] = first
            coeff = dot(base_ref[l], low).astype(LOW)
            for b in range(coeff_ref.shape[0]):
                coeff_ref[b, l * rank : (l + 1) * rank, :] = coeff
        for b in range(coeff_ref.shape[0]):
            coeff_ref[b, leaves * rank :, :] = ascend_ref[...]


def collect(got, gram, base, ascend, slots, branches, width):
    devices = got.shape[0]
    leaves, leaf = gram.shape[:2]
    rank = base.shape[1]
    rows_dev = leaves * leaf
    owners = COLLECT_BLOCK // slots
    sent_rows = leaves * rank + ascend.shape[0]
    return pl.pallas_call(
        functools.partial(collect_kernel, slots),
        grid=(devices // owners,),
        in_specs=[
            pl.BlockSpec((owners,) + got.shape[1:], lambda i: (i, 0, 0)),
            pl.BlockSpec(memory_space=pltpu.HBM),
            whole(base.shape),
            whole(ascend.shape),
        ],
        out_specs=(
            whole((rows_dev, width)),
            whole((branches, sent_rows, width)),
            whole((devices, LANES)),
        ),
        out_shape=(
            in_vmem((rows_dev, width), F32),
            in_hbm((branches, sent_rows, width), LOW),
            in_hbm((devices, LANES), F32),
        ),
        scratch_shapes=[
            pltpu.VMEM((rows_dev, 2 * width), F32),
            pltpu.VMEM((rows_dev, COLLECT_BLOCK), LOW),
            pltpu.VMEM((COLLECT_BLOCK, 2 * width), LOW),
            pltpu.VMEM(gram.shape, LOW),
            pltpu.SemaphoreType.DMA,
        ],
        compiler_params=params(("arbitrary",)),
        cost_estimate=cost(4 * devices * slots * rows_dev * width, 4 << 20),
        name="collect",
    )(got, gram, base, ascend)


def parent_kernel(coeff_ref, out_ref):
    rank, width = out_ref.shape
    branches, rows = coeff_ref.shape[:2]
    parts = width // rank
    leaves = rows * parts // (rank * (parts + 1))
    held = leaves * rank // parts
    sums = [jnp.zeros((held, width), F32) for _ in range(rank // held)]
    for b in range(branches):
        packed = coeff_ref[b, leaves * rank :, :]
        for q in range(parts):
            leaf, at = divmod(q * held, rank)
            term = dot(
                packed[:, q * rank : (q + 1) * rank], coeff_ref[b, leaf * rank : (leaf + 1) * rank, :]
            )
            sums[at // held] = sums[at // held] + term
    for i, total in enumerate(sums):
        out_ref[i * held : (i + 1) * held, :] = total.astype(LOW)


def parent_of(coeff, rank):
    width = coeff.shape[2]
    return pl.pallas_call(
        parent_kernel,
        out_shape=in_hbm((rank, width), LOW),
        compiler_params=params(),
        cost_estimate=cost(2 * coeff.size * rank, 1 << 20),
        name="parent_of",
    )(coeff)


def far_kernel(list_ref, coeff_ref, block_ref, out_ref):
    leaves, items, rank = block_ref.shape[:3]
    for l in range(leaves):
        total = jnp.zeros(out_ref.shape[1:], F32)
        for k in range(items):
            source = list_ref[l, k]
            at = pl.ds(pl.multiple_of(source % leaves * rank, rank), rank)
            total = total + dot(block_ref[l, k], coeff_ref[source // leaves, at, :])
        out_ref[l] = total


def far_field(far_list, coeff, far_block):
    leaves, items, rank = far_block.shape[:3]
    width = coeff.shape[2]
    return pl.pallas_call(
        far_kernel,
        grid_spec=pltpu.PrefetchScalarGridSpec(
            num_scalar_prefetch=1,
            grid=(1,),
            in_specs=[whole(coeff.shape), whole(far_block.shape)],
            out_specs=whole((leaves, rank, width)),
        ),
        out_shape=jax.ShapeDtypeStruct((leaves, rank, width), F32),
        compiler_params=params(("arbitrary",)),
        cost_estimate=cost(2 * far_block.size * width, 1 << 20),
        name="far_field",
    )(far_list, coeff, far_block)


def near_kernel(list_ref, block_ref, first_ref, out_ref, low_ref):
    leaf, item = pl.program_id(0), pl.program_id(1)
    size = out_ref.shape[0]

    @pl.when((leaf == 0) & (item == 0))
    def _():
        for l in range(low_ref.shape[0]):
            low_ref[l] = first_ref[l * size : (l + 1) * size, :].astype(LOW)

    count = block_ref.shape[1]
    term = dot(block_ref[0, 0], low_ref[list_ref[leaf, item * count]])
    for k in range(1, count):
        term = term + dot(block_ref[0, k], low_ref[list_ref[leaf, item * count + k]])

    @pl.when(item == 0)
    def _():
        out_ref[...] = first_ref[pl.ds(pl.multiple_of(leaf * size, size), size), :] + term

    @pl.when(item > 0)
    def _():
        out_ref[...] += term


def near_field(near_list, near_block, first):
    leaves, items, leaf = near_block.shape[:3]
    width = first.shape[1]
    count = 4 if items % 4 == 0 else 1
    return pl.pallas_call(
        near_kernel,
        grid_spec=pltpu.PrefetchScalarGridSpec(
            num_scalar_prefetch=1,
            grid=(leaves, items // count),
            in_specs=[
                pl.BlockSpec((1, count, leaf, leaf), lambda l, k, _: (l, k, 0, 0)),
                whole(first.shape),
            ],
            out_specs=pl.BlockSpec((leaf, width), lambda l, k, _: (l, 0)),
            scratch_shapes=[pltpu.VMEM((leaves, leaf, width), LOW)],
        ),
        out_shape=in_vmem(first.shape, F32),
        compiler_params=params(("arbitrary", "arbitrary")),
        cost_estimate=cost(2 * near_block.size * width, 2 * near_block.size),
        name="near_field",
    )(near_list, near_block, first)


def reply_kernel(slots, *refs):
    image_ref, far_ref, top_ref, descend_ref, base_ref, gram_ref, rows_ref = refs[:7]
    parents, (out_ref, dual_ref, pick_ref) = refs[7:-3], refs[-3:]
    step = pl.program_id(0)

    @pl.when(step == 0)
    def _():
        leaves, leaf = gram_ref.shape[:2]
        field = dot(top_ref[0], parents[0][...])
        for k in range(1, len(parents)):
            field = field + dot(top_ref[k], parents[k][...])
        field = field.astype(LOW)
        for l in range(leaves):
            at = slice(l * leaf, (l + 1) * leaf)
            descent = far_ref[l] + dot(descend_ref[l], field)
            image = image_ref[at, :] + dot(base_ref[l], descent.astype(LOW), 0, 0)
            dual_ref[at, :] = (image + dot(gram_ref[l], image.astype(LOW))).astype(LOW)

    rows_dev = dual_ref.shape[0]
    owners = REPLY_BLOCK // slots
    ids = lax.broadcasted_iota(jnp.int32, (slots, rows_dev), 1).astype(F32)
    for j in range(owners):
        row = column(rows_ref[pl.ds(step * owners + j, 1), :][:, :slots])
        pick_ref[j * slots : (j + 1) * slots, :] = jnp.where(ids == row, 1.0, 0.0).astype(LOW)
    out_ref[...] = dot(pick_ref[...], dual_ref[...]).astype(LOW)


def reply(image, far, top, parents, descend, base, gram, rows, slots):
    rows_dev, width = image.shape
    steps = rows.shape[0] * slots // REPLY_BLOCK
    args = (image, far, top, descend, base, gram, rows, *parents)
    return pl.pallas_call(
        functools.partial(reply_kernel, slots),
        grid=(steps,),
        in_specs=[whole(a.shape) for a in args],
        out_specs=pl.BlockSpec((REPLY_BLOCK, width), lambda i: (i, 0)),
        out_shape=in_hbm((steps * REPLY_BLOCK, width), LOW),
        scratch_shapes=[pltpu.VMEM((rows_dev, width), LOW), pltpu.VMEM((REPLY_BLOCK, rows_dev), LOW)],
        compiler_params=params(("arbitrary",)),
        cost_estimate=cost(2 * steps * REPLY_BLOCK * rows_dev * width, 4 << 20),
        name="reply",
    )(*args)


def gather_kernel(spread, ret_ref, place_ref, basis_ref, image_ref, sums_ref):
    step = pl.program_id(0)
    rows = place_ref.shape[0]
    total = ret_ref.shape[0]
    ids = lax.broadcasted_iota(jnp.int32, (rows, total), 1).astype(F32)
    image = jnp.zeros(image_ref.shape, F32)
    for s in range(spread):
        pick = jnp.where(ids == place_ref[:, s : s + 1], 1.0, 0.0).astype(LOW)
        image = image + place_ref[:, spread + s : spread + s + 1] * dot(pick, ret_ref[...])
    image_ref[...] = image
    krylov = basis_ref.shape[0]
    parts = [jnp.sum(basis_ref[k] * image, axis=0, keepdims=True) for k in range(krylov)]
    parts.append(jnp.sum(image * image, axis=0, keepdims=True))
    parts.append(jnp.zeros((sums_ref.shape[0] - krylov - 1, image.shape[1]), F32))
    added = jnp.concatenate(parts, axis=0)

    @pl.when(step == 0)
    def _():
        sums_ref[...] = added

    @pl.when(step > 0)
    def _():
        sums_ref[...] += added


def gather_back(ret, place_col, basis, spread):
    total, width = ret.shape
    krylov, rows_dev = basis.shape[:2]
    rows = 256
    return pl.pallas_call(
        functools.partial(gather_kernel, spread),
        grid=(rows_dev // rows,),
        in_specs=[
            whole(ret.shape),
            pl.BlockSpec((rows, place_col.shape[1]), lambda i: (i, 0)),
            pl.BlockSpec((krylov, rows, width), lambda i: (0, i, 0)),
        ],
        out_specs=(pl.BlockSpec((rows, width), lambda i: (i, 0)), whole((8, width))),
        out_shape=(
            jax.ShapeDtypeStruct((rows_dev, width), F32),
            jax.ShapeDtypeStruct((8, width), F32),
        ),
        compiler_params=params(("arbitrary",)),
        cost_estimate=cost(2 * spread * total * rows_dev * width, 6 << 20),
        name="gather_back",
    )(ret, place_col, basis)


AXES = ("branch", "group")


def exchange(values, axes=AXES):
    return lax.all_to_all(values, axes, split_axis=0, concat_axis=0, tiled=True)


def swaps(values, axis):
    size = lax.axis_size(axis)
    return [values] + [
        lax.ppermute(values, axis, [(i, i ^ k) for i in range(size)]) for k in range(1, size)
    ]


def to_all(values, axes, size):
    return exchange(jnp.broadcast_to(values[None], (size,) + values.shape), axes)


def body(
    basis,
    spread_owner,
    spread_row,
    spread_weight,
    gram_term,
    near_block,
    near_list,
    leaf_basis,
    far_block,
    far_list,
    ascend,
    descend,
    top_block,
):
    branches = lax.axis_size("branch")
    groups = lax.axis_size("group")
    devices = branches * groups
    rows_dev, columns = basis.shape[1:]
    krylov = basis.shape[0]
    spread = spread_owner.shape[1]
    slots = 2 * spread * rows_dev // devices
    total = devices * slots
    leaves, rank = leaf_basis.shape[:2]
    rank_of, side, place = route(
        kept(spread_owner.T), kept(spread_row.T), kept(spread_weight.T), devices, slots, LANES
    )
    sent = spread_out(kept(basis), rank_of, side, slots)
    sent, late_ascend, late_top = lax.optimization_barrier((sent, ascend, top_block))
    got = exchange(sent)

    parts = columns // rank
    held = leaves * rank // parts
    packed = late_ascend.reshape(parts, held, rank).transpose(1, 0, 2).reshape(held, columns)
    columns_of = (jnp.arange(groups) ^ lax.axis_index("group")) % groups
    top = late_top.reshape(rank, groups, rank).transpose(1, 0, 2)[columns_of]

    got, packed, top = lax.optimization_barrier((got, packed, top))
    first, coeff, rows = collect(
        got, kept(gram_term), kept(leaf_basis), kept(packed), slots, branches, columns
    )
    coeff = exchange(coeff, "branch")
    image = near_field(near_list, kept(near_block), first)
    coeff, image = lax.optimization_barrier((coeff, image))
    parents = swaps(parent_of(coeff, rank), "group")
    far = far_field(far_list, coeff, kept(far_block))
    replies = reply(
        image,
        far,
        kept(top),
        parents,
        kept(descend),
        kept(leaf_basis),
        kept(gram_term),
        kept(rows),
        slots,
    )
    returned = exchange(replies.reshape(devices, slots, columns)).reshape(total, columns)
    primal, sums = gather_back(returned, kept(place.T), basis, spread)
    pairs = [(i, j) for i in range(krylov) for j in range(i, krylov)]
    mutual = jnp.stack([jnp.sum(basis[i] * basis[j], axis=0) for i, j in pairs])
    sums = jnp.concatenate([sums[: krylov + 1], mutual], axis=0)
    sums = jnp.sum(to_all(sums, AXES, devices), axis=0)
    mutual = sums[krylov + 1 :]

    total_rows = rows_dev * devices
    projection = sums[:krylov] / total_rows
    remainder = primal - jnp.sum(projection[:, None, :] * basis, axis=0)
    square = sums[krylov] / total_rows - 2.0 * jnp.sum(projection * projection, axis=0)
    for at, (i, j) in enumerate(pairs):
        times = 1.0 if i == j else 2.0
        square = square + times * projection[i] * projection[j] * mutual[at] / total_rows
    norm_scale = jnp.sqrt(jnp.maximum(square, 0.0) + 1e-06)
    return (remainder / norm_scale, jnp.concatenate([projection, norm_scale[None]], axis=0))


def solution(mesh):
    both = ("branch", "group")
    return jax.shard_map(
        body,
        mesh=mesh,
        in_specs=(
            P(None, both, None),
            P(both, None),
            P(both, None),
            P(both, None),
            P(both, None, None),
            P(both, None, None, None),
            P(both, None),
            P(both, None, None),
            P(both, None, None, None),
            P(both, None),
            P(both, None, None),
            P(both, None, None),
            P("group", None),
        ),
        out_specs=(P(both, None), P()),
        check_vma=False,
    )
```

```python
import functools

import jax
import jax.numpy as jnp
from jax import lax
from jax.experimental import pallas as pl
from jax.experimental.pallas import tpu as pltpu
from jax.sharding import PartitionSpec as P

F32 = jnp.float32
LOW = jnp.bfloat16
CODE = jnp.int16
TOP = 32767.0
REST = 65534.0
LOG2 = 0.6931471805599453
SPREAD_BLOCK = 1024
COLLECT_BLOCK = 512
REPLY_BLOCK = 1024
LANES = 128


def rounded(values):
    return values.astype(LOW)


def contract(pattern, first_op, second_op):
    return jnp.einsum(pattern, first_op, second_op, preferred_element_type=F32)


def dot(lhs, rhs, lhs_dim=1, rhs_dim=0):
    return lax.dot_general(
        lhs, rhs, (((lhs_dim,), (rhs_dim,)), ((), ())), preferred_element_type=F32
    )


def params(semantics=None, mib=24):
    return pltpu.CompilerParams(dimension_semantics=semantics, vmem_limit_bytes=mib << 20)


def whole(shape):
    zeros = (0,) * len(shape)
    return pl.BlockSpec(shape, lambda *_: zeros)


def in_hbm(shape, dtype):
    return pltpu.HBM(shape, dtype)


def in_vmem(shape, dtype):
    return pltpu.VMEM(shape, dtype)


def near_by(values):
    return pltpu.with_memory_space_constraint(values, pltpu.VMEM)


def kept(values):
    return pltpu.with_memory_space_constraint(values, pltpu.HBM)


def cost(flops, nbytes):
    return pl.CostEstimate(flops=int(flops), bytes_accessed=int(nbytes), transcendentals=0)


def column(row):
    size = row.shape[1]
    same = lax.broadcasted_iota(jnp.int32, (size, size), 0) == lax.broadcasted_iota(
        jnp.int32, (size, size), 1
    )
    return jnp.sum(jnp.where(same, row, 0.0), axis=1, keepdims=True)


def split(code):
    high = jnp.round(code * (1.0 / 256.0))
    return high, code - 256.0 * high


def find_routes(slots, owner_ref, row_ref, weight_ref, rank_ref, side_ref, place_ref):
    devices, rows_dev = rank_ref.shape
    spread = owner_ref.shape[0]
    width = side_ref.shape[2]
    ids = lax.broadcasted_iota(jnp.int32, (devices, rows_dev), 0)
    named = [owner_ref[s : s + 1, :] == ids for s in range(spread)]
    chosen = functools.reduce(jnp.logical_or, named)
    flag = jnp.where(chosen, 1.0, 0.0)
    lane = 128
    upper = jnp.where(
        lax.broadcasted_iota(jnp.int32, (lane, lane), 0)
        <= lax.broadcasted_iota(jnp.int32, (lane, lane), 1),
        1.0,
        0.0,
    ).astype(LOW)
    before = jnp.zeros((devices, 1), F32)
    pieces = []
    for start in range(0, rows_dev, lane):
        part = flag[:, start : start + lane]
        upto = dot(part.astype(LOW), upper)
        pieces.append(upto - part + before)
        before = before + upto[:, lane - 1 : lane]
    rank = jnp.concatenate(pieces, axis=1)
    rank_ref[...] = jnp.where(chosen, rank, -1.0)
    slot_ids = lax.broadcasted_iota(jnp.int32, (width, rows_dev), 0).astype(F32)
    place_ref[...] = jnp.zeros_like(place_ref)
    total = jnp.zeros((6 * devices, width), F32)
    for s in range(spread):
        slot = jnp.sum(jnp.where(named[s], rank, 0.0), axis=0, keepdims=True)
        place_ref[s : s + 1, :] = owner_ref[s : s + 1, :].astype(F32) * slots + slot
        weight = weight_ref[s : s + 1, :]
        place_ref[spread + s : spread + s + 1, :] = weight
        code = weight * TOP
        whole_code = jnp.round(code)
        rest_code = jnp.round((code - whole_code) * REST)
        fields = split(row_ref[s : s + 1, :].astype(F32)) + split(whole_code) + split(rest_code)
        lhs = jnp.concatenate([jnp.where(named[s], f, 0.0) for f in fields], axis=0).astype(LOW)
        total = total + dot(lhs, jnp.where(slot_ids == slot, 1.0, 0.0).astype(LOW), 1, 1)
    for i in range(3):
        high = total[2 * i * devices : (2 * i + 1) * devices]
        low = total[(2 * i + 1) * devices : (2 * i + 2) * devices]
        side_ref[i] = 256.0 * high + low


def spread_kernel(
    slots,
    owner_ref,
    row_ref,
    weight_ref,
    basis_hbm,
    out_ref,
    place_ref,
    vector_ref,
    rank_ref,
    side_ref,
    code_ref,
    level_ref,
    pick_ref,
    vector_sem,
):
    step = pl.program_id(0)
    columns = vector_ref.shape[1]

    @pl.when(step == 0)
    def _():
        copy = pltpu.make_async_copy(basis_hbm.at[basis_hbm.shape[0] - 1], vector_ref, vector_sem)
        copy.start()
        find_routes(slots, owner_ref, row_ref, weight_ref, rank_ref, side_ref, place_ref)
        copy.wait()
        vector = vector_ref[...]
        peak = jnp.maximum(jnp.max(jnp.abs(vector), axis=0, keepdims=True), 1e-30)
        level = jnp.floor(jnp.log(peak) * (1.0 / LOG2)) + 1.0
        level_ref[...] = level
        code = jnp.clip(jnp.round(vector * (TOP / jnp.exp(level * LOG2))), -TOP, TOP)
        high, low = split(code)
        code_ref[:, :columns] = high.astype(LOW)
        code_ref[:, columns:] = low.astype(LOW)

    rows_dev = rank_ref.shape[1]
    owners = SPREAD_BLOCK // slots
    slot_ids = lax.broadcasted_iota(jnp.int32, (slots, rows_dev), 0).astype(F32)
    for j in range(owners):
        rank = rank_ref[pl.ds(step * owners + j, 1), :]
        pick_ref[j * slots : (j + 1) * slots, :] = jnp.where(slot_ids == rank, 1.0, 0.0).astype(LOW)
    picked = dot(pick_ref[...], code_ref[...])
    codes = (256.0 * picked[:, :columns] + picked[:, columns:]).astype(jnp.int32).astype(CODE)
    line = lax.broadcasted_iota(jnp.int32, (8, LANES), 0)
    parts = columns // LANES
    for j in range(owners):
        extra = jnp.zeros((8, LANES), F32)
        for k in range(3):
            extra = jnp.where(line == k, side_ref[k, pl.ds(step * owners + j, 1), :], extra)
        for h in range(parts):
            at = slice(h * LANES, (h + 1) * LANES)
            extra = jnp.where(line == 3 + h, level_ref[:, at], extra)
            out_ref[j, h * slots : (h + 1) * slots, :] = codes[j * slots : (j + 1) * slots, at]
        out_ref[j, parts * slots :, :] = extra.astype(jnp.int32).astype(CODE)


def spread_out(owner_t, row_t, weight_t, basis, devices, slots):
    rows_dev, columns = basis.shape[1:]
    owners = SPREAD_BLOCK // slots
    shape = (devices, columns // LANES * slots + 8, LANES)
    return pl.pallas_call(
        functools.partial(spread_kernel, slots),
        grid=(devices // owners,),
        in_specs=[
            whole(owner_t.shape),
            whole(row_t.shape),
            whole(weight_t.shape),
            pl.BlockSpec(memory_space=pltpu.HBM),
        ],
        out_specs=(
            pl.BlockSpec((owners,) + shape[1:], lambda i: (i, 0, 0)),
            whole((8, rows_dev)),
        ),
        out_shape=(in_hbm(shape, CODE), in_hbm((8, rows_dev), F32)),
        scratch_shapes=[
            pltpu.VMEM((rows_dev, columns), F32),
            pltpu.VMEM((devices, rows_dev), F32),
            pltpu.VMEM((3, devices, LANES), F32),
            pltpu.VMEM((rows_dev, 2 * columns), LOW),
            pltpu.VMEM((1, columns), F32),
            pltpu.VMEM((SPREAD_BLOCK, rows_dev), LOW),
            pltpu.SemaphoreType.DMA,
        ],
        compiler_params=params(("arbitrary",)),
        cost_estimate=cost(4 * devices * slots * rows_dev * columns, 4 << 20),
        name="spread_out",
    )(owner_t, row_t, weight_t, basis)


def add_slots(slots, low_part, got_ref, rows_ref, sum_ref, picks, terms):
    rows_dev, width = sum_ref.shape
    owners = COLLECT_BLOCK // slots
    parts = width // LANES
    blocks = got_ref.shape[0] // owners
    tile = 16
    ids = lax.broadcasted_iota(jnp.int32, (rows_dev, slots), 0).astype(CODE)
    one, zero = jnp.ones((rows_dev, slots), LOW), jnp.zeros((rows_dev, slots), LOW)

    def build(block):
        pick_ref, term_ref = picks[block % 2], terms[block % 2]
        for j in range(owners):
            at = slice(j * slots, (j + 1) * slots)
            source = block * owners + j
            extra = got_ref[source, parts * slots :, :].astype(jnp.int32)
            row = jnp.broadcast_to(extra[0:1, :slots], (tile, slots)).astype(CODE)
            row = jnp.broadcast_to(row[None], (rows_dev // tile, tile, slots))
            pick_ref[:, at] = jnp.where(ids == row.reshape(rows_dev, slots), one, zero)
            extra = extra.astype(F32)
            weight = (extra[1:2, :slots] + extra[2:3, :slots] * (1.0 / REST)) * (1.0 / TOP)
            weight = column(weight)
            if rows_ref is not None:
                rows_ref[source : source + 1, :] = extra[0:1, :]
            for h in range(parts):
                scale = jnp.exp(extra[3 + h : 4 + h, :] * LOG2) * (1.0 / TOP)
                codes = got_ref[source, h * slots : (h + 1) * slots, :].astype(jnp.int32).astype(F32)
                values = codes * weight * scale
                term = values.astype(LOW)
                if low_part:
                    term = (values - term.astype(F32)).astype(LOW)
                term_ref[at, h * LANES : (h + 1) * LANES] = term

    build(0)
    for block in range(blocks):
        if block + 1 < blocks:
            build(block + 1)
        added = dot(picks[block % 2][...], terms[block % 2][...])
        sum_ref[...] = added if block == 0 else sum_ref[...] + added


def rise_kernel(base_ref, gram_ref, out_ref):
    for l in range(base_ref.shape[0]):
        base = base_ref[l]
        out_ref[l] = (base.astype(F32) + dot(base, gram_ref[l], 1, 1)).astype(LOW)


def rise(base, gram):
    return pl.pallas_call(
        rise_kernel,
        out_shape=in_vmem(base.shape, LOW),
        compiler_params=params(mib=8),
        cost_estimate=cost(2 * gram.size * base.shape[1], 2 * gram.size),
        name="rise",
    )(base, gram)


def collect_kernel(
    slots,
    got_ref,
    rise_ref,
    ascend_ref,
    dual_ref,
    coeff_ref,
    rows_ref,
    pick_a,
    pick_b,
    term_a,
    term_b,
):
    add_slots(slots, False, got_ref, rows_ref, dual_ref, (pick_a, pick_b), (term_a, term_b))
    leaves, rank, leaf = rise_ref.shape
    for b in range(coeff_ref.shape[0]):
        coeff_ref[b, leaves * rank :, :] = ascend_ref[...]
    for l in range(leaves):
        dual = dual_ref[l * leaf : (l + 1) * leaf, :]
        coeff = dot(rise_ref[l], dual.astype(LOW)).astype(LOW)
        for b in range(coeff_ref.shape[0]):
            coeff_ref[b, l * rank : (l + 1) * rank, :] = coeff


def slot_scratch(rows_dev, width):
    return [
        pltpu.VMEM((rows_dev, COLLECT_BLOCK), LOW),
        pltpu.VMEM((rows_dev, COLLECT_BLOCK), LOW),
        pltpu.VMEM((COLLECT_BLOCK, width), LOW),
        pltpu.VMEM((COLLECT_BLOCK, width), LOW),
    ]


def collect(got, lift, ascend, slots, branches, width):
    devices = got.shape[0]
    leaves, rank, leaf = lift.shape
    rows_dev = leaves * leaf
    sent_rows = leaves * rank + ascend.shape[0]
    direct = pl.BlockSpec(memory_space=pltpu.VMEM)
    return pl.pallas_call(
        functools.partial(collect_kernel, slots),
        in_specs=[direct] * 3,
        out_specs=[direct] * 3,
        out_shape=(
            in_vmem((rows_dev, width), F32),
            in_hbm((branches, sent_rows, width), LOW),
            in_hbm((devices, LANES), F32),
        ),
        scratch_shapes=slot_scratch(rows_dev, width),
        compiler_params=params(),
        cost_estimate=cost(2 * devices * slots * rows_dev * width, 4 << 20),
        name="collect",
    )(got, lift, ascend)


def refine_kernel(
    slots,
    got_ref,
    dual_ref,
    gram_hbm,
    out_ref,
    sum_ref,
    gram_ref,
    gram_sem,
    pick_a,
    pick_b,
    term_a,
    term_b,
):
    gram_copy = pltpu.make_async_copy(gram_hbm, gram_ref, gram_sem)
    gram_copy.start()
    add_slots(slots, True, got_ref, None, sum_ref, (pick_a, pick_b), (term_a, term_b))
    gram_copy.wait()
    leaves, leaf = gram_ref.shape[:2]
    for l in range(leaves):
        at = slice(l * leaf, (l + 1) * leaf)
        dual = dual_ref[at, :] + sum_ref[at, :]
        out_ref[at, :] = dual + dot(gram_ref[l], dual.astype(LOW), 0, 0)


def refine(got, dual, gram, slots):
    rows_dev, width = dual.shape
    devices = got.shape[0]
    direct = pl.BlockSpec(memory_space=pltpu.VMEM)
    return pl.pallas_call(
        functools.partial(refine_kernel, slots),
        in_specs=[direct, direct, pl.BlockSpec(memory_space=pltpu.HBM)],
        out_specs=direct,
        out_shape=in_vmem(dual.shape, F32),
        scratch_shapes=[
            pltpu.VMEM((rows_dev, width), F32),
            pltpu.VMEM(gram.shape, LOW),
            pltpu.SemaphoreType.DMA,
        ]
        + slot_scratch(rows_dev, width),
        compiler_params=params(),
        cost_estimate=cost(2 * devices * slots * rows_dev * width, 4 << 20),
        name="refine",
    )(got, dual, gram)


def parent_kernel(coeff_ref, out_ref):
    rank, width = out_ref.shape
    branches, rows = coeff_ref.shape[:2]
    parts = width // rank
    leaves = rows * parts // (rank * (parts + 1))
    held = leaves * rank // parts
    sums = [jnp.zeros((held, width), F32) for _ in range(rank // held)]
    for b in range(branches):
        packed = coeff_ref[b, leaves * rank :, :]
        for q in range(parts):
            leaf, at = divmod(q * held, rank)
            term = dot(
                packed[:, q * rank : (q + 1) * rank], coeff_ref[b, leaf * rank : (leaf + 1) * rank, :]
            )
            sums[at // held] = sums[at // held] + term
    for i, total in enumerate(sums):
        out_ref[i * held : (i + 1) * held, :] = total.astype(LOW)


def parent_of(coeff, rank):
    width = coeff.shape[2]
    return pl.pallas_call(
        parent_kernel,
        out_shape=in_vmem((rank, width), LOW),
        compiler_params=params(mib=6),
        cost_estimate=cost(2 * coeff.size * rank, 1 << 20),
        name="parent_of",
    )(coeff)


def far_kernel(list_ref, coeff_ref, block_ref, out_ref):
    leaves, items, rank = block_ref.shape[:3]
    for l in range(leaves):
        total = jnp.zeros(out_ref.shape[1:], F32)
        for k in range(items):
            source = list_ref[l, k]
            at = pl.ds(pl.multiple_of(source % leaves * rank, rank), rank)
            total = total + dot(block_ref[l, k], coeff_ref[source // leaves, at, :])
        out_ref[l] = total


def far_field(far_list, coeff, far_block):
    leaves, items, rank = far_block.shape[:3]
    width = coeff.shape[2]
    return pl.pallas_call(
        far_kernel,
        grid_spec=pltpu.PrefetchScalarGridSpec(
            num_scalar_prefetch=1,
            grid=(1,),
            in_specs=[whole(coeff.shape), whole(far_block.shape)],
            out_specs=whole((leaves, rank, width)),
        ),
        out_shape=jax.ShapeDtypeStruct((leaves, rank, width), F32),
        compiler_params=params(("arbitrary",), 6),
        cost_estimate=cost(2 * far_block.size * width, 1 << 20),
        name="far_field",
    )(far_list, coeff, far_block)


def near_kernel(list_ref, block_ref, first_ref, out_ref, low_ref):
    leaf, item = pl.program_id(0), pl.program_id(1)
    size = out_ref.shape[0]

    @pl.when((leaf == 0) & (item == 0))
    def _():
        for l in range(low_ref.shape[0]):
            low_ref[l] = first_ref[l * size : (l + 1) * size, :].astype(LOW)

    count = block_ref.shape[1]
    term = dot(block_ref[0, 0], low_ref[list_ref[leaf, item * count]])
    for k in range(1, count):
        term = term + dot(block_ref[0, k], low_ref[list_ref[leaf, item * count + k]])

    @pl.when(item == 0)
    def _():
        out_ref[...] = first_ref[pl.ds(pl.multiple_of(leaf * size, size), size), :] + term

    @pl.when(item > 0)
    def _():
        out_ref[...] += term


def near_field(near_list, near_block, first):
    leaves, items, leaf = near_block.shape[:3]
    width = first.shape[1]
    count = 4 if items % 4 == 0 else 1
    return pl.pallas_call(
        near_kernel,
        grid_spec=pltpu.PrefetchScalarGridSpec(
            num_scalar_prefetch=1,
            grid=(leaves, items // count),
            in_specs=[
                pl.BlockSpec((1, count, leaf, leaf), lambda l, k, _: (l, k, 0, 0)),
                whole(first.shape),
            ],
            out_specs=pl.BlockSpec((leaf, width), lambda l, k, _: (l, 0)),
            scratch_shapes=[pltpu.VMEM((leaves, leaf, width), LOW)],
        ),
        out_shape=in_vmem(first.shape, F32),
        compiler_params=params(("arbitrary", "arbitrary"), 12),
        cost_estimate=cost(2 * near_block.size * width, 2 * near_block.size),
        name="near_field",
    )(near_list, near_block, first)


def prepare_kernel(image_ref, base_ref, gram_ref, dual_ref, lift_ref):
    leaves, leaf = gram_ref.shape[:2]
    ids = lax.broadcasted_iota(jnp.int32, (leaf, leaf), 0)
    same = ids == lax.broadcasted_iota(jnp.int32, (leaf, leaf), 1)
    unit = jnp.where(same, 1.0, 0.0).astype(LOW)
    for l in range(leaves):
        at = slice(l * leaf, (l + 1) * leaf)
        image = image_ref[at, :]
        dual_ref[at, :] = image + dot(gram_ref[l], image.astype(LOW))
        lifted = dot(unit, base_ref[l], 1, 1) + dot(gram_ref[l], base_ref[l], 1, 1)
        parts = [lifted if i == l else jnp.zeros_like(lifted) for i in range(leaves)]
        lift_ref[at, :] = jnp.concatenate(parts, axis=1).astype(LOW)


def prepare(image, base, gram):
    rows_dev, width = image.shape
    lanes = base.shape[0] * base.shape[1]
    return pl.pallas_call(
        prepare_kernel,
        out_shape=(in_vmem((rows_dev, width), F32), in_vmem((rows_dev, lanes), LOW)),
        compiler_params=params(mib=12),
        cost_estimate=cost(2 * gram.size * (width + 2 * lanes), 4 << 20),
        name="prepare",
    )(image, base, gram)


def reply_kernel(slots, *refs):
    dual_ref, lift_ref, far_ref, top_ref, descend_ref, rows_ref = refs[:6]
    parents, (out_ref, field_ref, low_ref, pick_ref) = refs[6:-4], refs[-4:]
    step = pl.program_id(0)

    @pl.when(step == 0)
    def _():
        leaves, rank = far_ref.shape[:2]
        field = dot(top_ref[0], parents[0][...])
        for k in range(1, len(parents)):
            field = field + dot(top_ref[k], parents[k][...])
        field = field.astype(LOW)
        for l in range(leaves):
            descent = far_ref[l] + dot(descend_ref[l], field)
            field_ref[l * rank : (l + 1) * rank, :] = descent.astype(LOW)
        low_ref[...] = (dual_ref[...] + dot(lift_ref[...], field_ref[...])).astype(LOW)

    owners = REPLY_BLOCK // slots
    ids = lax.broadcasted_iota(jnp.int32, (slots, low_ref.shape[0]), 1).astype(F32)
    for j in range(owners):
        row = column(rows_ref[pl.ds(step * owners + j, 1), :][:, :slots])
        pick_ref[j * slots : (j + 1) * slots, :] = jnp.where(ids == row, 1.0, 0.0).astype(LOW)
    out_ref[...] = dot(pick_ref[...], low_ref[...]).astype(LOW)


def reply(dual, lift, far, top, parents, descend, rows, slots):
    rows_dev, width = dual.shape
    total = rows.shape[0] * slots
    args = (far, top, descend, rows, *parents)
    direct = pl.BlockSpec(memory_space=pltpu.VMEM)
    return pl.pallas_call(
        functools.partial(reply_kernel, slots),
        grid=(total // REPLY_BLOCK,),
        in_specs=[direct, direct] + [whole(a.shape) for a in args[:4]] + [direct] * len(parents),
        out_specs=pl.BlockSpec((REPLY_BLOCK, width), lambda i: (i, 0)),
        out_shape=in_hbm((total, width), LOW),
        scratch_shapes=[
            pltpu.VMEM((lift.shape[1], width), LOW),
            pltpu.VMEM((rows_dev, width), LOW),
            pltpu.VMEM((REPLY_BLOCK, rows_dev), LOW),
        ],
        compiler_params=params(("arbitrary",), 16),
        cost_estimate=cost(2 * total * rows_dev * width, 4 << 20),
        name="reply",
    )(dual, lift, *args)


def gather_kernel(spread, ret_ref, place_ref, basis_ref, mutual_ref, image_ref, sums_ref):
    step = pl.program_id(0)
    rows = place_ref.shape[0]
    total = ret_ref.shape[0]
    ids = lax.broadcasted_iota(jnp.int32, (rows, total), 1).astype(F32)
    image = jnp.zeros(image_ref.shape, F32)
    for s in range(spread):
        pick = jnp.where(ids == place_ref[:, s : s + 1], 1.0, 0.0).astype(LOW)
        image = image + place_ref[:, spread + s : spread + s + 1] * dot(pick, ret_ref[...])
    image_ref[...] = image
    krylov = basis_ref.shape[0]
    parts = [jnp.sum(basis_ref[k] * image, axis=0, keepdims=True) for k in range(krylov)]
    parts.append(jnp.sum(image * image, axis=0, keepdims=True))
    added = jnp.concatenate(parts, axis=0)

    @pl.when(step == 0)
    def _():
        sums_ref[: krylov + 1, :] = added
        sums_ref[krylov + 1 :, :] = mutual_ref[...]

    @pl.when(step > 0)
    def _():
        sums_ref[: krylov + 1, :] += added


def gather_back(ret, place_col, basis, mutual, spread):
    lines = basis.shape[0] + 1 + mutual.shape[0]
    total, width = ret.shape
    krylov, rows_dev = basis.shape[:2]
    rows = 256
    return pl.pallas_call(
        functools.partial(gather_kernel, spread),
        grid=(rows_dev // rows,),
        in_specs=[
            pl.BlockSpec(memory_space=pltpu.VMEM),
            pl.BlockSpec((rows, place_col.shape[1]), lambda i: (i, 0)),
            pl.BlockSpec((krylov, rows, width), lambda i: (0, i, 0)),
            whole(mutual.shape),
        ],
        out_specs=(pl.BlockSpec((rows, width), lambda i: (i, 0)), whole((lines, width))),
        out_shape=(
            jax.ShapeDtypeStruct((rows_dev, width), F32),
            jax.ShapeDtypeStruct((lines, width), F32),
        ),
        compiler_params=params(("arbitrary",)),
        cost_estimate=cost(2 * spread * total * rows_dev * width, 6 << 20),
        name="gather_back",
    )(ret, place_col, basis, mutual)


AXES = ("branch", "group")


def exchange(values, axes=AXES):
    return lax.all_to_all(values, axes, split_axis=0, concat_axis=0, tiled=True)


def swaps(values, axis):
    size = lax.axis_size(axis)
    return [values] + [
        lax.ppermute(values, axis, [(i, i ^ k) for i in range(size)]) for k in range(1, size)
    ]


def to_all(values, axes, size):
    return exchange(jnp.broadcast_to(values[None], (size,) + values.shape), axes)


def body(
    basis,
    spread_owner,
    spread_row,
    spread_weight,
    gram_term,
    near_block,
    near_list,
    leaf_basis,
    far_block,
    far_list,
    ascend,
    descend,
    top_block,
):
    branches = lax.axis_size("branch")
    groups = lax.axis_size("group")
    devices = branches * groups
    rows_dev, columns = basis.shape[1:]
    krylov = basis.shape[0]
    spread = spread_owner.shape[1]
    slots = 2 * spread * rows_dev // devices
    total = devices * slots
    leaves, rank = leaf_basis.shape[:2]
    sent, place = spread_out(
        kept(spread_owner.T), kept(spread_row.T), kept(spread_weight.T), kept(basis), devices, slots
    )
    sent, late_ascend, late_top, late_base, late_gram = lax.optimization_barrier(
        (sent, ascend, top_block, leaf_basis, gram_term)
    )
    got = exchange(sent)

    parts = columns // rank
    held = leaves * rank // parts
    packed = late_ascend.reshape(parts, held, rank).transpose(1, 0, 2).reshape(held, columns)
    columns_of = (jnp.arange(groups) ^ lax.axis_index("group")) % groups
    top = late_top.reshape(rank, groups, rank).transpose(1, 0, 2)[columns_of]

    raised = rise(late_base, late_gram)
    got, packed, top, raised = lax.optimization_barrier((got, packed, top, raised))
    dual, coeff, rows = collect(got, raised, packed, slots, branches, columns)
    coeff = kept(exchange(coeff, "branch"))
    first = refine(got, dual, kept(gram_term), slots)
    image = near_field(near_list, kept(near_block), first)
    dual, lift = prepare(image, kept(leaf_basis), kept(gram_term))
    coeff, dual, lift = lax.optimization_barrier((coeff, dual, lift))
    parents = swaps(parent_of(coeff, rank), "group")
    far = far_field(far_list, coeff, kept(far_block))
    replies = reply(dual, lift, far, kept(top), parents, kept(descend), kept(rows), slots)
    returned = exchange(replies.reshape(devices, slots, columns)).reshape(total, columns)
    pairs = [(i, j) for i in range(krylov) for j in range(i, krylov)]
    mutual = jnp.stack([jnp.sum(basis[i] * basis[j], axis=0) for i, j in pairs])
    primal, sums = gather_back(near_by(returned), kept(place.T), basis, mutual, spread)
    sums = jnp.sum(to_all(sums, AXES, devices), axis=0)
    mutual = sums[krylov + 1 :]

    total_rows = rows_dev * devices
    projection = sums[:krylov] / total_rows
    remainder = primal - jnp.sum(projection[:, None, :] * basis, axis=0)
    square = sums[krylov] / total_rows - 2.0 * jnp.sum(projection * projection, axis=0)
    for at, (i, j) in enumerate(pairs):
        times = 1.0 if i == j else 2.0
        square = square + times * projection[i] * projection[j] * mutual[at] / total_rows
    norm_scale = jnp.sqrt(jnp.maximum(square, 0.0) + 1e-06)
    return (remainder / norm_scale, jnp.concatenate([projection, norm_scale[None]], axis=0))


def solution(mesh):
    both = ("branch", "group")
    return jax.shard_map(
        body,
        mesh=mesh,
        in_specs=(
            P(None, both, None),
            P(both, None),
            P(both, None),
            P(both, None),
            P(both, None, None),
            P(both, None, None, None),
            P(both, None),
            P(both, None, None),
            P(both, None, None, None),
            P(both, None),
            P(both, None, None),
            P(both, None, None),
            P("group", None),
        ),
        out_specs=(P(both, None), P()),
        check_vma=False,
    )
```

```python
import functools

import jax
import jax.numpy as jnp
from jax import lax
from jax.experimental import pallas as pl
from jax.experimental.pallas import tpu as pltpu
from jax.sharding import PartitionSpec as P

F32 = jnp.float32
LOW = jnp.bfloat16
CODE = jnp.int16
TOP = 32767.0
REST = 65534.0
LOG2 = 0.6931471805599453
SPREAD_BLOCK = 1024
COLLECT_BLOCK = 512
REPLY_BLOCK = 1024
LANES = 128


def rounded(values):
    return values.astype(LOW)


def contract(pattern, first_op, second_op):
    return jnp.einsum(pattern, first_op, second_op, preferred_element_type=F32)


def dot(lhs, rhs, lhs_dim=1, rhs_dim=0):
    return lax.dot_general(
        lhs, rhs, (((lhs_dim,), (rhs_dim,)), ((), ())), preferred_element_type=F32
    )


def params(semantics=None, mib=24):
    return pltpu.CompilerParams(dimension_semantics=semantics, vmem_limit_bytes=mib << 20)


def whole(shape):
    zeros = (0,) * len(shape)
    return pl.BlockSpec(shape, lambda *_: zeros)


def in_hbm(shape, dtype):
    return pltpu.HBM(shape, dtype)


def in_vmem(shape, dtype):
    return pltpu.VMEM(shape, dtype)


def near_by(values):
    return pltpu.with_memory_space_constraint(values, pltpu.VMEM)


def kept(values):
    return pltpu.with_memory_space_constraint(values, pltpu.HBM)


def cost(flops, nbytes):
    return pl.CostEstimate(flops=int(flops), bytes_accessed=int(nbytes), transcendentals=0)


def column(row):
    size = row.shape[1]
    same = lax.broadcasted_iota(jnp.int32, (size, size), 0) == lax.broadcasted_iota(
        jnp.int32, (size, size), 1
    )
    return jnp.sum(jnp.where(same, row, 0.0), axis=1, keepdims=True)


def split(code):
    high = jnp.round(code * (1.0 / 256.0))
    return high, code - 256.0 * high


def find_routes(slots, owner_ref, row_ref, weight_ref, rank_ref, side_ref, place_ref):
    devices, rows_dev = rank_ref.shape
    spread = owner_ref.shape[0]
    width = side_ref.shape[2]
    ids = lax.broadcasted_iota(jnp.int32, (devices, rows_dev), 0)
    named = [owner_ref[s : s + 1, :] == ids for s in range(spread)]
    chosen = functools.reduce(jnp.logical_or, named)
    flag = jnp.where(chosen, 1.0, 0.0)
    lane = 128
    upper = jnp.where(
        lax.broadcasted_iota(jnp.int32, (lane, lane), 0)
        <= lax.broadcasted_iota(jnp.int32, (lane, lane), 1),
        1.0,
        0.0,
    ).astype(LOW)
    before = jnp.zeros((devices, 1), F32)
    pieces = []
    for start in range(0, rows_dev, lane):
        part = flag[:, start : start + lane]
        upto = dot(part.astype(LOW), upper)
        pieces.append(upto - part + before)
        before = before + upto[:, lane - 1 : lane]
    rank = jnp.concatenate(pieces, axis=1)
    rank_ref[...] = jnp.where(chosen, rank, -1.0)
    slot_ids = lax.broadcasted_iota(jnp.int32, (width, rows_dev), 0).astype(F32)
    place_ref[...] = jnp.zeros_like(place_ref)
    total = jnp.zeros((6 * devices, width), F32)
    for s in range(spread):
        slot = jnp.sum(jnp.where(named[s], rank, 0.0), axis=0, keepdims=True)
        place_ref[s : s + 1, :] = owner_ref[s : s + 1, :].astype(F32) * slots + slot
        weight = weight_ref[s : s + 1, :]
        place_ref[spread + s : spread + s + 1, :] = weight
        code = weight * TOP
        whole_code = jnp.round(code)
        rest_code = jnp.round((code - whole_code) * REST)
        fields = split(row_ref[s : s + 1, :].astype(F32)) + split(whole_code) + split(rest_code)
        lhs = jnp.concatenate([jnp.where(named[s], f, 0.0) for f in fields], axis=0).astype(LOW)
        total = total + dot(lhs, jnp.where(slot_ids == slot, 1.0, 0.0).astype(LOW), 1, 1)
    for i in range(3):
        high = total[2 * i * devices : (2 * i + 1) * devices]
        low = total[(2 * i + 1) * devices : (2 * i + 2) * devices]
        side_ref[i] = 256.0 * high + low


def spread_kernel(
    slots,
    owner_ref,
    row_ref,
    weight_ref,
    basis_hbm,
    out_ref,
    place_ref,
    vector_ref,
    rank_ref,
    side_ref,
    code_ref,
    level_ref,
    pick_ref,
    vector_sem,
):
    step = pl.program_id(0)
    columns = vector_ref.shape[1]

    @pl.when(step == 0)
    def _():
        copy = pltpu.make_async_copy(basis_hbm.at[basis_hbm.shape[0] - 1], vector_ref, vector_sem)
        copy.start()
        find_routes(slots, owner_ref, row_ref, weight_ref, rank_ref, side_ref, place_ref)
        copy.wait()
        vector = vector_ref[...]
        peak = jnp.maximum(jnp.max(jnp.abs(vector), axis=0, keepdims=True), 1e-30)
        level = jnp.floor(jnp.log(peak) * (1.0 / LOG2)) + 1.0
        level_ref[...] = level
        code = jnp.clip(jnp.round(vector * (TOP / jnp.exp(level * LOG2))), -TOP, TOP)
        high, low = split(code)
        code_ref[:, :columns] = high.astype(LOW)
        code_ref[:, columns:] = low.astype(LOW)

    rows_dev = rank_ref.shape[1]
    owners = SPREAD_BLOCK // slots
    slot_ids = lax.broadcasted_iota(jnp.int32, (slots, rows_dev), 0).astype(F32)
    for j in range(owners):
        rank = rank_ref[pl.ds(step * owners + j, 1), :]
        pick_ref[j * slots : (j + 1) * slots, :] = jnp.where(slot_ids == rank, 1.0, 0.0).astype(LOW)
    picked = dot(pick_ref[...], code_ref[...])
    codes = (256.0 * picked[:, :columns] + picked[:, columns:]).astype(jnp.int32).astype(CODE)
    line = lax.broadcasted_iota(jnp.int32, (8, LANES), 0)
    parts = columns // LANES
    for j in range(owners):
        extra = jnp.zeros((8, LANES), F32)
        for k in range(3):
            extra = jnp.where(line == k, side_ref[k, pl.ds(step * owners + j, 1), :], extra)
        for h in range(parts):
            at = slice(h * LANES, (h + 1) * LANES)
            extra = jnp.where(line == 3 + h, level_ref[:, at], extra)
            out_ref[j, h * slots : (h + 1) * slots, :] = codes[j * slots : (j + 1) * slots, at]
        out_ref[j, parts * slots :, :] = extra.astype(jnp.int32).astype(CODE)


def spread_out(owner_t, row_t, weight_t, basis, devices, slots):
    rows_dev, columns = basis.shape[1:]
    owners = SPREAD_BLOCK // slots
    shape = (devices, columns // LANES * slots + 8, LANES)
    return pl.pallas_call(
        functools.partial(spread_kernel, slots),
        grid=(devices // owners,),
        in_specs=[
            whole(owner_t.shape),
            whole(row_t.shape),
            whole(weight_t.shape),
            pl.BlockSpec(memory_space=pltpu.HBM),
        ],
        out_specs=(
            pl.BlockSpec((owners,) + shape[1:], lambda i: (i, 0, 0)),
            whole((8, rows_dev)),
        ),
        out_shape=(in_hbm(shape, CODE), in_hbm((8, rows_dev), F32)),
        scratch_shapes=[
            pltpu.VMEM((rows_dev, columns), F32),
            pltpu.VMEM((devices, rows_dev), F32),
            pltpu.VMEM((3, devices, LANES), F32),
            pltpu.VMEM((rows_dev, 2 * columns), LOW),
            pltpu.VMEM((1, columns), F32),
            pltpu.VMEM((SPREAD_BLOCK, rows_dev), LOW),
            pltpu.SemaphoreType.DMA,
        ],
        compiler_params=params(("arbitrary",)),
        cost_estimate=cost(4 * devices * slots * rows_dev * columns, 4 << 20),
        name="spread_out",
    )(owner_t, row_t, weight_t, basis)


def add_slots(slots, low_part, got_ref, rows_ref, sum_ref, picks, terms):
    rows_dev, width = sum_ref.shape
    owners = COLLECT_BLOCK // slots
    parts = width // LANES
    blocks = got_ref.shape[0] // owners
    tile = 16
    ids = lax.broadcasted_iota(jnp.int32, (rows_dev, slots), 0).astype(CODE)
    one, zero = jnp.ones((rows_dev, slots), LOW), jnp.zeros((rows_dev, slots), LOW)

    def build(block):
        pick_ref, term_ref = picks[block % 2], terms[block % 2]
        for j in range(owners):
            at = slice(j * slots, (j + 1) * slots)
            source = block * owners + j
            extra = got_ref[source, parts * slots :, :].astype(jnp.int32)
            row = jnp.broadcast_to(extra[0:1, :slots], (tile, slots)).astype(CODE)
            row = jnp.broadcast_to(row[None], (rows_dev // tile, tile, slots))
            pick_ref[:, at] = jnp.where(ids == row.reshape(rows_dev, slots), one, zero)
            extra = extra.astype(F32)
            weight = (extra[1:2, :slots] + extra[2:3, :slots] * (1.0 / REST)) * (1.0 / TOP)
            weight = column(weight)
            if rows_ref is not None:
                rows_ref[source : source + 1, :] = extra[0:1, :]
            for h in range(parts):
                scale = jnp.exp(extra[3 + h : 4 + h, :] * LOG2) * (1.0 / TOP)
                codes = got_ref[source, h * slots : (h + 1) * slots, :].astype(jnp.int32).astype(F32)
                values = codes * weight * scale
                term = values.astype(LOW)
                if low_part:
                    term = (values - term.astype(F32)).astype(LOW)
                term_ref[at, h * LANES : (h + 1) * LANES] = term

    build(0)
    for block in range(blocks):
        if block + 1 < blocks:
            build(block + 1)
        added = dot(picks[block % 2][...], terms[block % 2][...])
        sum_ref[...] = added if block == 0 else sum_ref[...] + added


def rise_kernel(base_ref, gram_ref, out_ref):
    for l in range(base_ref.shape[0]):
        base = base_ref[l]
        out_ref[l] = (base.astype(F32) + dot(base, gram_ref[l], 1, 1)).astype(LOW)


def rise(base, gram):
    return pl.pallas_call(
        rise_kernel,
        out_shape=in_vmem(base.shape, LOW),
        compiler_params=params(mib=8),
        cost_estimate=cost(2 * gram.size * base.shape[1], 2 * gram.size),
        name="rise",
    )(base, gram)


def collect_kernel(
    slots,
    got_ref,
    rise_ref,
    ascend_ref,
    dual_ref,
    coeff_ref,
    rows_ref,
    pick_a,
    pick_b,
    term_a,
    term_b,
):
    add_slots(slots, False, got_ref, rows_ref, dual_ref, (pick_a, pick_b), (term_a, term_b))
    leaves, rank, leaf = rise_ref.shape
    for b in range(coeff_ref.shape[0]):
        coeff_ref[b, leaves * rank :, :] = ascend_ref[...]
    for l in range(leaves):
        dual = dual_ref[l * leaf : (l + 1) * leaf, :]
        coeff = dot(rise_ref[l], dual.astype(LOW)).astype(LOW)
        for b in range(coeff_ref.shape[0]):
            coeff_ref[b, l * rank : (l + 1) * rank, :] = coeff


def slot_scratch(rows_dev, width):
    return [
        pltpu.VMEM((rows_dev, COLLECT_BLOCK), LOW),
        pltpu.VMEM((rows_dev, COLLECT_BLOCK), LOW),
        pltpu.VMEM((COLLECT_BLOCK, width), LOW),
        pltpu.VMEM((COLLECT_BLOCK, width), LOW),
    ]


def collect(got, lift, ascend, slots, branches, width):
    devices = got.shape[0]
    leaves, rank, leaf = lift.shape
    rows_dev = leaves * leaf
    sent_rows = leaves * rank + ascend.shape[0]
    direct = pl.BlockSpec(memory_space=pltpu.VMEM)
    return pl.pallas_call(
        functools.partial(collect_kernel, slots),
        in_specs=[direct] * 3,
        out_specs=[direct] * 3,
        out_shape=(
            in_vmem((rows_dev, width), F32),
            in_hbm((branches, sent_rows, width), LOW),
            in_hbm((devices, LANES), F32),
        ),
        scratch_shapes=slot_scratch(rows_dev, width),
        compiler_params=params(),
        cost_estimate=cost(2 * devices * slots * rows_dev * width, 4 << 20),
        name="collect",
    )(got, lift, ascend)


def refine_kernel(
    slots,
    got_ref,
    dual_ref,
    gram_hbm,
    out_ref,
    sum_ref,
    gram_ref,
    gram_sem,
    pick_a,
    pick_b,
    term_a,
    term_b,
):
    gram_copy = pltpu.make_async_copy(gram_hbm, gram_ref, gram_sem)
    gram_copy.start()
    add_slots(slots, True, got_ref, None, sum_ref, (pick_a, pick_b), (term_a, term_b))
    gram_copy.wait()
    leaves, leaf = gram_ref.shape[:2]
    for l in range(leaves):
        at = slice(l * leaf, (l + 1) * leaf)
        dual = dual_ref[at, :] + sum_ref[at, :]
        out_ref[at, :] = dual + dot(gram_ref[l], dual.astype(LOW), 0, 0)


def refine(got, dual, gram, slots):
    rows_dev, width = dual.shape
    devices = got.shape[0]
    direct = pl.BlockSpec(memory_space=pltpu.VMEM)
    return pl.pallas_call(
        functools.partial(refine_kernel, slots),
        in_specs=[direct, direct, pl.BlockSpec(memory_space=pltpu.HBM)],
        out_specs=direct,
        out_shape=in_vmem(dual.shape, F32),
        scratch_shapes=[
            pltpu.VMEM((rows_dev, width), F32),
            pltpu.VMEM(gram.shape, LOW),
            pltpu.SemaphoreType.DMA,
        ]
        + slot_scratch(rows_dev, width),
        compiler_params=params(),
        cost_estimate=cost(2 * devices * slots * rows_dev * width, 4 << 20),
        name="refine",
    )(got, dual, gram)


def parent_kernel(coeff_ref, out_ref):
    rank, width = out_ref.shape
    branches, rows = coeff_ref.shape[:2]
    parts = width // rank
    leaves = rows * parts // (rank * (parts + 1))
    held = leaves * rank // parts
    sums = [jnp.zeros((held, width), F32) for _ in range(rank // held)]
    for b in range(branches):
        packed = coeff_ref[b, leaves * rank :, :]
        for q in range(parts):
            leaf, at = divmod(q * held, rank)
            term = dot(
                packed[:, q * rank : (q + 1) * rank], coeff_ref[b, leaf * rank : (leaf + 1) * rank, :]
            )
            sums[at // held] = sums[at // held] + term
    for i, total in enumerate(sums):
        out_ref[i * held : (i + 1) * held, :] = total.astype(LOW)


def parent_of(coeff, rank):
    width = coeff.shape[2]
    return pl.pallas_call(
        parent_kernel,
        out_shape=in_vmem((rank, width), LOW),
        compiler_params=params(mib=6),
        cost_estimate=cost(2 * coeff.size * rank, 1 << 20),
        name="parent_of",
    )(coeff)


def far_kernel(list_ref, coeff_ref, block_ref, out_ref):
    leaves, items, rank = block_ref.shape[:3]
    for l in range(leaves):
        total = jnp.zeros(out_ref.shape[1:], F32)
        for k in range(items):
            source = list_ref[l, k]
            at = pl.ds(pl.multiple_of(source % leaves * rank, rank), rank)
            total = total + dot(block_ref[l, k], coeff_ref[source // leaves, at, :])
        out_ref[l] = total


def far_field(far_list, coeff, far_block):
    leaves, items, rank = far_block.shape[:3]
    width = coeff.shape[2]
    return pl.pallas_call(
        far_kernel,
        grid_spec=pltpu.PrefetchScalarGridSpec(
            num_scalar_prefetch=1,
            grid=(1,),
            in_specs=[whole(coeff.shape), whole(far_block.shape)],
            out_specs=whole((leaves, rank, width)),
        ),
        out_shape=jax.ShapeDtypeStruct((leaves, rank, width), F32),
        compiler_params=params(("arbitrary",), 6),
        cost_estimate=cost(2 * far_block.size * width, 1 << 20),
        name="far_field",
    )(far_list, coeff, far_block)


def near_kernel(list_ref, block_ref, first_ref, out_ref, low_ref):
    leaf, item = pl.program_id(0), pl.program_id(1)
    size = out_ref.shape[0]

    @pl.when((leaf == 0) & (item == 0))
    def _():
        for l in range(low_ref.shape[0]):
            low_ref[l] = first_ref[l * size : (l + 1) * size, :].astype(LOW)

    count = block_ref.shape[1]
    term = dot(block_ref[0, 0], low_ref[list_ref[leaf, item * count]])
    for k in range(1, count):
        term = term + dot(block_ref[0, k], low_ref[list_ref[leaf, item * count + k]])

    @pl.when(item == 0)
    def _():
        out_ref[...] = first_ref[pl.ds(pl.multiple_of(leaf * size, size), size), :] + term

    @pl.when(item > 0)
    def _():
        out_ref[...] += term


def near_field(near_list, near_block, first):
    leaves, items, leaf = near_block.shape[:3]
    width = first.shape[1]
    count = 4 if items % 4 == 0 else 1
    return pl.pallas_call(
        near_kernel,
        grid_spec=pltpu.PrefetchScalarGridSpec(
            num_scalar_prefetch=1,
            grid=(leaves, items // count),
            in_specs=[
                pl.BlockSpec((1, count, leaf, leaf), lambda l, k, _: (l, k, 0, 0)),
                whole(first.shape),
            ],
            out_specs=pl.BlockSpec((leaf, width), lambda l, k, _: (l, 0)),
            scratch_shapes=[pltpu.VMEM((leaves, leaf, width), LOW)],
        ),
        out_shape=in_vmem(first.shape, F32),
        compiler_params=params(("arbitrary", "arbitrary"), 12),
        cost_estimate=cost(2 * near_block.size * width, 2 * near_block.size),
        name="near_field",
    )(near_list, near_block, first)


def prepare_kernel(image_ref, base_ref, gram_ref, dual_ref, lift_ref):
    leaves, leaf = gram_ref.shape[:2]
    ids = lax.broadcasted_iota(jnp.int32, (leaf, leaf), 0)
    same = ids == lax.broadcasted_iota(jnp.int32, (leaf, leaf), 1)
    unit = jnp.where(same, 1.0, 0.0).astype(LOW)
    for l in range(leaves):
        at = slice(l * leaf, (l + 1) * leaf)
        image = image_ref[at, :]
        dual_ref[at, :] = image + dot(gram_ref[l], image.astype(LOW))
        lifted = dot(unit, base_ref[l], 1, 1) + dot(gram_ref[l], base_ref[l], 1, 1)
        parts = [lifted if i == l else jnp.zeros_like(lifted) for i in range(leaves)]
        lift_ref[at, :] = jnp.concatenate(parts, axis=1).astype(LOW)


def prepare(image, base, gram):
    rows_dev, width = image.shape
    lanes = base.shape[0] * base.shape[1]
    return pl.pallas_call(
        prepare_kernel,
        out_shape=(in_vmem((rows_dev, width), F32), in_vmem((rows_dev, lanes), LOW)),
        compiler_params=params(mib=12),
        cost_estimate=cost(2 * gram.size * (width + 2 * lanes), 4 << 20),
        name="prepare",
    )(image, base, gram)


def reply_kernel(slots, *refs):
    dual_ref, lift_ref, far_ref, top_ref, descend_ref, rows_ref = refs[:6]
    parents, (out_ref, field_ref, low_ref, pick_ref) = refs[6:-4], refs[-4:]
    step = pl.program_id(0)

    @pl.when(step == 0)
    def _():
        leaves, rank = far_ref.shape[:2]
        field = dot(top_ref[0], parents[0][...])
        for k in range(1, len(parents)):
            field = field + dot(top_ref[k], parents[k][...])
        field = field.astype(LOW)
        for l in range(leaves):
            descent = far_ref[l] + dot(descend_ref[l], field)
            field_ref[l * rank : (l + 1) * rank, :] = descent.astype(LOW)
        low_ref[...] = (dual_ref[...] + dot(lift_ref[...], field_ref[...])).astype(LOW)

    owners = REPLY_BLOCK // slots
    ids = lax.broadcasted_iota(jnp.int32, (slots, low_ref.shape[0]), 1).astype(F32)
    for j in range(owners):
        row = column(rows_ref[pl.ds(step * owners + j, 1), :][:, :slots])
        pick_ref[j * slots : (j + 1) * slots, :] = jnp.where(ids == row, 1.0, 0.0).astype(LOW)
    out_ref[...] = dot(pick_ref[...], low_ref[...]).astype(LOW)


def reply(dual, lift, far, top, parents, descend, rows, slots):
    rows_dev, width = dual.shape
    total = rows.shape[0] * slots
    args = (far, top, descend, rows, *parents)
    direct = pl.BlockSpec(memory_space=pltpu.VMEM)
    return pl.pallas_call(
        functools.partial(reply_kernel, slots),
        grid=(total // REPLY_BLOCK,),
        in_specs=[direct, direct] + [whole(a.shape) for a in args[:4]] + [direct] * len(parents),
        out_specs=pl.BlockSpec((REPLY_BLOCK, width), lambda i: (i, 0)),
        out_shape=in_hbm((total, width), LOW),
        scratch_shapes=[
            pltpu.VMEM((lift.shape[1], width), LOW),
            pltpu.VMEM((rows_dev, width), LOW),
            pltpu.VMEM((REPLY_BLOCK, rows_dev), LOW),
        ],
        compiler_params=params(("arbitrary",), 16),
        cost_estimate=cost(2 * total * rows_dev * width, 4 << 20),
        name="reply",
    )(dual, lift, *args)


def gather_kernel(spread, ret_ref, place_ref, basis_ref, mutual_ref, image_ref, sums_ref):
    step = pl.program_id(0)
    rows = place_ref.shape[0]
    total = ret_ref.shape[0]
    ids = lax.broadcasted_iota(jnp.int32, (rows, total), 1).astype(F32)
    image = jnp.zeros(image_ref.shape, F32)
    for s in range(spread):
        pick = jnp.where(ids == place_ref[:, s : s + 1], 1.0, 0.0).astype(LOW)
        image = image + place_ref[:, spread + s : spread + s + 1] * dot(pick, ret_ref[...])
    image_ref[...] = image
    krylov = basis_ref.shape[0]
    parts = [jnp.sum(basis_ref[k] * image, axis=0, keepdims=True) for k in range(krylov)]
    parts.append(jnp.sum(image * image, axis=0, keepdims=True))
    added = jnp.concatenate(parts, axis=0)

    @pl.when(step == 0)
    def _():
        sums_ref[: krylov + 1, :] = added
        sums_ref[krylov + 1 :, :] = mutual_ref[...]

    @pl.when(step > 0)
    def _():
        sums_ref[: krylov + 1, :] += added


def gather_back(ret, place_col, basis, mutual, spread):
    lines = basis.shape[0] + 1 + mutual.shape[0]
    total, width = ret.shape
    krylov, rows_dev = basis.shape[:2]
    rows = 256
    return pl.pallas_call(
        functools.partial(gather_kernel, spread),
        grid=(rows_dev // rows,),
        in_specs=[
            pl.BlockSpec(memory_space=pltpu.VMEM),
            pl.BlockSpec((rows, place_col.shape[1]), lambda i: (i, 0)),
            pl.BlockSpec((krylov, rows, width), lambda i: (0, i, 0)),
            whole(mutual.shape),
        ],
        out_specs=(pl.BlockSpec((rows, width), lambda i: (i, 0)), whole((lines, width))),
        out_shape=(
            jax.ShapeDtypeStruct((rows_dev, width), F32),
            jax.ShapeDtypeStruct((lines, width), F32),
        ),
        compiler_params=params(("arbitrary",)),
        cost_estimate=cost(2 * spread * total * rows_dev * width, 6 << 20),
        name="gather_back",
    )(ret, place_col, basis, mutual)


AXES = ("branch", "group")


def exchange(values, axes=AXES):
    return lax.all_to_all(values, axes, split_axis=0, concat_axis=0, tiled=True)


def swaps(values, axis):
    size = lax.axis_size(axis)
    return [values] + [
        lax.ppermute(values, axis, [(i, i ^ k) for i in range(size)]) for k in range(1, size)
    ]


def to_all(values, axes, size):
    return exchange(jnp.broadcast_to(values[None], (size,) + values.shape), axes)


def body(
    basis,
    spread_owner,
    spread_row,
    spread_weight,
    gram_term,
    near_block,
    near_list,
    leaf_basis,
    far_block,
    far_list,
    ascend,
    descend,
    top_block,
):
    branches = lax.axis_size("branch")
    groups = lax.axis_size("group")
    devices = branches * groups
    rows_dev, columns = basis.shape[1:]
    krylov = basis.shape[0]
    spread = spread_owner.shape[1]
    slots = 2 * spread * rows_dev // devices
    total = devices * slots
    leaves, rank = leaf_basis.shape[:2]
    sent, place = spread_out(
        kept(spread_owner.T), kept(spread_row.T), kept(spread_weight.T), kept(basis), devices, slots
    )
    sent, late_ascend, late_top, late_base, late_gram = lax.optimization_barrier(
        (sent, ascend, top_block, leaf_basis, gram_term)
    )
    got = exchange(sent)

    parts = columns // rank
    held = leaves * rank // parts
    packed = late_ascend.reshape(parts, held, rank).transpose(1, 0, 2).reshape(held, columns)
    columns_of = (jnp.arange(groups) ^ lax.axis_index("group")) % groups
    top = late_top.reshape(rank, groups, rank).transpose(1, 0, 2)[columns_of]

    raised = rise(late_base, late_gram)
    got, packed, top, raised = lax.optimization_barrier((got, packed, top, raised))
    dual, coeff, rows = collect(got, raised, packed, slots, branches, columns)
    coeff = kept(exchange(coeff, "branch"))
    first = refine(got, dual, kept(gram_term), slots)
    image = near_field(near_list, kept(near_block), first)
    dual, lift = prepare(image, kept(leaf_basis), kept(gram_term))
    coeff, dual, lift = lax.optimization_barrier((coeff, dual, lift))
    parents = swaps(parent_of(coeff, rank), "group")
    far = far_field(far_list, coeff, kept(far_block))
    replies = reply(dual, lift, far, kept(top), parents, kept(descend), kept(rows), slots)
    returned = exchange(replies.reshape(devices, slots, columns)).reshape(total, columns)
    pairs = [(i, j) for i in range(krylov) for j in range(i, krylov)]
    mutual = jnp.stack([jnp.sum(basis[i] * basis[j], axis=0) for i, j in pairs])
    mutual = sum(swaps(mutual, "group"))
    share = -(-len(pairs) // groups)
    mutual = jnp.pad(mutual, ((0, share * groups - len(pairs)), (0, 0)))
    own = lax.dynamic_slice_in_dim(mutual, share * lax.axis_index("group"), share, 0)
    primal, sums = gather_back(near_by(returned), kept(place.T), basis, own, spread)
    everyone = to_all(sums, AXES, devices)
    sums = jnp.sum(everyone[:, : krylov + 1], axis=0)
    mutual = jnp.sum(everyone.reshape(branches, groups, -1, columns)[:, :, krylov + 1 :], axis=0)
    mutual = mutual.reshape(share * groups, columns)

    total_rows = rows_dev * devices
    projection = sums[:krylov] / total_rows
    remainder = primal - jnp.sum(projection[:, None, :] * basis, axis=0)
    square = sums[krylov] / total_rows - 2.0 * jnp.sum(projection * projection, axis=0)
    for at, (i, j) in enumerate(pairs):
        times = 1.0 if i == j else 2.0
        square = square + times * projection[i] * projection[j] * mutual[at] / total_rows
    norm_scale = jnp.sqrt(jnp.maximum(square, 0.0) + 1e-06)
    return (remainder / norm_scale, jnp.concatenate([projection, norm_scale[None]], axis=0))


def solution(mesh):
    both = ("branch", "group")
    return jax.shard_map(
        body,
        mesh=mesh,
        in_specs=(
            P(None, both, None),
            P(both, None),
            P(both, None),
            P(both, None),
            P(both, None, None),
            P(both, None, None, None),
            P(both, None),
            P(both, None, None),
            P(both, None, None, None),
            P(both, None),
            P(both, None, None),
            P(both, None, None),
            P("group", None),
        ),
        out_specs=(P(both, None), P()),
        check_vma=False,
    )
```

```python
import functools

import jax
import jax.numpy as jnp
from jax import lax
from jax.experimental import pallas as pl
from jax.experimental.pallas import tpu as pltpu
from jax.sharding import PartitionSpec as P

F32 = jnp.float32
LOW = jnp.bfloat16
CODE = jnp.int16
TOP = 32767.0
REST = 65534.0
LOG2 = 0.6931471805599453
SPREAD_BLOCK = 1024
COLLECT_BLOCK = 512
REPLY_BLOCK = 512
GATHER_BLOCK = 256
LANES = 128


def rounded(values):
    return values.astype(LOW)


def contract(pattern, first_op, second_op):
    return jnp.einsum(pattern, first_op, second_op, preferred_element_type=F32)


def dot(lhs, rhs, lhs_dim=1, rhs_dim=0):
    return lax.dot_general(
        lhs, rhs, (((lhs_dim,), (rhs_dim,)), ((), ())), preferred_element_type=F32
    )


def params(semantics=None, mib=24):
    return pltpu.CompilerParams(dimension_semantics=semantics, vmem_limit_bytes=mib << 20)


def whole(shape):
    zeros = (0,) * len(shape)
    return pl.BlockSpec(shape, lambda *_: zeros)


def in_hbm(shape, dtype):
    return pltpu.HBM(shape, dtype)


def in_vmem(shape, dtype):
    return pltpu.VMEM(shape, dtype)


def near_by(values):
    return pltpu.with_memory_space_constraint(values, pltpu.VMEM)


def kept(values):
    return pltpu.with_memory_space_constraint(values, pltpu.HBM)


def cost(flops, nbytes):
    return pl.CostEstimate(flops=int(flops), bytes_accessed=int(nbytes), transcendentals=0)


def column(row):
    size = row.shape[1]
    same = lax.broadcasted_iota(jnp.int32, (size, size), 0) == lax.broadcasted_iota(
        jnp.int32, (size, size), 1
    )
    return jnp.sum(jnp.where(same, row, 0.0), axis=1, keepdims=True)


def split(code):
    high = jnp.round(code * (1.0 / 256.0))
    return high, code - 256.0 * high


def find_routes(slots, owner_ref, row_ref, weight_ref, rank_ref, side_ref, place_ref):
    devices, rows_dev = rank_ref.shape
    spread = owner_ref.shape[0]
    width = side_ref.shape[2]
    ids = lax.broadcasted_iota(jnp.int32, (devices, rows_dev), 0)
    named = [owner_ref[s : s + 1, :] == ids for s in range(spread)]
    chosen = functools.reduce(jnp.logical_or, named)
    flag = jnp.where(chosen, 1.0, 0.0)
    lane = 128
    upper = jnp.where(
        lax.broadcasted_iota(jnp.int32, (lane, lane), 0)
        <= lax.broadcasted_iota(jnp.int32, (lane, lane), 1),
        1.0,
        0.0,
    ).astype(LOW)
    before = jnp.zeros((devices, 1), F32)
    pieces = []
    for start in range(0, rows_dev, lane):
        part = flag[:, start : start + lane]
        upto = dot(part.astype(LOW), upper)
        pieces.append(upto - part + before)
        before = before + upto[:, lane - 1 : lane]
    rank = jnp.concatenate(pieces, axis=1)
    rank_ref[...] = jnp.where(chosen, rank, -1.0)
    slot_ids = lax.broadcasted_iota(jnp.int32, (width, rows_dev), 0).astype(F32)
    place_ref[...] = jnp.zeros_like(place_ref)
    total = jnp.zeros((6 * devices, width), F32)
    for s in range(spread):
        slot = jnp.sum(jnp.where(named[s], rank, 0.0), axis=0, keepdims=True)
        place_ref[s : s + 1, :] = owner_ref[s : s + 1, :].astype(F32) * slots + slot
        weight = weight_ref[s : s + 1, :]
        place_ref[spread + s : spread + s + 1, :] = weight
        code = weight * TOP
        whole_code = jnp.round(code)
        rest_code = jnp.round((code - whole_code) * REST)
        fields = split(row_ref[s : s + 1, :].astype(F32)) + split(whole_code) + split(rest_code)
        lhs = jnp.concatenate([jnp.where(named[s], f, 0.0) for f in fields], axis=0).astype(LOW)
        total = total + dot(lhs, jnp.where(slot_ids == slot, 1.0, 0.0).astype(LOW), 1, 1)
    for i in range(3):
        high = total[2 * i * devices : (2 * i + 1) * devices]
        low = total[(2 * i + 1) * devices : (2 * i + 2) * devices]
        side_ref[i] = 256.0 * high + low


def spread_kernel(
    slots,
    owner_ref,
    row_ref,
    weight_ref,
    basis_hbm,
    out_ref,
    place_ref,
    vector_ref,
    rank_ref,
    side_ref,
    code_ref,
    level_ref,
    pick_ref,
    vector_sem,
):
    step = pl.program_id(0)
    columns = vector_ref.shape[1]

    @pl.when(step == 0)
    def _():
        copy = pltpu.make_async_copy(basis_hbm.at[basis_hbm.shape[0] - 1], vector_ref, vector_sem)
        copy.start()
        find_routes(slots, owner_ref, row_ref, weight_ref, rank_ref, side_ref, place_ref)
        copy.wait()
        vector = vector_ref[...]
        peak = jnp.maximum(jnp.max(jnp.abs(vector), axis=0, keepdims=True), 1e-30)
        level = jnp.floor(jnp.log(peak) * (1.0 / LOG2)) + 1.0
        level_ref[...] = level
        code = jnp.clip(jnp.round(vector * (TOP / jnp.exp(level * LOG2))), -TOP, TOP)
        high, low = split(code)
        code_ref[:, :columns] = high.astype(LOW)
        code_ref[:, columns:] = low.astype(LOW)

    rows_dev = rank_ref.shape[1]
    owners = SPREAD_BLOCK // slots
    slot_ids = lax.broadcasted_iota(jnp.int32, (slots, rows_dev), 0).astype(F32)
    for j in range(owners):
        rank = rank_ref[pl.ds(step * owners + j, 1), :]
        pick_ref[j * slots : (j + 1) * slots, :] = jnp.where(slot_ids == rank, 1.0, 0.0).astype(LOW)
    picked = dot(pick_ref[...], code_ref[...])
    codes = (256.0 * picked[:, :columns] + picked[:, columns:]).astype(jnp.int32).astype(CODE)
    line = lax.broadcasted_iota(jnp.int32, (8, LANES), 0)
    parts = columns // LANES
    for j in range(owners):
        extra = jnp.zeros((8, LANES), F32)
        for k in range(3):
            extra = jnp.where(line == k, side_ref[k, pl.ds(step * owners + j, 1), :], extra)
        for h in range(parts):
            at = slice(h * LANES, (h + 1) * LANES)
            extra = jnp.where(line == 3 + h, level_ref[:, at], extra)
            out_ref[j, h * slots : (h + 1) * slots, :] = codes[j * slots : (j + 1) * slots, at]
        out_ref[j, parts * slots :, :] = extra.astype(jnp.int32).astype(CODE)


def spread_out(owner_t, row_t, weight_t, basis, devices, slots):
    rows_dev, columns = basis.shape[1:]
    owners = SPREAD_BLOCK // slots
    shape = (devices, columns // LANES * slots + 8, LANES)
    return pl.pallas_call(
        functools.partial(spread_kernel, slots),
        grid=(devices // owners,),
        in_specs=[
            whole(owner_t.shape),
            whole(row_t.shape),
            whole(weight_t.shape),
            pl.BlockSpec(memory_space=pltpu.HBM),
        ],
        out_specs=(
            pl.BlockSpec((owners,) + shape[1:], lambda i: (i, 0, 0)),
            whole((8, rows_dev)),
        ),
        out_shape=(in_hbm(shape, CODE), in_hbm((8, rows_dev), F32)),
        scratch_shapes=[
            pltpu.VMEM((rows_dev, columns), F32),
            pltpu.VMEM((devices, rows_dev), F32),
            pltpu.VMEM((3, devices, LANES), F32),
            pltpu.VMEM((rows_dev, 2 * columns), LOW),
            pltpu.VMEM((1, columns), F32),
            pltpu.VMEM((SPREAD_BLOCK, rows_dev), LOW),
            pltpu.SemaphoreType.DMA,
        ],
        compiler_params=params(("arbitrary",)),
        cost_estimate=cost(4 * devices * slots * rows_dev * columns, 4 << 20),
        name="spread_out",
    )(owner_t, row_t, weight_t, basis)


def add_slots(slots, low_part, got_ref, rows_ref, sum_ref, picks, terms):
    rows_dev, width = sum_ref.shape
    owners = COLLECT_BLOCK // slots
    parts = width // LANES
    blocks = got_ref.shape[0] // owners
    tile = 16
    ids = lax.broadcasted_iota(jnp.int32, (rows_dev, slots), 0).astype(CODE)
    one, zero = jnp.ones((rows_dev, slots), LOW), jnp.zeros((rows_dev, slots), LOW)

    def build(block):
        pick_ref, term_ref = picks[block % 2], terms[block % 2]
        for j in range(owners):
            at = slice(j * slots, (j + 1) * slots)
            source = block * owners + j
            extra = got_ref[source, parts * slots :, :].astype(jnp.int32)
            row = jnp.broadcast_to(extra[0:1, :slots], (tile, slots)).astype(CODE)
            row = jnp.broadcast_to(row[None], (rows_dev // tile, tile, slots))
            pick_ref[:, at] = jnp.where(ids == row.reshape(rows_dev, slots), one, zero)
            extra = extra.astype(F32)
            weight = (extra[1:2, :slots] + extra[2:3, :slots] * (1.0 / REST)) * (1.0 / TOP)
            weight = column(weight)
            if rows_ref is not None:
                rows_ref[source : source + 1, :] = extra[0:1, :]
            for h in range(parts):
                scale = jnp.exp(extra[3 + h : 4 + h, :] * LOG2) * (1.0 / TOP)
                codes = got_ref[source, h * slots : (h + 1) * slots, :].astype(jnp.int32).astype(F32)
                values = codes * weight * scale
                term = values.astype(LOW)
                if low_part:
                    term = (values - term.astype(F32)).astype(LOW)
                term_ref[at, h * LANES : (h + 1) * LANES] = term

    build(0)
    for block in range(blocks):
        if block + 1 < blocks:
            build(block + 1)
        added = dot(picks[block % 2][...], terms[block % 2][...])
        sum_ref[...] = added if block == 0 else sum_ref[...] + added


def rise_kernel(base_ref, gram_ref, out_ref):
    for l in range(base_ref.shape[0]):
        base = base_ref[l]
        out_ref[l] = (base.astype(F32) + dot(base, gram_ref[l], 1, 1)).astype(LOW)


def rise(base, gram):
    return pl.pallas_call(
        rise_kernel,
        out_shape=in_vmem(base.shape, LOW),
        compiler_params=params(mib=8),
        cost_estimate=cost(2 * gram.size * base.shape[1], 2 * gram.size),
        name="rise",
    )(base, gram)


def collect_kernel(
    slots,
    got_ref,
    rise_ref,
    ascend_ref,
    dual_ref,
    coeff_ref,
    rows_ref,
    pick_a,
    pick_b,
    term_a,
    term_b,
):
    add_slots(slots, False, got_ref, rows_ref, dual_ref, (pick_a, pick_b), (term_a, term_b))
    leaves, rank, leaf = rise_ref.shape
    for b in range(coeff_ref.shape[0]):
        coeff_ref[b, leaves * rank :, :] = ascend_ref[...]
    for l in range(leaves):
        dual = dual_ref[l * leaf : (l + 1) * leaf, :]
        coeff = dot(rise_ref[l], dual.astype(LOW)).astype(LOW)
        for b in range(coeff_ref.shape[0]):
            coeff_ref[b, l * rank : (l + 1) * rank, :] = coeff


def slot_scratch(rows_dev, width):
    return [
        pltpu.VMEM((rows_dev, COLLECT_BLOCK), LOW),
        pltpu.VMEM((rows_dev, COLLECT_BLOCK), LOW),
        pltpu.VMEM((COLLECT_BLOCK, width), LOW),
        pltpu.VMEM((COLLECT_BLOCK, width), LOW),
    ]


def collect(got, lift, ascend, slots, branches, width):
    devices = got.shape[0]
    leaves, rank, leaf = lift.shape
    rows_dev = leaves * leaf
    sent_rows = leaves * rank + ascend.shape[0]
    direct = pl.BlockSpec(memory_space=pltpu.VMEM)
    return pl.pallas_call(
        functools.partial(collect_kernel, slots),
        in_specs=[direct] * 3,
        out_specs=[direct] * 3,
        out_shape=(
            in_vmem((rows_dev, width), F32),
            in_hbm((branches, sent_rows, width), LOW),
            in_hbm((devices, LANES), F32),
        ),
        scratch_shapes=slot_scratch(rows_dev, width),
        compiler_params=params(),
        cost_estimate=cost(2 * devices * slots * rows_dev * width, 4 << 20),
        name="collect",
    )(got, lift, ascend)


def refine_kernel(
    slots,
    got_ref,
    dual_ref,
    gram_hbm,
    out_ref,
    sum_ref,
    gram_ref,
    gram_sem,
    pick_a,
    pick_b,
    term_a,
    term_b,
):
    gram_copy = pltpu.make_async_copy(gram_hbm, gram_ref, gram_sem)
    gram_copy.start()
    add_slots(slots, True, got_ref, None, sum_ref, (pick_a, pick_b), (term_a, term_b))
    gram_copy.wait()
    leaves, leaf = gram_ref.shape[:2]
    for l in range(leaves):
        at = slice(l * leaf, (l + 1) * leaf)
        dual = dual_ref[at, :] + sum_ref[at, :]
        out_ref[at, :] = dual + dot(gram_ref[l], dual.astype(LOW), 0, 0)


def refine(got, dual, gram, slots):
    rows_dev, width = dual.shape
    devices = got.shape[0]
    direct = pl.BlockSpec(memory_space=pltpu.VMEM)
    return pl.pallas_call(
        functools.partial(refine_kernel, slots),
        in_specs=[direct, direct, pl.BlockSpec(memory_space=pltpu.HBM)],
        out_specs=direct,
        out_shape=in_vmem(dual.shape, F32),
        scratch_shapes=[
            pltpu.VMEM((rows_dev, width), F32),
            pltpu.VMEM(gram.shape, LOW),
            pltpu.SemaphoreType.DMA,
        ]
        + slot_scratch(rows_dev, width),
        compiler_params=params(),
        cost_estimate=cost(2 * devices * slots * rows_dev * width, 4 << 20),
        name="refine",
    )(got, dual, gram)


def parent_kernel(coeff_ref, out_ref):
    rank, width = out_ref.shape
    branches, rows = coeff_ref.shape[:2]
    parts = width // rank
    leaves = rows * parts // (rank * (parts + 1))
    held = leaves * rank // parts
    sums = [jnp.zeros((held, width), F32) for _ in range(rank // held)]
    for b in range(branches):
        packed = coeff_ref[b, leaves * rank :, :]
        for q in range(parts):
            leaf, at = divmod(q * held, rank)
            term = dot(
                packed[:, q * rank : (q + 1) * rank], coeff_ref[b, leaf * rank : (leaf + 1) * rank, :]
            )
            sums[at // held] = sums[at // held] + term
    for i, total in enumerate(sums):
        out_ref[i * held : (i + 1) * held, :] = total.astype(LOW)


def parent_of(coeff, rank):
    width = coeff.shape[2]
    return pl.pallas_call(
        parent_kernel,
        out_shape=in_vmem((rank, width), LOW),
        compiler_params=params(mib=6),
        cost_estimate=cost(2 * coeff.size * rank, 1 << 20),
        name="parent_of",
    )(coeff)


def far_kernel(list_ref, coeff_ref, block_ref, out_ref):
    leaves, items, rank = block_ref.shape[:3]
    for l in range(leaves):
        total = jnp.zeros(out_ref.shape[1:], F32)
        for k in range(items):
            source = list_ref[l, k]
            at = pl.ds(pl.multiple_of(source % leaves * rank, rank), rank)
            total = total + dot(block_ref[l, k], coeff_ref[source // leaves, at, :])
        out_ref[l] = total


def far_field(far_list, coeff, far_block):
    leaves, items, rank = far_block.shape[:3]
    width = coeff.shape[2]
    return pl.pallas_call(
        far_kernel,
        grid_spec=pltpu.PrefetchScalarGridSpec(
            num_scalar_prefetch=1,
            grid=(1,),
            in_specs=[whole(coeff.shape), whole(far_block.shape)],
            out_specs=whole((leaves, rank, width)),
        ),
        out_shape=jax.ShapeDtypeStruct((leaves, rank, width), F32),
        compiler_params=params(("arbitrary",), 6),
        cost_estimate=cost(2 * far_block.size * width, 1 << 20),
        name="far_field",
    )(far_list, coeff, far_block)


def near_kernel(list_ref, block_ref, first_ref, out_ref, low_ref):
    leaf, item = pl.program_id(0), pl.program_id(1)
    size = out_ref.shape[0]

    @pl.when((leaf == 0) & (item == 0))
    def _():
        for l in range(low_ref.shape[0]):
            low_ref[l] = first_ref[l * size : (l + 1) * size, :].astype(LOW)

    count = block_ref.shape[1]
    term = dot(block_ref[0, 0], low_ref[list_ref[leaf, item * count]])
    for k in range(1, count):
        term = term + dot(block_ref[0, k], low_ref[list_ref[leaf, item * count + k]])

    @pl.when(item == 0)
    def _():
        out_ref[...] = first_ref[pl.ds(pl.multiple_of(leaf * size, size), size), :] + term

    @pl.when(item > 0)
    def _():
        out_ref[...] += term


def near_field(near_list, near_block, first):
    leaves, items, leaf = near_block.shape[:3]
    width = first.shape[1]
    count = 4 if items % 4 == 0 else 1
    return pl.pallas_call(
        near_kernel,
        grid_spec=pltpu.PrefetchScalarGridSpec(
            num_scalar_prefetch=1,
            grid=(leaves, items // count),
            in_specs=[
                pl.BlockSpec((1, count, leaf, leaf), lambda l, k, _: (l, k, 0, 0)),
                whole(first.shape),
            ],
            out_specs=pl.BlockSpec((leaf, width), lambda l, k, _: (l, 0)),
            scratch_shapes=[pltpu.VMEM((leaves, leaf, width), LOW)],
        ),
        out_shape=in_vmem(first.shape, F32),
        compiler_params=params(("arbitrary", "arbitrary"), 12),
        cost_estimate=cost(2 * near_block.size * width, 2 * near_block.size),
        name="near_field",
    )(near_list, near_block, first)


def prepare_kernel(image_ref, base_ref, gram_ref, dual_ref, lift_ref):
    leaves, leaf = gram_ref.shape[:2]
    ids = lax.broadcasted_iota(jnp.int32, (leaf, leaf), 0)
    same = ids == lax.broadcasted_iota(jnp.int32, (leaf, leaf), 1)
    unit = jnp.where(same, 1.0, 0.0).astype(LOW)
    for l in range(leaves):
        at = slice(l * leaf, (l + 1) * leaf)
        image = image_ref[at, :]
        dual_ref[at, :] = image + dot(gram_ref[l], image.astype(LOW))
        lifted = dot(unit, base_ref[l], 1, 1) + dot(gram_ref[l], base_ref[l], 1, 1)
        parts = [lifted if i == l else jnp.zeros_like(lifted) for i in range(leaves)]
        lift_ref[at, :] = jnp.concatenate(parts, axis=1).astype(LOW)


def prepare(image, base, gram):
    rows_dev, width = image.shape
    lanes = base.shape[0] * base.shape[1]
    return pl.pallas_call(
        prepare_kernel,
        out_shape=(in_vmem((rows_dev, width), F32), in_vmem((rows_dev, lanes), LOW)),
        compiler_params=params(mib=12),
        cost_estimate=cost(2 * gram.size * (width + 2 * lanes), 4 << 20),
        name="prepare",
    )(image, base, gram)


def reply_kernel(slots, *refs):
    dual_ref, lift_ref, far_ref, top_ref, descend_ref, rows_ref = refs[:6]
    parents, rest = refs[6:-7], refs[-7:]
    out_hbm, field_ref, low_ref, pick_a, pick_b, ready_ref, sems = rest
    picks = (pick_a, pick_b)
    owners = REPLY_BLOCK // slots
    blocks = ready_ref.shape[0] // REPLY_BLOCK
    ids = lax.broadcasted_iota(jnp.int32, (slots, low_ref.shape[0]), 1).astype(F32)

    def build(block):
        for j in range(owners):
            source = block * owners + j
            row = column(rows_ref[source : source + 1, :][:, :slots])
            pick = jnp.where(ids == row, 1.0, 0.0).astype(LOW)
            picks[block % 2][j * slots : (j + 1) * slots, :] = pick

    build(0)
    leaves, rank = far_ref.shape[:2]
    field = dot(top_ref[0], parents[0][...])
    for k in range(1, len(parents)):
        field = field + dot(top_ref[k], parents[k][...])
    field = field.astype(LOW)
    for l in range(leaves):
        descent = far_ref[l] + dot(descend_ref[l], field)
        field_ref[l * rank : (l + 1) * rank, :] = descent.astype(LOW)
    low_ref[...] = (dual_ref[...] + dot(lift_ref[...], field_ref[...])).astype(LOW)
    copies = []
    for block in range(blocks):
        if block + 1 < blocks:
            build(block + 1)
        at = pl.ds(block * REPLY_BLOCK, REPLY_BLOCK)
        ready_ref[at, :] = dot(picks[block % 2][...], low_ref[...]).astype(LOW)
        copies.append(pltpu.make_async_copy(ready_ref.at[at], out_hbm.at[at], sems.at[block]))
        copies[-1].start()
    for copy in copies:
        copy.wait()


def reply(dual, lift, far, top, parents, descend, rows, slots):
    rows_dev, width = dual.shape
    total = rows.shape[0] * slots
    args = (dual, lift, far, top, descend, rows, *parents)
    direct = pl.BlockSpec(memory_space=pltpu.VMEM)
    return pl.pallas_call(
        functools.partial(reply_kernel, slots),
        in_specs=[direct] * len(args),
        out_specs=pl.BlockSpec(memory_space=pltpu.HBM),
        out_shape=in_hbm((total, width), LOW),
        scratch_shapes=[
            pltpu.VMEM((lift.shape[1], width), LOW),
            pltpu.VMEM((rows_dev, width), LOW),
            pltpu.VMEM((REPLY_BLOCK, rows_dev), LOW),
            pltpu.VMEM((REPLY_BLOCK, rows_dev), LOW),
            pltpu.VMEM((total, width), LOW),
            pltpu.SemaphoreType.DMA((total // REPLY_BLOCK,)),
        ],
        compiler_params=params(mib=16),
        cost_estimate=cost(2 * total * rows_dev * width, 4 << 20),
        name="reply",
    )(*args)


def gather_kernel(spread, ret_ref, place_ref, basis_ref, mutual_ref, image_ref, sums_ref, pick_a, pick_b):
    picks = (pick_a, pick_b)
    total, width = ret_ref.shape
    krylov = basis_ref.shape[0]
    blocks = image_ref.shape[0] // GATHER_BLOCK
    ids = lax.broadcasted_iota(jnp.int32, (GATHER_BLOCK, total), 1).astype(F32)

    def build(block):
        at = slice(block * GATHER_BLOCK, (block + 1) * GATHER_BLOCK)
        for s in range(spread):
            pick = jnp.where(ids == place_ref[at, s : s + 1], 1.0, 0.0).astype(LOW)
            picks[block % 2][s * GATHER_BLOCK : (s + 1) * GATHER_BLOCK, :] = pick

    build(0)
    sums = [jnp.zeros((1, width), F32) for _ in range(krylov + 1)]
    for block in range(blocks):
        if block + 1 < blocks:
            build(block + 1)
        at = slice(block * GATHER_BLOCK, (block + 1) * GATHER_BLOCK)
        picked = dot(picks[block % 2][...], ret_ref[...])
        image = jnp.zeros((GATHER_BLOCK, width), F32)
        for s in range(spread):
            weight = place_ref[at, spread + s : spread + s + 1]
            image = image + weight * picked[s * GATHER_BLOCK : (s + 1) * GATHER_BLOCK, :]
        image_ref[at, :] = image
        for k in range(krylov):
            sums[k] = sums[k] + jnp.sum(basis_ref[k, at, :] * image, axis=0, keepdims=True)
        sums[krylov] = sums[krylov] + jnp.sum(image * image, axis=0, keepdims=True)
    sums_ref[: krylov + 1, :] = jnp.concatenate(sums, axis=0)
    sums_ref[krylov + 1 :, :] = mutual_ref[...]


def gather_back(ret, place_col, basis, mutual, spread):
    total, width = ret.shape
    krylov, rows_dev = basis.shape[:2]
    lines = krylov + 1 + mutual.shape[0]
    direct = pl.BlockSpec(memory_space=pltpu.VMEM)
    return pl.pallas_call(
        functools.partial(gather_kernel, spread),
        in_specs=[direct] * 4,
        out_specs=[direct] * 2,
        out_shape=(
            jax.ShapeDtypeStruct((rows_dev, width), F32),
            jax.ShapeDtypeStruct((lines, width), F32),
        ),
        scratch_shapes=[
            pltpu.VMEM((spread * GATHER_BLOCK, total), LOW),
            pltpu.VMEM((spread * GATHER_BLOCK, total), LOW),
        ],
        compiler_params=params(),
        cost_estimate=cost(2 * spread * total * rows_dev * width, 6 << 20),
        name="gather_back",
    )(ret, place_col, basis, mutual)


AXES = ("branch", "group")


def exchange(values, axes=AXES):
    return lax.all_to_all(values, axes, split_axis=0, concat_axis=0, tiled=True)


def swaps(values, axis):
    size = lax.axis_size(axis)
    return [values] + [
        lax.ppermute(values, axis, [(i, i ^ k) for i in range(size)]) for k in range(1, size)
    ]


def to_all(values, axes, size):
    return exchange(jnp.broadcast_to(values[None], (size,) + values.shape), axes)


def body(
    basis,
    spread_owner,
    spread_row,
    spread_weight,
    gram_term,
    near_block,
    near_list,
    leaf_basis,
    far_block,
    far_list,
    ascend,
    descend,
    top_block,
):
    branches = lax.axis_size("branch")
    groups = lax.axis_size("group")
    devices = branches * groups
    rows_dev, columns = basis.shape[1:]
    krylov = basis.shape[0]
    spread = spread_owner.shape[1]
    slots = 2 * spread * rows_dev // devices
    total = devices * slots
    leaves, rank = leaf_basis.shape[:2]
    sent, place = spread_out(
        kept(spread_owner.T), kept(spread_row.T), kept(spread_weight.T), kept(basis), devices, slots
    )
    sent, late_ascend, late_top, late_base, late_gram = lax.optimization_barrier(
        (sent, ascend, top_block, leaf_basis, gram_term)
    )
    got = exchange(sent)

    parts = columns // rank
    held = leaves * rank // parts
    packed = late_ascend.reshape(parts, held, rank).transpose(1, 0, 2).reshape(held, columns)
    columns_of = (jnp.arange(groups) ^ lax.axis_index("group")) % groups
    top = late_top.reshape(rank, groups, rank).transpose(1, 0, 2)[columns_of]

    raised = rise(late_base, late_gram)
    got, packed, top, raised = lax.optimization_barrier((got, packed, top, raised))
    dual, coeff, rows = collect(got, raised, packed, slots, branches, columns)
    coeff = kept(exchange(coeff, "branch"))
    first = refine(got, dual, kept(gram_term), slots)
    image = near_field(near_list, kept(near_block), first)
    dual, lift = prepare(image, kept(leaf_basis), kept(gram_term))
    coeff, dual, lift = lax.optimization_barrier((coeff, dual, lift))
    parents = swaps(parent_of(coeff, rank), "group")
    far = far_field(far_list, coeff, kept(far_block))
    replies = reply(dual, lift, far, kept(top), parents, kept(descend), kept(rows), slots)
    returned = exchange(replies.reshape(devices, slots, columns)).reshape(total, columns)
    pairs = [(i, j) for i in range(krylov) for j in range(i, krylov)]
    mutual = jnp.stack([jnp.sum(basis[i] * basis[j], axis=0) for i, j in pairs])
    mutual = sum(swaps(mutual, "group"))
    share = -(-len(pairs) // groups)
    mutual = jnp.pad(mutual, ((0, share * groups - len(pairs)), (0, 0)))
    own = lax.dynamic_slice_in_dim(mutual, share * lax.axis_index("group"), share, 0)
    primal, sums = gather_back(near_by(returned), kept(place.T), basis, own, spread)
    everyone = to_all(sums, AXES, devices)
    sums = jnp.sum(everyone[:, : krylov + 1], axis=0)
    mutual = jnp.sum(everyone.reshape(branches, groups, -1, columns)[:, :, krylov + 1 :], axis=0)
    mutual = mutual.reshape(share * groups, columns)

    total_rows = rows_dev * devices
    projection = sums[:krylov] / total_rows
    remainder = primal - jnp.sum(projection[:, None, :] * basis, axis=0)
    square = sums[krylov] / total_rows - 2.0 * jnp.sum(projection * projection, axis=0)
    for at, (i, j) in enumerate(pairs):
        times = 1.0 if i == j else 2.0
        square = square + times * projection[i] * projection[j] * mutual[at] / total_rows
    norm_scale = jnp.sqrt(jnp.maximum(square, 0.0) + 1e-06)
    return (remainder / norm_scale, jnp.concatenate([projection, norm_scale[None]], axis=0))


def solution(mesh):
    both = ("branch", "group")
    return jax.shard_map(
        body,
        mesh=mesh,
        in_specs=(
            P(None, both, None),
            P(both, None),
            P(both, None),
            P(both, None),
            P(both, None, None),
            P(both, None, None, None),
            P(both, None),
            P(both, None, None),
            P(both, None, None, None),
            P(both, None),
            P(both, None, None),
            P(both, None, None),
            P("group", None),
        ),
        out_specs=(P(both, None), P()),
        check_vma=False,
    )
```

```python
import functools

import jax
import jax.numpy as jnp
from jax import lax
from jax.experimental import pallas as pl
from jax.experimental.pallas import tpu as pltpu
from jax.sharding import PartitionSpec as P

F32 = jnp.float32
LOW = jnp.bfloat16
CODE = jnp.int16
TOP = 32767.0
REST = 65534.0
LOG2 = 0.6931471805599453
SPREAD_BLOCK = 1024
COLLECT_BLOCK = 512
REPLY_BLOCK = 512
GATHER_BLOCK = 256
LANES = 128


def rounded(values):
    return values.astype(LOW)


def contract(pattern, first_op, second_op):
    return jnp.einsum(pattern, first_op, second_op, preferred_element_type=F32)


def dot(lhs, rhs, lhs_dim=1, rhs_dim=0):
    return lax.dot_general(
        lhs, rhs, (((lhs_dim,), (rhs_dim,)), ((), ())), preferred_element_type=F32
    )


def params(semantics=None, mib=24):
    return pltpu.CompilerParams(dimension_semantics=semantics, vmem_limit_bytes=mib << 20)


def whole(shape):
    zeros = (0,) * len(shape)
    return pl.BlockSpec(shape, lambda *_: zeros)


def in_hbm(shape, dtype):
    return pltpu.HBM(shape, dtype)


def in_vmem(shape, dtype):
    return pltpu.VMEM(shape, dtype)


def near_by(values):
    return pltpu.with_memory_space_constraint(values, pltpu.VMEM)


def kept(values):
    return pltpu.with_memory_space_constraint(values, pltpu.HBM)


def cost(flops, nbytes):
    return pl.CostEstimate(flops=int(flops), bytes_accessed=int(nbytes), transcendentals=0)


def column(row):
    size = row.shape[1]
    same = lax.broadcasted_iota(jnp.int32, (size, size), 0) == lax.broadcasted_iota(
        jnp.int32, (size, size), 1
    )
    return jnp.sum(jnp.where(same, row, 0.0), axis=1, keepdims=True)


def split(code):
    high = jnp.round(code * (1.0 / 256.0))
    return high, code - 256.0 * high


def find_routes(slots, owner_ref, row_ref, weight_ref, rank_ref, side_ref, place_ref):
    devices, rows_dev = rank_ref.shape
    spread = owner_ref.shape[0]
    width = side_ref.shape[2]
    ids = lax.broadcasted_iota(jnp.int32, (devices, rows_dev), 0)
    named = [owner_ref[s : s + 1, :] == ids for s in range(spread)]
    chosen = functools.reduce(jnp.logical_or, named)
    flag = jnp.where(chosen, 1.0, 0.0)
    lane = 128
    upper = jnp.where(
        lax.broadcasted_iota(jnp.int32, (lane, lane), 0)
        <= lax.broadcasted_iota(jnp.int32, (lane, lane), 1),
        1.0,
        0.0,
    ).astype(LOW)
    before = jnp.zeros((devices, 1), F32)
    pieces = []
    for start in range(0, rows_dev, lane):
        part = flag[:, start : start + lane]
        upto = dot(part.astype(LOW), upper)
        pieces.append(upto - part + before)
        before = before + upto[:, lane - 1 : lane]
    rank = jnp.concatenate(pieces, axis=1)
    rank_ref[...] = jnp.where(chosen, rank, -1.0)
    slot_ids = lax.broadcasted_iota(jnp.int32, (width, rows_dev), 0).astype(F32)
    place_ref[...] = jnp.zeros_like(place_ref)
    total = jnp.zeros((6 * devices, width), F32)
    for s in range(spread):
        slot = jnp.sum(jnp.where(named[s], rank, 0.0), axis=0, keepdims=True)
        place_ref[s : s + 1, :] = owner_ref[s : s + 1, :].astype(F32) * slots + slot
        weight = weight_ref[s : s + 1, :]
        place_ref[spread + s : spread + s + 1, :] = weight
        code = weight * TOP
        whole_code = jnp.round(code)
        rest_code = jnp.round((code - whole_code) * REST)
        fields = split(row_ref[s : s + 1, :].astype(F32)) + split(whole_code) + split(rest_code)
        lhs = jnp.concatenate([jnp.where(named[s], f, 0.0) for f in fields], axis=0).astype(LOW)
        total = total + dot(lhs, jnp.where(slot_ids == slot, 1.0, 0.0).astype(LOW), 1, 1)
    for i in range(3):
        high = total[2 * i * devices : (2 * i + 1) * devices]
        low = total[(2 * i + 1) * devices : (2 * i + 2) * devices]
        side_ref[i] = 256.0 * high + low


def spread_kernel(
    slots,
    owner_ref,
    row_ref,
    weight_ref,
    basis_hbm,
    out_ref,
    place_ref,
    vector_ref,
    rank_ref,
    side_ref,
    code_ref,
    level_ref,
    pick_ref,
    vector_sem,
):
    step = pl.program_id(0)
    columns = vector_ref.shape[1]

    @pl.when(step == 0)
    def _():
        copy = pltpu.make_async_copy(basis_hbm.at[basis_hbm.shape[0] - 1], vector_ref, vector_sem)
        copy.start()
        find_routes(slots, owner_ref, row_ref, weight_ref, rank_ref, side_ref, place_ref)
        copy.wait()
        vector = vector_ref[...]
        peak = jnp.maximum(jnp.max(jnp.abs(vector), axis=0, keepdims=True), 1e-30)
        level = jnp.floor(jnp.log(peak) * (1.0 / LOG2)) + 1.0
        level_ref[...] = level
        code = jnp.clip(jnp.round(vector * (TOP / jnp.exp(level * LOG2))), -TOP, TOP)
        high, low = split(code)
        code_ref[:, :columns] = high.astype(LOW)
        code_ref[:, columns:] = low.astype(LOW)

    rows_dev = rank_ref.shape[1]
    owners = SPREAD_BLOCK // slots
    slot_ids = lax.broadcasted_iota(jnp.int32, (slots, rows_dev), 0).astype(F32)
    for j in range(owners):
        rank = rank_ref[pl.ds(step * owners + j, 1), :]
        pick_ref[j * slots : (j + 1) * slots, :] = jnp.where(slot_ids == rank, 1.0, 0.0).astype(LOW)
    picked = dot(pick_ref[...], code_ref[...])
    codes = (256.0 * picked[:, :columns] + picked[:, columns:]).astype(jnp.int32).astype(CODE)
    line = lax.broadcasted_iota(jnp.int32, (8, LANES), 0)
    parts = columns // LANES
    for j in range(owners):
        extra = jnp.zeros((8, LANES), F32)
        for k in range(3):
            extra = jnp.where(line == k, side_ref[k, pl.ds(step * owners + j, 1), :], extra)
        for h in range(parts):
            at = slice(h * LANES, (h + 1) * LANES)
            extra = jnp.where(line == 3 + h, level_ref[:, at], extra)
            out_ref[j, h * slots : (h + 1) * slots, :] = codes[j * slots : (j + 1) * slots, at]
        out_ref[j, parts * slots :, :] = extra.astype(jnp.int32).astype(CODE)


def spread_out(owner_t, row_t, weight_t, basis, devices, slots):
    rows_dev, columns = basis.shape[1:]
    owners = SPREAD_BLOCK // slots
    shape = (devices, columns // LANES * slots + 8, LANES)
    return pl.pallas_call(
        functools.partial(spread_kernel, slots),
        grid=(devices // owners,),
        in_specs=[
            whole(owner_t.shape),
            whole(row_t.shape),
            whole(weight_t.shape),
            pl.BlockSpec(memory_space=pltpu.HBM),
        ],
        out_specs=(
            pl.BlockSpec((owners,) + shape[1:], lambda i: (i, 0, 0)),
            whole((8, rows_dev)),
        ),
        out_shape=(in_hbm(shape, CODE), in_hbm((8, rows_dev), F32)),
        scratch_shapes=[
            pltpu.VMEM((rows_dev, columns), F32),
            pltpu.VMEM((devices, rows_dev), F32),
            pltpu.VMEM((3, devices, LANES), F32),
            pltpu.VMEM((rows_dev, 2 * columns), LOW),
            pltpu.VMEM((1, columns), F32),
            pltpu.VMEM((SPREAD_BLOCK, rows_dev), LOW),
            pltpu.SemaphoreType.DMA,
        ],
        compiler_params=params(("arbitrary",)),
        cost_estimate=cost(4 * devices * slots * rows_dev * columns, 4 << 20),
        name="spread_out",
    )(owner_t, row_t, weight_t, basis)


def add_slots(slots, low_part, got_ref, rows_ref, sum_ref, picks, terms):
    rows_dev, width = sum_ref.shape
    owners = COLLECT_BLOCK // slots
    parts = width // LANES
    blocks = got_ref.shape[0] // owners
    tile = 16
    ids = lax.broadcasted_iota(jnp.int32, (rows_dev, slots), 0).astype(CODE)
    one, zero = jnp.ones((rows_dev, slots), LOW), jnp.zeros((rows_dev, slots), LOW)

    def build(block):
        pick_ref, term_ref = picks[block % 2], terms[block % 2]
        for j in range(owners):
            at = slice(j * slots, (j + 1) * slots)
            source = block * owners + j
            extra = got_ref[source, parts * slots :, :].astype(jnp.int32)
            row = jnp.broadcast_to(extra[0:1, :slots], (tile, slots)).astype(CODE)
            row = jnp.broadcast_to(row[None], (rows_dev // tile, tile, slots))
            pick_ref[:, at] = jnp.where(ids == row.reshape(rows_dev, slots), one, zero)
            extra = extra.astype(F32)
            weight = (extra[1:2, :slots] + extra[2:3, :slots] * (1.0 / REST)) * (1.0 / TOP)
            weight = column(weight)
            if rows_ref is not None:
                rows_ref[source : source + 1, :] = extra[0:1, :]
            for h in range(parts):
                scale = jnp.exp(extra[3 + h : 4 + h, :] * LOG2) * (1.0 / TOP)
                codes = got_ref[source, h * slots : (h + 1) * slots, :].astype(jnp.int32).astype(F32)
                values = codes * weight * scale
                term = values.astype(LOW)
                if low_part:
                    term = (values - term.astype(F32)).astype(LOW)
                term_ref[at, h * LANES : (h + 1) * LANES] = term

    build(0)
    for block in range(blocks):
        if block + 1 < blocks:
            build(block + 1)
        added = dot(picks[block % 2][...], terms[block % 2][...])
        sum_ref[...] = added if block == 0 else sum_ref[...] + added


def rise_kernel(base_ref, gram_ref, out_ref):
    for l in range(base_ref.shape[0]):
        base = base_ref[l]
        out_ref[l] = (base.astype(F32) + dot(base, gram_ref[l], 1, 1)).astype(LOW)


def rise(base, gram):
    return pl.pallas_call(
        rise_kernel,
        out_shape=in_vmem(base.shape, LOW),
        compiler_params=params(mib=8),
        cost_estimate=cost(2 * gram.size * base.shape[1], 2 * gram.size),
        name="rise",
    )(base, gram)


def collect_kernel(
    slots,
    got_ref,
    rise_ref,
    ascend_ref,
    dual_ref,
    coeff_ref,
    rows_ref,
    pick_a,
    pick_b,
    term_a,
    term_b,
):
    add_slots(slots, False, got_ref, rows_ref, dual_ref, (pick_a, pick_b), (term_a, term_b))
    leaves, rank, leaf = rise_ref.shape
    for b in range(coeff_ref.shape[0]):
        coeff_ref[b, leaves * rank :, :] = ascend_ref[...]
    for l in range(leaves):
        dual = dual_ref[l * leaf : (l + 1) * leaf, :]
        coeff = dot(rise_ref[l], dual.astype(LOW)).astype(LOW)
        for b in range(coeff_ref.shape[0]):
            coeff_ref[b, l * rank : (l + 1) * rank, :] = coeff


def slot_scratch(rows_dev, width):
    return [
        pltpu.VMEM((rows_dev, COLLECT_BLOCK), LOW),
        pltpu.VMEM((rows_dev, COLLECT_BLOCK), LOW),
        pltpu.VMEM((COLLECT_BLOCK, width), LOW),
        pltpu.VMEM((COLLECT_BLOCK, width), LOW),
    ]


def collect(got, lift, ascend, slots, branches, width):
    devices = got.shape[0]
    leaves, rank, leaf = lift.shape
    rows_dev = leaves * leaf
    sent_rows = leaves * rank + ascend.shape[0]
    direct = pl.BlockSpec(memory_space=pltpu.VMEM)
    return pl.pallas_call(
        functools.partial(collect_kernel, slots),
        in_specs=[direct] * 3,
        out_specs=[direct] * 3,
        out_shape=(
            in_vmem((rows_dev, width), F32),
            in_hbm((branches, sent_rows, width), LOW),
            in_hbm((devices, LANES), F32),
        ),
        scratch_shapes=slot_scratch(rows_dev, width),
        compiler_params=params(),
        cost_estimate=cost(2 * devices * slots * rows_dev * width, 4 << 20),
        name="collect",
    )(got, lift, ascend)


def refine_kernel(
    slots,
    got_ref,
    dual_ref,
    gram_hbm,
    out_ref,
    sum_ref,
    gram_ref,
    gram_sem,
    pick_a,
    pick_b,
    term_a,
    term_b,
):
    gram_copy = pltpu.make_async_copy(gram_hbm, gram_ref, gram_sem)
    gram_copy.start()
    add_slots(slots, True, got_ref, None, sum_ref, (pick_a, pick_b), (term_a, term_b))
    gram_copy.wait()
    leaves, leaf = gram_ref.shape[:2]
    for l in range(leaves):
        at = slice(l * leaf, (l + 1) * leaf)
        dual = dual_ref[at, :] + sum_ref[at, :]
        out_ref[at, :] = dual + dot(gram_ref[l], dual.astype(LOW), 0, 0)


def refine(got, dual, gram, slots):
    rows_dev, width = dual.shape
    devices = got.shape[0]
    direct = pl.BlockSpec(memory_space=pltpu.VMEM)
    return pl.pallas_call(
        functools.partial(refine_kernel, slots),
        in_specs=[direct, direct, pl.BlockSpec(memory_space=pltpu.HBM)],
        out_specs=direct,
        out_shape=in_vmem(dual.shape, F32),
        scratch_shapes=[
            pltpu.VMEM((rows_dev, width), F32),
            pltpu.VMEM(gram.shape, LOW),
            pltpu.SemaphoreType.DMA,
        ]
        + slot_scratch(rows_dev, width),
        compiler_params=params(),
        cost_estimate=cost(2 * devices * slots * rows_dev * width, 4 << 20),
        name="refine",
    )(got, dual, gram)


def parent_kernel(coeff_ref, out_ref):
    rank, width = out_ref.shape
    branches, rows = coeff_ref.shape[:2]
    parts = width // rank
    leaves = rows * parts // (rank * (parts + 1))
    held = leaves * rank // parts
    sums = [jnp.zeros((held, width), F32) for _ in range(rank // held)]
    for b in range(branches):
        packed = coeff_ref[b, leaves * rank :, :]
        for q in range(parts):
            leaf, at = divmod(q * held, rank)
            term = dot(
                packed[:, q * rank : (q + 1) * rank], coeff_ref[b, leaf * rank : (leaf + 1) * rank, :]
            )
            sums[at // held] = sums[at // held] + term
    for i, total in enumerate(sums):
        out_ref[i * held : (i + 1) * held, :] = total.astype(LOW)


def parent_of(coeff, rank):
    width = coeff.shape[2]
    return pl.pallas_call(
        parent_kernel,
        out_shape=in_vmem((rank, width), LOW),
        compiler_params=params(mib=6),
        cost_estimate=cost(2 * coeff.size * rank, 1 << 20),
        name="parent_of",
    )(coeff)


def far_kernel(list_ref, coeff_ref, block_ref, out_ref):
    leaves, items, rank = block_ref.shape[:3]
    for l in range(leaves):
        total = jnp.zeros(out_ref.shape[1:], F32)
        for k in range(items):
            source = list_ref[l, k]
            at = pl.ds(pl.multiple_of(source % leaves * rank, rank), rank)
            total = total + dot(block_ref[l, k], coeff_ref[source // leaves, at, :])
        out_ref[l] = total


def far_field(far_list, coeff, far_block):
    leaves, items, rank = far_block.shape[:3]
    width = coeff.shape[2]
    return pl.pallas_call(
        far_kernel,
        grid_spec=pltpu.PrefetchScalarGridSpec(
            num_scalar_prefetch=1,
            grid=(1,),
            in_specs=[whole(coeff.shape), whole(far_block.shape)],
            out_specs=whole((leaves, rank, width)),
        ),
        out_shape=jax.ShapeDtypeStruct((leaves, rank, width), F32),
        compiler_params=params(("arbitrary",), 6),
        cost_estimate=cost(2 * far_block.size * width, 1 << 20),
        name="far_field",
    )(far_list, coeff, far_block)


def near_kernel(list_ref, block_ref, first_ref, out_ref, low_ref):
    leaf, item = pl.program_id(0), pl.program_id(1)
    size = out_ref.shape[0]

    @pl.when((leaf == 0) & (item == 0))
    def _():
        for l in range(low_ref.shape[0]):
            low_ref[l] = first_ref[l * size : (l + 1) * size, :].astype(LOW)

    count = block_ref.shape[1]
    term = dot(block_ref[0, 0], low_ref[list_ref[leaf, item * count]])
    for k in range(1, count):
        term = term + dot(block_ref[0, k], low_ref[list_ref[leaf, item * count + k]])

    @pl.when(item == 0)
    def _():
        out_ref[...] = first_ref[pl.ds(pl.multiple_of(leaf * size, size), size), :] + term

    @pl.when(item > 0)
    def _():
        out_ref[...] += term


def near_field(near_list, near_block, first):
    leaves, items, leaf = near_block.shape[:3]
    width = first.shape[1]
    count = 4 if items % 4 == 0 else 1
    return pl.pallas_call(
        near_kernel,
        grid_spec=pltpu.PrefetchScalarGridSpec(
            num_scalar_prefetch=1,
            grid=(leaves, items // count),
            in_specs=[
                pl.BlockSpec((1, count, leaf, leaf), lambda l, k, _: (l, k, 0, 0)),
                whole(first.shape),
            ],
            out_specs=pl.BlockSpec((leaf, width), lambda l, k, _: (l, 0)),
            scratch_shapes=[pltpu.VMEM((leaves, leaf, width), LOW)],
        ),
        out_shape=in_vmem(first.shape, F32),
        compiler_params=params(("arbitrary", "arbitrary"), 12),
        cost_estimate=cost(2 * near_block.size * width, 2 * near_block.size),
        name="near_field",
    )(near_list, near_block, first)


def prepare_kernel(image_ref, base_ref, gram_ref, dual_ref, lift_ref):
    leaves, leaf = gram_ref.shape[:2]
    ids = lax.broadcasted_iota(jnp.int32, (leaf, leaf), 0)
    same = ids == lax.broadcasted_iota(jnp.int32, (leaf, leaf), 1)
    unit = jnp.where(same, 1.0, 0.0).astype(LOW)
    for l in range(leaves):
        at = slice(l * leaf, (l + 1) * leaf)
        image = image_ref[at, :]
        dual_ref[at, :] = image + dot(gram_ref[l], image.astype(LOW))
        lifted = dot(unit, base_ref[l], 1, 1) + dot(gram_ref[l], base_ref[l], 1, 1)
        parts = [lifted if i == l else jnp.zeros_like(lifted) for i in range(leaves)]
        lift_ref[at, :] = jnp.concatenate(parts, axis=1).astype(LOW)


def prepare(image, base, gram):
    rows_dev, width = image.shape
    lanes = base.shape[0] * base.shape[1]
    return pl.pallas_call(
        prepare_kernel,
        out_shape=(in_vmem((rows_dev, width), F32), in_vmem((rows_dev, lanes), LOW)),
        compiler_params=params(mib=12),
        cost_estimate=cost(2 * gram.size * (width + 2 * lanes), 4 << 20),
        name="prepare",
    )(image, base, gram)


def reply_kernel(slots, *refs):
    dual_ref, lift_ref, far_ref, top_ref, descend_ref, rows_ref = refs[:6]
    parents, rest = refs[6:-7], refs[-7:]
    out_hbm, field_ref, low_ref, pick_a, pick_b, ready_ref, sems = rest
    picks = (pick_a, pick_b)
    owners = REPLY_BLOCK // slots
    blocks = ready_ref.shape[0] // REPLY_BLOCK
    ids = lax.broadcasted_iota(jnp.int32, (slots, low_ref.shape[0]), 1).astype(F32)

    def build(block):
        for j in range(owners):
            source = block * owners + j
            row = column(rows_ref[source : source + 1, :][:, :slots])
            pick = jnp.where(ids == row, 1.0, 0.0).astype(LOW)
            picks[block % 2][j * slots : (j + 1) * slots, :] = pick

    build(0)
    leaves, rank = far_ref.shape[:2]
    field = dot(top_ref[0], parents[0][...])
    for k in range(1, len(parents)):
        field = field + dot(top_ref[k], parents[k][...])
    field = field.astype(LOW)
    for l in range(leaves):
        descent = far_ref[l] + dot(descend_ref[l], field)
        field_ref[l * rank : (l + 1) * rank, :] = descent.astype(LOW)
    low_ref[...] = (dual_ref[...] + dot(lift_ref[...], field_ref[...])).astype(LOW)
    copies = []
    for block in range(blocks):
        if block + 1 < blocks:
            build(block + 1)
        at = pl.ds(block * REPLY_BLOCK, REPLY_BLOCK)
        ready_ref[at, :] = dot(picks[block % 2][...], low_ref[...]).astype(LOW)
        copies.append(pltpu.make_async_copy(ready_ref.at[at], out_hbm.at[at], sems.at[block]))
        copies[-1].start()
    for copy in copies:
        copy.wait()


def reply(dual, lift, far, top, parents, descend, rows, slots):
    rows_dev, width = dual.shape
    total = rows.shape[0] * slots
    args = (dual, lift, far, top, descend, rows, *parents)
    direct = pl.BlockSpec(memory_space=pltpu.VMEM)
    return pl.pallas_call(
        functools.partial(reply_kernel, slots),
        in_specs=[direct] * len(args),
        out_specs=pl.BlockSpec(memory_space=pltpu.HBM),
        out_shape=in_hbm((total, width), LOW),
        scratch_shapes=[
            pltpu.VMEM((lift.shape[1], width), LOW),
            pltpu.VMEM((rows_dev, width), LOW),
            pltpu.VMEM((REPLY_BLOCK, rows_dev), LOW),
            pltpu.VMEM((REPLY_BLOCK, rows_dev), LOW),
            pltpu.VMEM((total, width), LOW),
            pltpu.SemaphoreType.DMA((total // REPLY_BLOCK,)),
        ],
        compiler_params=params(mib=16),
        cost_estimate=cost(2 * total * rows_dev * width, 4 << 20),
        name="reply",
    )(*args)


def gather_kernel(spread, ret_ref, place_ref, basis_ref, mutual_ref, image_ref, sums_ref, pick_a, pick_b):
    picks = (pick_a, pick_b)
    total, width = ret_ref.shape
    krylov = basis_ref.shape[0]
    blocks = image_ref.shape[0] // GATHER_BLOCK
    ids = lax.broadcasted_iota(jnp.int32, (GATHER_BLOCK, total), 1).astype(F32)

    def build(block):
        at = slice(block * GATHER_BLOCK, (block + 1) * GATHER_BLOCK)
        for s in range(spread):
            pick = jnp.where(ids == place_ref[at, s : s + 1], 1.0, 0.0).astype(LOW)
            picks[block % 2][s * GATHER_BLOCK : (s + 1) * GATHER_BLOCK, :] = pick

    build(0)
    sums = [jnp.zeros((1, width), F32) for _ in range(krylov + 1)]
    for block in range(blocks):
        if block + 1 < blocks:
            build(block + 1)
        at = slice(block * GATHER_BLOCK, (block + 1) * GATHER_BLOCK)
        picked = dot(picks[block % 2][...], ret_ref[...])
        image = jnp.zeros((GATHER_BLOCK, width), F32)
        for s in range(spread):
            weight = place_ref[at, spread + s : spread + s + 1]
            image = image + weight * picked[s * GATHER_BLOCK : (s + 1) * GATHER_BLOCK, :]
        image_ref[at, :] = image
        for k in range(krylov):
            sums[k] = sums[k] + jnp.sum(basis_ref[k, at, :] * image, axis=0, keepdims=True)
        sums[krylov] = sums[krylov] + jnp.sum(image * image, axis=0, keepdims=True)
    sums_ref[: krylov + 1, :] = jnp.concatenate(sums, axis=0)
    sums_ref[krylov + 1 :, :] = mutual_ref[...]


def gather_back(ret, place_col, basis, mutual, spread):
    total, width = ret.shape
    krylov, rows_dev = basis.shape[:2]
    lines = krylov + 1 + mutual.shape[0]
    direct = pl.BlockSpec(memory_space=pltpu.VMEM)
    return pl.pallas_call(
        functools.partial(gather_kernel, spread),
        in_specs=[direct] * 4,
        out_specs=[direct] * 2,
        out_shape=(
            jax.ShapeDtypeStruct((rows_dev, width), F32),
            jax.ShapeDtypeStruct((lines, width), F32),
        ),
        scratch_shapes=[
            pltpu.VMEM((spread * GATHER_BLOCK, total), LOW),
            pltpu.VMEM((spread * GATHER_BLOCK, total), LOW),
        ],
        compiler_params=params(),
        cost_estimate=cost(2 * spread * total * rows_dev * width, 6 << 20),
        name="gather_back",
    )(ret, place_col, basis, mutual)


def finish_kernel(groups, total_rows, sums_ref, image_ref, basis_ref, next_hbm, column_ref, ready_ref, sems):
    krylov, rows_dev, width = basis_ref.shape
    devices, lines = sums_ref.shape[:2]
    share = lines - krylov - 1
    whole_sum = jnp.sum(sums_ref[...], axis=0)
    projection = [whole_sum[k : k + 1, :] * (1.0 / total_rows) for k in range(krylov)]
    square = whole_sum[krylov : krylov + 1, :] * (1.0 / total_rows)
    for part in projection:
        square = square - 2.0 * part * part
    pairs = [(i, j) for i in range(krylov) for j in range(i, krylov)]
    for at, (i, j) in enumerate(pairs):
        line = krylov + 1 + at % share
        mutual = jnp.zeros((1, width), F32)
        for d in range(at // share, devices, groups):
            mutual = mutual + sums_ref[d, line : line + 1, :]
        times = (1.0 if i == j else 2.0) / total_rows
        square = square + times * projection[i] * projection[j] * mutual
    scale = jnp.sqrt(jnp.maximum(square, 0.0) + 1e-06)
    column_ref[...] = jnp.concatenate(projection + [scale], axis=0)
    inverse = 1.0 / scale
    size = rows_dev // sems.shape[0]
    copies = []
    for block in range(sems.shape[0]):
        at = pl.ds(block * size, size)
        remainder = image_ref[at, :]
        for k in range(krylov):
            remainder = remainder - projection[k] * basis_ref[k, at, :]
        ready_ref[at, :] = remainder * inverse
        copies.append(pltpu.make_async_copy(ready_ref.at[at], next_hbm.at[at], sems.at[block]))
        copies[-1].start()
    for copy in copies:
        copy.wait()


def finish(sums, image, basis, groups, total_rows):
    krylov, rows_dev, width = basis.shape
    direct = pl.BlockSpec(memory_space=pltpu.VMEM)
    return pl.pallas_call(
        functools.partial(finish_kernel, groups, total_rows),
        in_specs=[direct] * 3,
        out_specs=(pl.BlockSpec(memory_space=pltpu.HBM), direct),
        out_shape=(
            in_hbm((rows_dev, width), F32),
            jax.ShapeDtypeStruct((krylov + 1, width), F32),
        ),
        scratch_shapes=[pltpu.VMEM((rows_dev, width), F32), pltpu.SemaphoreType.DMA((4,))],
        compiler_params=params(mib=8),
        cost_estimate=cost(8 * rows_dev * width, 4 << 20),
        name="finish",
    )(sums, image, basis)


AXES = ("branch", "group")


def exchange(values, axes=AXES):
    return lax.all_to_all(values, axes, split_axis=0, concat_axis=0, tiled=True)


def swaps(values, axis):
    size = lax.axis_size(axis)
    return [values] + [
        lax.ppermute(values, axis, [(i, i ^ k) for i in range(size)]) for k in range(1, size)
    ]


def to_all(values, axes, size):
    return exchange(jnp.broadcast_to(values[None], (size,) + values.shape), axes)


def body(
    basis,
    spread_owner,
    spread_row,
    spread_weight,
    gram_term,
    near_block,
    near_list,
    leaf_basis,
    far_block,
    far_list,
    ascend,
    descend,
    top_block,
):
    branches = lax.axis_size("branch")
    groups = lax.axis_size("group")
    devices = branches * groups
    rows_dev, columns = basis.shape[1:]
    krylov = basis.shape[0]
    spread = spread_owner.shape[1]
    slots = 2 * spread * rows_dev // devices
    total = devices * slots
    leaves, rank = leaf_basis.shape[:2]
    sent, place = spread_out(
        kept(spread_owner.T), kept(spread_row.T), kept(spread_weight.T), kept(basis), devices, slots
    )
    sent, late_ascend, late_top, late_base, late_gram = lax.optimization_barrier(
        (sent, ascend, top_block, leaf_basis, gram_term)
    )
    got = exchange(sent)

    parts = columns // rank
    held = leaves * rank // parts
    packed = late_ascend.reshape(parts, held, rank).transpose(1, 0, 2).reshape(held, columns)
    columns_of = (jnp.arange(groups) ^ lax.axis_index("group")) % groups
    top = late_top.reshape(rank, groups, rank).transpose(1, 0, 2)[columns_of]

    raised = rise(late_base, late_gram)
    got, packed, top, raised = lax.optimization_barrier((got, packed, top, raised))
    dual, coeff, rows = collect(got, raised, packed, slots, branches, columns)
    coeff = kept(exchange(coeff, "branch"))
    first = refine(got, dual, kept(gram_term), slots)
    image = near_field(near_list, kept(near_block), first)
    dual, lift = prepare(image, kept(leaf_basis), kept(gram_term))
    coeff, dual, lift = lax.optimization_barrier((coeff, dual, lift))
    parents = swaps(parent_of(coeff, rank), "group")
    far = far_field(far_list, coeff, kept(far_block))
    replies = reply(dual, lift, far, kept(top), parents, kept(descend), kept(rows), slots)
    returned = exchange(replies.reshape(devices, slots, columns)).reshape(total, columns)
    pairs = [(i, j) for i in range(krylov) for j in range(i, krylov)]
    mutual = jnp.stack([jnp.sum(basis[i] * basis[j], axis=0) for i, j in pairs])
    mutual = sum(swaps(mutual, "group"))
    share = -(-len(pairs) // groups)
    mutual = jnp.pad(mutual, ((0, share * groups - len(pairs)), (0, 0)))
    own = lax.dynamic_slice_in_dim(mutual, share * lax.axis_index("group"), share, 0)
    primal, sums = gather_back(near_by(returned), kept(place.T), basis, own, spread)
    everyone = to_all(sums, AXES, devices)
    return finish(everyone, primal, basis, groups, rows_dev * devices)


def solution(mesh):
    both = ("branch", "group")
    return jax.shard_map(
        body,
        mesh=mesh,
        in_specs=(
            P(None, both, None),
            P(both, None),
            P(both, None),
            P(both, None),
            P(both, None, None),
            P(both, None, None, None),
            P(both, None),
            P(both, None, None),
            P(both, None, None, None),
            P(both, None),
            P(both, None, None),
            P(both, None, None),
            P("group", None),
        ),
        out_specs=(P(both, None), P()),
        check_vma=False,
    )
```

```python
import functools

import jax
import jax.numpy as jnp
from jax import lax
from jax.experimental import pallas as pl
from jax.experimental.pallas import tpu as pltpu
from jax.sharding import PartitionSpec as P

F32 = jnp.float32
LOW = jnp.bfloat16
CODE = jnp.int16
TOP = 32767.0
REST = 65534.0
LOG2 = 0.6931471805599453
SPREAD_BLOCK = 2048
COLLECT_BLOCK = 512
REPLY_BLOCK = 512
GATHER_BLOCK = 256
LANES = 128


def rounded(values):
    return values.astype(LOW)


def contract(pattern, first_op, second_op):
    return jnp.einsum(pattern, first_op, second_op, preferred_element_type=F32)


def dot(lhs, rhs, lhs_dim=1, rhs_dim=0):
    return lax.dot_general(
        lhs, rhs, (((lhs_dim,), (rhs_dim,)), ((), ())), preferred_element_type=F32
    )


def params(semantics=None, mib=24):
    return pltpu.CompilerParams(dimension_semantics=semantics, vmem_limit_bytes=mib << 20)


def whole(shape):
    zeros = (0,) * len(shape)
    return pl.BlockSpec(shape, lambda *_: zeros)


def in_hbm(shape, dtype):
    return pltpu.HBM(shape, dtype)


def in_vmem(shape, dtype):
    return pltpu.VMEM(shape, dtype)


def near_by(values):
    return pltpu.with_memory_space_constraint(values, pltpu.VMEM)


def kept(values):
    return pltpu.with_memory_space_constraint(values, pltpu.HBM)


def cost(flops, nbytes):
    return pl.CostEstimate(flops=int(flops), bytes_accessed=int(nbytes), transcendentals=0)


def column(row):
    size = row.shape[1]
    same = lax.broadcasted_iota(jnp.int32, (size, size), 0) == lax.broadcasted_iota(
        jnp.int32, (size, size), 1
    )
    return jnp.sum(jnp.where(same, row, 0.0), axis=1, keepdims=True)


def split(code):
    high = jnp.round(code * (1.0 / 256.0))
    return high, code - 256.0 * high


def find_routes(slots, owner_ref, row_ref, weight_ref, rank_ref, side_ref, place_ref):
    devices, rows_dev = rank_ref.shape
    spread = owner_ref.shape[0]
    width = side_ref.shape[2]
    ids = lax.broadcasted_iota(jnp.int32, (devices, rows_dev), 0)
    named = [owner_ref[s : s + 1, :] == ids for s in range(spread)]
    chosen = functools.reduce(jnp.logical_or, named)
    flag = jnp.where(chosen, 1.0, 0.0)
    lane = 128
    upper = jnp.where(
        lax.broadcasted_iota(jnp.int32, (lane, lane), 0)
        <= lax.broadcasted_iota(jnp.int32, (lane, lane), 1),
        1.0,
        0.0,
    ).astype(LOW)
    before = jnp.zeros((devices, 1), F32)
    pieces = []
    for start in range(0, rows_dev, lane):
        part = flag[:, start : start + lane]
        upto = dot(part.astype(LOW), upper)
        pieces.append(upto - part + before)
        before = before + upto[:, lane - 1 : lane]
    rank = jnp.concatenate(pieces, axis=1)
    rank_ref[...] = jnp.where(chosen, rank, -1.0)
    slot_ids = lax.broadcasted_iota(jnp.int32, (width, rows_dev), 0).astype(F32)
    place_ref[...] = jnp.zeros_like(place_ref)
    total = jnp.zeros((6 * devices, width), F32)
    for s in range(spread):
        slot = jnp.sum(jnp.where(named[s], rank, 0.0), axis=0, keepdims=True)
        place_ref[s : s + 1, :] = owner_ref[s : s + 1, :].astype(F32) * slots + slot
        weight = weight_ref[s : s + 1, :]
        place_ref[spread + s : spread + s + 1, :] = weight
        code = weight * TOP
        whole_code = jnp.round(code)
        rest_code = jnp.round((code - whole_code) * REST)
        fields = split(row_ref[s : s + 1, :].astype(F32)) + split(whole_code) + split(rest_code)
        lhs = jnp.concatenate([jnp.where(named[s], f, 0.0) for f in fields], axis=0).astype(LOW)
        total = total + dot(lhs, jnp.where(slot_ids == slot, 1.0, 0.0).astype(LOW), 1, 1)
    for i in range(3):
        high = total[2 * i * devices : (2 * i + 1) * devices]
        low = total[(2 * i + 1) * devices : (2 * i + 2) * devices]
        side_ref[i] = 256.0 * high + low


def spread_kernel(
    slots,
    owner_ref,
    row_ref,
    weight_ref,
    basis_hbm,
    out_ref,
    place_ref,
    vector_ref,
    rank_ref,
    side_ref,
    code_ref,
    level_ref,
    pick_ref,
    vector_sem,
):
    step = pl.program_id(0)
    columns = vector_ref.shape[1]

    @pl.when(step == 0)
    def _():
        copy = pltpu.make_async_copy(basis_hbm.at[basis_hbm.shape[0] - 1], vector_ref, vector_sem)
        copy.start()
        find_routes(slots, owner_ref, row_ref, weight_ref, rank_ref, side_ref, place_ref)
        copy.wait()
        vector = vector_ref[...]
        peak = jnp.maximum(jnp.max(jnp.abs(vector), axis=0, keepdims=True), 1e-30)
        level = jnp.floor(jnp.log(peak) * (1.0 / LOG2)) + 1.0
        level_ref[...] = level
        code = jnp.clip(jnp.round(vector * (TOP / jnp.exp(level * LOG2))), -TOP, TOP)
        high, low = split(code)
        code_ref[:, :columns] = high.astype(LOW)
        code_ref[:, columns:] = low.astype(LOW)

    rows_dev = rank_ref.shape[1]
    owners = SPREAD_BLOCK // slots
    slot_ids = lax.broadcasted_iota(jnp.int32, (slots, rows_dev), 0).astype(F32)
    for j in range(owners):
        rank = rank_ref[pl.ds(step * owners + j, 1), :]
        pick_ref[j * slots : (j + 1) * slots, :] = jnp.where(slot_ids == rank, 1.0, 0.0).astype(LOW)
    picked = dot(pick_ref[...], code_ref[...])
    codes = (256.0 * picked[:, :columns] + picked[:, columns:]).astype(jnp.int32).astype(CODE)
    line = lax.broadcasted_iota(jnp.int32, (8, LANES), 0)
    parts = columns // LANES
    for j in range(owners):
        extra = jnp.zeros((8, LANES), F32)
        for k in range(3):
            extra = jnp.where(line == k, side_ref[k, pl.ds(step * owners + j, 1), :], extra)
        for h in range(parts):
            at = slice(h * LANES, (h + 1) * LANES)
            extra = jnp.where(line == 3 + h, level_ref[:, at], extra)
            out_ref[j, h * slots : (h + 1) * slots, :] = codes[j * slots : (j + 1) * slots, at]
        out_ref[j, parts * slots :, :] = extra.astype(jnp.int32).astype(CODE)


def spread_out(owner_t, row_t, weight_t, basis, devices, slots):
    rows_dev, columns = basis.shape[1:]
    owners = SPREAD_BLOCK // slots
    shape = (devices, columns // LANES * slots + 8, LANES)
    return pl.pallas_call(
        functools.partial(spread_kernel, slots),
        grid=(devices // owners,),
        in_specs=[
            whole(owner_t.shape),
            whole(row_t.shape),
            whole(weight_t.shape),
            pl.BlockSpec(memory_space=pltpu.HBM),
        ],
        out_specs=(
            pl.BlockSpec((owners,) + shape[1:], lambda i: (i, 0, 0)),
            whole((8, rows_dev)),
        ),
        out_shape=(in_hbm(shape, CODE), in_hbm((8, rows_dev), F32)),
        scratch_shapes=[
            pltpu.VMEM((rows_dev, columns), F32),
            pltpu.VMEM((devices, rows_dev), F32),
            pltpu.VMEM((3, devices, LANES), F32),
            pltpu.VMEM((rows_dev, 2 * columns), LOW),
            pltpu.VMEM((1, columns), F32),
            pltpu.VMEM((SPREAD_BLOCK, rows_dev), LOW),
            pltpu.SemaphoreType.DMA,
        ],
        compiler_params=params(("arbitrary",)),
        cost_estimate=cost(4 * devices * slots * rows_dev * columns, 4 << 20),
        name="spread_out",
    )(owner_t, row_t, weight_t, basis)


def add_slots(slots, low_part, got_ref, rows_ref, sum_ref, picks, terms):
    rows_dev, width = sum_ref.shape
    owners = COLLECT_BLOCK // slots
    parts = width // LANES
    blocks = got_ref.shape[0] // owners
    tile = 16
    ids = lax.broadcasted_iota(jnp.int32, (rows_dev, slots), 0).astype(CODE)
    one, zero = jnp.ones((rows_dev, slots), LOW), jnp.zeros((rows_dev, slots), LOW)

    def build(block):
        pick_ref, term_ref = picks[block % 2], terms[block % 2]
        for j in range(owners):
            at = slice(j * slots, (j + 1) * slots)
            source = block * owners + j
            extra = got_ref[source, parts * slots :, :].astype(jnp.int32)
            row = jnp.broadcast_to(extra[0:1, :slots], (tile, slots)).astype(CODE)
            row = jnp.broadcast_to(row[None], (rows_dev // tile, tile, slots))
            pick_ref[:, at] = jnp.where(ids == row.reshape(rows_dev, slots), one, zero)
            extra = extra.astype(F32)
            weight = (extra[1:2, :slots] + extra[2:3, :slots] * (1.0 / REST)) * (1.0 / TOP)
            weight = column(weight)
            if rows_ref is not None:
                rows_ref[source : source + 1, :] = extra[0:1, :]
            for h in range(parts):
                scale = jnp.exp(extra[3 + h : 4 + h, :] * LOG2) * (1.0 / TOP)
                codes = got_ref[source, h * slots : (h + 1) * slots, :].astype(jnp.int32).astype(F32)
                values = codes * weight * scale
                term = values.astype(LOW)
                if low_part:
                    term = (values - term.astype(F32)).astype(LOW)
                term_ref[at, h * LANES : (h + 1) * LANES] = term

    build(0)
    for block in range(blocks):
        if block + 1 < blocks:
            build(block + 1)
        added = dot(picks[block % 2][...], terms[block % 2][...])
        sum_ref[...] = added if block == 0 else sum_ref[...] + added


def rise_kernel(base_ref, gram_ref, out_ref):
    for l in range(base_ref.shape[0]):
        base = base_ref[l]
        out_ref[l] = (base.astype(F32) + dot(base, gram_ref[l], 1, 1)).astype(LOW)


def rise(base, gram):
    return pl.pallas_call(
        rise_kernel,
        out_shape=in_vmem(base.shape, LOW),
        compiler_params=params(mib=8),
        cost_estimate=cost(2 * gram.size * base.shape[1], 2 * gram.size),
        name="rise",
    )(base, gram)


def collect_kernel(
    slots,
    got_ref,
    rise_ref,
    ascend_ref,
    dual_ref,
    coeff_ref,
    rows_ref,
    pick_a,
    pick_b,
    term_a,
    term_b,
):
    add_slots(slots, False, got_ref, rows_ref, dual_ref, (pick_a, pick_b), (term_a, term_b))
    leaves, rank, leaf = rise_ref.shape
    for b in range(coeff_ref.shape[0]):
        coeff_ref[b, leaves * rank :, :] = ascend_ref[...]
    for l in range(leaves):
        dual = dual_ref[l * leaf : (l + 1) * leaf, :]
        coeff = dot(rise_ref[l], dual.astype(LOW)).astype(LOW)
        for b in range(coeff_ref.shape[0]):
            coeff_ref[b, l * rank : (l + 1) * rank, :] = coeff


def slot_scratch(rows_dev, width):
    return [
        pltpu.VMEM((rows_dev, COLLECT_BLOCK), LOW),
        pltpu.VMEM((rows_dev, COLLECT_BLOCK), LOW),
        pltpu.VMEM((COLLECT_BLOCK, width), LOW),
        pltpu.VMEM((COLLECT_BLOCK, width), LOW),
    ]


def collect(got, lift, ascend, slots, branches, width):
    devices = got.shape[0]
    leaves, rank, leaf = lift.shape
    rows_dev = leaves * leaf
    sent_rows = leaves * rank + ascend.shape[0]
    direct = pl.BlockSpec(memory_space=pltpu.VMEM)
    return pl.pallas_call(
        functools.partial(collect_kernel, slots),
        in_specs=[direct] * 3,
        out_specs=[direct] * 3,
        out_shape=(
            in_vmem((rows_dev, width), F32),
            in_hbm((branches, sent_rows, width), LOW),
            in_hbm((devices, LANES), F32),
        ),
        scratch_shapes=slot_scratch(rows_dev, width),
        compiler_params=params(),
        cost_estimate=cost(2 * devices * slots * rows_dev * width, 4 << 20),
        name="collect",
    )(got, lift, ascend)


def refine_kernel(
    slots,
    got_ref,
    dual_ref,
    gram_hbm,
    out_ref,
    sum_ref,
    gram_ref,
    gram_sem,
    pick_a,
    pick_b,
    term_a,
    term_b,
):
    gram_copy = pltpu.make_async_copy(gram_hbm, gram_ref, gram_sem)
    gram_copy.start()
    add_slots(slots, True, got_ref, None, sum_ref, (pick_a, pick_b), (term_a, term_b))
    gram_copy.wait()
    leaves, leaf = gram_ref.shape[:2]
    for l in range(leaves):
        at = slice(l * leaf, (l + 1) * leaf)
        dual = dual_ref[at, :] + sum_ref[at, :]
        out_ref[at, :] = dual + dot(gram_ref[l], dual.astype(LOW), 0, 0)


def refine(got, dual, gram, slots):
    rows_dev, width = dual.shape
    devices = got.shape[0]
    direct = pl.BlockSpec(memory_space=pltpu.VMEM)
    return pl.pallas_call(
        functools.partial(refine_kernel, slots),
        in_specs=[direct, direct, pl.BlockSpec(memory_space=pltpu.HBM)],
        out_specs=direct,
        out_shape=in_vmem(dual.shape, F32),
        scratch_shapes=[
            pltpu.VMEM((rows_dev, width), F32),
            pltpu.VMEM(gram.shape, LOW),
            pltpu.SemaphoreType.DMA,
        ]
        + slot_scratch(rows_dev, width),
        compiler_params=params(),
        cost_estimate=cost(2 * devices * slots * rows_dev * width, 4 << 20),
        name="refine",
    )(got, dual, gram)


def parent_kernel(coeff_ref, out_ref):
    rank, width = out_ref.shape
    branches, rows = coeff_ref.shape[:2]
    parts = width // rank
    leaves = rows * parts // (rank * (parts + 1))
    held = leaves * rank // parts
    sums = [jnp.zeros((held, width), F32) for _ in range(rank // held)]
    for b in range(branches):
        packed = coeff_ref[b, leaves * rank :, :]
        for q in range(parts):
            leaf, at = divmod(q * held, rank)
            term = dot(
                packed[:, q * rank : (q + 1) * rank], coeff_ref[b, leaf * rank : (leaf + 1) * rank, :]
            )
            sums[at // held] = sums[at // held] + term
    for i, total in enumerate(sums):
        out_ref[i * held : (i + 1) * held, :] = total.astype(LOW)


def parent_of(coeff, rank):
    width = coeff.shape[2]
    return pl.pallas_call(
        parent_kernel,
        out_shape=in_vmem((rank, width), LOW),
        compiler_params=params(mib=6),
        cost_estimate=cost(2 * coeff.size * rank, 1 << 20),
        name="parent_of",
    )(coeff)


def far_kernel(list_ref, coeff_ref, block_ref, out_ref):
    leaves, items, rank = block_ref.shape[:3]
    for l in range(leaves):
        total = jnp.zeros(out_ref.shape[1:], F32)
        for k in range(items):
            source = list_ref[l, k]
            at = pl.ds(pl.multiple_of(source % leaves * rank, rank), rank)
            total = total + dot(block_ref[l, k], coeff_ref[source // leaves, at, :])
        out_ref[l] = total


def far_field(far_list, coeff, far_block):
    leaves, items, rank = far_block.shape[:3]
    width = coeff.shape[2]
    return pl.pallas_call(
        far_kernel,
        grid_spec=pltpu.PrefetchScalarGridSpec(
            num_scalar_prefetch=1,
            grid=(1,),
            in_specs=[whole(coeff.shape), whole(far_block.shape)],
            out_specs=whole((leaves, rank, width)),
        ),
        out_shape=jax.ShapeDtypeStruct((leaves, rank, width), F32),
        compiler_params=params(("arbitrary",), 6),
        cost_estimate=cost(2 * far_block.size * width, 1 << 20),
        name="far_field",
    )(far_list, coeff, far_block)


def near_kernel(list_ref, block_ref, first_ref, out_ref, low_ref):
    leaf, item = pl.program_id(0), pl.program_id(1)
    size = out_ref.shape[0]

    @pl.when((leaf == 0) & (item == 0))
    def _():
        for l in range(low_ref.shape[0]):
            low_ref[l] = first_ref[l * size : (l + 1) * size, :].astype(LOW)

    count = block_ref.shape[1]
    term = dot(block_ref[0, 0], low_ref[list_ref[leaf, item * count]])
    for k in range(1, count):
        term = term + dot(block_ref[0, k], low_ref[list_ref[leaf, item * count + k]])

    @pl.when(item == 0)
    def _():
        out_ref[...] = first_ref[pl.ds(pl.multiple_of(leaf * size, size), size), :] + term

    @pl.when(item > 0)
    def _():
        out_ref[...] += term


def near_field(near_list, near_block, first):
    leaves, items, leaf = near_block.shape[:3]
    width = first.shape[1]
    count = 4 if items % 4 == 0 else 1
    return pl.pallas_call(
        near_kernel,
        grid_spec=pltpu.PrefetchScalarGridSpec(
            num_scalar_prefetch=1,
            grid=(leaves, items // count),
            in_specs=[
                pl.BlockSpec((1, count, leaf, leaf), lambda l, k, _: (l, k, 0, 0)),
                whole(first.shape),
            ],
            out_specs=pl.BlockSpec((leaf, width), lambda l, k, _: (l, 0)),
            scratch_shapes=[pltpu.VMEM((leaves, leaf, width), LOW)],
        ),
        out_shape=in_vmem(first.shape, F32),
        compiler_params=params(("arbitrary", "arbitrary"), 12),
        cost_estimate=cost(2 * near_block.size * width, 2 * near_block.size),
        name="near_field",
    )(near_list, near_block, first)


def prepare_kernel(image_ref, base_ref, gram_ref, dual_ref, lift_ref):
    leaves, leaf = gram_ref.shape[:2]
    ids = lax.broadcasted_iota(jnp.int32, (leaf, leaf), 0)
    same = ids == lax.broadcasted_iota(jnp.int32, (leaf, leaf), 1)
    unit = jnp.where(same, 1.0, 0.0).astype(LOW)
    for l in range(leaves):
        at = slice(l * leaf, (l + 1) * leaf)
        image = image_ref[at, :]
        dual_ref[at, :] = image + dot(gram_ref[l], image.astype(LOW))
        lifted = dot(unit, base_ref[l], 1, 1) + dot(gram_ref[l], base_ref[l], 1, 1)
        parts = [lifted if i == l else jnp.zeros_like(lifted) for i in range(leaves)]
        lift_ref[at, :] = jnp.concatenate(parts, axis=1).astype(LOW)


def prepare(image, base, gram):
    rows_dev, width = image.shape
    lanes = base.shape[0] * base.shape[1]
    return pl.pallas_call(
        prepare_kernel,
        out_shape=(in_vmem((rows_dev, width), F32), in_vmem((rows_dev, lanes), LOW)),
        compiler_params=params(mib=12),
        cost_estimate=cost(2 * gram.size * (width + 2 * lanes), 4 << 20),
        name="prepare",
    )(image, base, gram)


def reply_kernel(slots, *refs):
    dual_ref, lift_ref, far_ref, top_ref, descend_ref, rows_ref = refs[:6]
    parents, rest = refs[6:-7], refs[-7:]
    out_hbm, field_ref, low_ref, pick_a, pick_b, ready_ref, sems = rest
    picks = (pick_a, pick_b)
    owners = REPLY_BLOCK // slots
    blocks = ready_ref.shape[0] // REPLY_BLOCK
    ids = lax.broadcasted_iota(jnp.int32, (slots, low_ref.shape[0]), 1).astype(F32)

    def build(block):
        for j in range(owners):
            source = block * owners + j
            row = column(rows_ref[source : source + 1, :][:, :slots])
            pick = jnp.where(ids == row, 1.0, 0.0).astype(LOW)
            picks[block % 2][j * slots : (j + 1) * slots, :] = pick

    build(0)
    leaves, rank = far_ref.shape[:2]
    field = dot(top_ref[0], parents[0][...])
    for k in range(1, len(parents)):
        field = field + dot(top_ref[k], parents[k][...])
    field = field.astype(LOW)
    for l in range(leaves):
        descent = far_ref[l] + dot(descend_ref[l], field)
        field_ref[l * rank : (l + 1) * rank, :] = descent.astype(LOW)
    low_ref[...] = (dual_ref[...] + dot(lift_ref[...], field_ref[...])).astype(LOW)
    copies = []
    for block in range(blocks):
        if block + 1 < blocks:
            build(block + 1)
        at = pl.ds(block * REPLY_BLOCK, REPLY_BLOCK)
        ready_ref[at, :] = dot(picks[block % 2][...], low_ref[...]).astype(LOW)
        copies.append(pltpu.make_async_copy(ready_ref.at[at], out_hbm.at[at], sems.at[block]))
        copies[-1].start()
    for copy in copies:
        copy.wait()


def reply(dual, lift, far, top, parents, descend, rows, slots):
    rows_dev, width = dual.shape
    total = rows.shape[0] * slots
    args = (dual, lift, far, top, descend, rows, *parents)
    direct = pl.BlockSpec(memory_space=pltpu.VMEM)
    return pl.pallas_call(
        functools.partial(reply_kernel, slots),
        in_specs=[direct] * len(args),
        out_specs=pl.BlockSpec(memory_space=pltpu.HBM),
        out_shape=in_hbm((total, width), LOW),
        scratch_shapes=[
            pltpu.VMEM((lift.shape[1], width), LOW),
            pltpu.VMEM((rows_dev, width), LOW),
            pltpu.VMEM((REPLY_BLOCK, rows_dev), LOW),
            pltpu.VMEM((REPLY_BLOCK, rows_dev), LOW),
            pltpu.VMEM((total, width), LOW),
            pltpu.SemaphoreType.DMA((total // REPLY_BLOCK,)),
        ],
        compiler_params=params(mib=16),
        cost_estimate=cost(2 * total * rows_dev * width, 4 << 20),
        name="reply",
    )(*args)


def gather_kernel(spread, ret_ref, place_ref, basis_ref, mutual_ref, image_ref, sums_ref, pick_a, pick_b):
    picks = (pick_a, pick_b)
    total, width = ret_ref.shape
    krylov = basis_ref.shape[0]
    blocks = image_ref.shape[0] // GATHER_BLOCK
    ids = lax.broadcasted_iota(jnp.int32, (GATHER_BLOCK, total), 1).astype(F32)

    def build(block):
        at = slice(block * GATHER_BLOCK, (block + 1) * GATHER_BLOCK)
        for s in range(spread):
            pick = jnp.where(ids == place_ref[at, s : s + 1], 1.0, 0.0).astype(LOW)
            picks[block % 2][s * GATHER_BLOCK : (s + 1) * GATHER_BLOCK, :] = pick

    build(0)
    sums = [jnp.zeros((1, width), F32) for _ in range(krylov + 1)]
    for block in range(blocks):
        if block + 1 < blocks:
            build(block + 1)
        at = slice(block * GATHER_BLOCK, (block + 1) * GATHER_BLOCK)
        picked = dot(picks[block % 2][...], ret_ref[...])
        image = jnp.zeros((GATHER_BLOCK, width), F32)
        for s in range(spread):
            weight = place_ref[at, spread + s : spread + s + 1]
            image = image + weight * picked[s * GATHER_BLOCK : (s + 1) * GATHER_BLOCK, :]
        image_ref[at, :] = image
        for k in range(krylov):
            sums[k] = sums[k] + jnp.sum(basis_ref[k, at, :] * image, axis=0, keepdims=True)
        sums[krylov] = sums[krylov] + jnp.sum(image * image, axis=0, keepdims=True)
    sums_ref[: krylov + 1, :] = jnp.concatenate(sums, axis=0)
    sums_ref[krylov + 1 :, :] = mutual_ref[...]


def gather_back(ret, place_col, basis, mutual, spread):
    total, width = ret.shape
    krylov, rows_dev = basis.shape[:2]
    lines = krylov + 1 + mutual.shape[0]
    direct = pl.BlockSpec(memory_space=pltpu.VMEM)
    return pl.pallas_call(
        functools.partial(gather_kernel, spread),
        in_specs=[direct] * 4,
        out_specs=[direct] * 2,
        out_shape=(
            jax.ShapeDtypeStruct((rows_dev, width), F32),
            jax.ShapeDtypeStruct((lines, width), F32),
        ),
        scratch_shapes=[
            pltpu.VMEM((spread * GATHER_BLOCK, total), LOW),
            pltpu.VMEM((spread * GATHER_BLOCK, total), LOW),
        ],
        compiler_params=params(),
        cost_estimate=cost(2 * spread * total * rows_dev * width, 6 << 20),
        name="gather_back",
    )(ret, place_col, basis, mutual)


def finish_kernel(groups, total_rows, sums_ref, image_ref, basis_ref, next_hbm, column_ref, ready_ref, sems):
    krylov, rows_dev, width = basis_ref.shape
    devices, lines = sums_ref.shape[:2]
    share = lines - krylov - 1
    whole_sum = jnp.sum(sums_ref[...], axis=0)
    projection = [whole_sum[k : k + 1, :] * (1.0 / total_rows) for k in range(krylov)]
    square = whole_sum[krylov : krylov + 1, :] * (1.0 / total_rows)
    for part in projection:
        square = square - 2.0 * part * part
    pairs = [(i, j) for i in range(krylov) for j in range(i, krylov)]
    for at, (i, j) in enumerate(pairs):
        line = krylov + 1 + at % share
        mutual = jnp.zeros((1, width), F32)
        for d in range(at // share, devices, groups):
            mutual = mutual + sums_ref[d, line : line + 1, :]
        times = (1.0 if i == j else 2.0) / total_rows
        square = square + times * projection[i] * projection[j] * mutual
    scale = jnp.sqrt(jnp.maximum(square, 0.0) + 1e-06)
    column_ref[...] = jnp.concatenate(projection + [scale], axis=0)
    inverse = 1.0 / scale
    size = rows_dev // sems.shape[0]
    copies = []
    for block in range(sems.shape[0]):
        at = pl.ds(block * size, size)
        remainder = image_ref[at, :]
        for k in range(krylov):
            remainder = remainder - projection[k] * basis_ref[k, at, :]
        ready_ref[at, :] = remainder * inverse
        copies.append(pltpu.make_async_copy(ready_ref.at[at], next_hbm.at[at], sems.at[block]))
        copies[-1].start()
    for copy in copies:
        copy.wait()


def finish(sums, image, basis, groups, total_rows):
    krylov, rows_dev, width = basis.shape
    direct = pl.BlockSpec(memory_space=pltpu.VMEM)
    return pl.pallas_call(
        functools.partial(finish_kernel, groups, total_rows),
        in_specs=[direct] * 3,
        out_specs=(pl.BlockSpec(memory_space=pltpu.HBM), direct),
        out_shape=(
            in_hbm((rows_dev, width), F32),
            jax.ShapeDtypeStruct((krylov + 1, width), F32),
        ),
        scratch_shapes=[pltpu.VMEM((rows_dev, width), F32), pltpu.SemaphoreType.DMA((4,))],
        compiler_params=params(mib=8),
        cost_estimate=cost(8 * rows_dev * width, 4 << 20),
        name="finish",
    )(sums, image, basis)


AXES = ("branch", "group")


def exchange(values, axes=AXES):
    return lax.all_to_all(values, axes, split_axis=0, concat_axis=0, tiled=True)


def swaps(values, axis):
    size = lax.axis_size(axis)
    return [values] + [
        lax.ppermute(values, axis, [(i, i ^ k) for i in range(size)]) for k in range(1, size)
    ]


def to_all(values, axes, size):
    return exchange(jnp.broadcast_to(values[None], (size,) + values.shape), axes)


def body(
    basis,
    spread_owner,
    spread_row,
    spread_weight,
    gram_term,
    near_block,
    near_list,
    leaf_basis,
    far_block,
    far_list,
    ascend,
    descend,
    top_block,
):
    branches = lax.axis_size("branch")
    groups = lax.axis_size("group")
    devices = branches * groups
    rows_dev, columns = basis.shape[1:]
    krylov = basis.shape[0]
    spread = spread_owner.shape[1]
    slots = 2 * spread * rows_dev // devices
    total = devices * slots
    leaves, rank = leaf_basis.shape[:2]
    sent, place = spread_out(
        kept(spread_owner.T), kept(spread_row.T), kept(spread_weight.T), kept(basis), devices, slots
    )
    sent, late_ascend, late_top, late_base, late_gram = lax.optimization_barrier(
        (sent, ascend, top_block, leaf_basis, gram_term)
    )
    got = exchange(sent)

    parts = columns // rank
    held = leaves * rank // parts
    packed = late_ascend.reshape(parts, held, rank).transpose(1, 0, 2).reshape(held, columns)
    columns_of = (jnp.arange(groups) ^ lax.axis_index("group")) % groups
    top = late_top.reshape(rank, groups, rank).transpose(1, 0, 2)[columns_of]

    raised = rise(late_base, late_gram)
    got, packed, top, raised = lax.optimization_barrier((got, packed, top, raised))
    dual, coeff, rows = collect(got, raised, packed, slots, branches, columns)
    coeff = kept(exchange(coeff, "branch"))
    first = refine(got, dual, kept(gram_term), slots)
    image = near_field(near_list, kept(near_block), first)
    dual, lift = prepare(image, kept(leaf_basis), kept(gram_term))
    coeff, dual, lift = lax.optimization_barrier((coeff, dual, lift))
    parents = swaps(parent_of(coeff, rank), "group")
    far = far_field(far_list, coeff, kept(far_block))
    replies = reply(dual, lift, far, kept(top), parents, kept(descend), kept(rows), slots)
    returned = exchange(replies.reshape(devices, slots, columns)).reshape(total, columns)
    pairs = [(i, j) for i in range(krylov) for j in range(i, krylov)]
    mutual = jnp.stack([jnp.sum(basis[i] * basis[j], axis=0) for i, j in pairs])
    mutual = sum(swaps(mutual, "group"))
    share = -(-len(pairs) // groups)
    mutual = jnp.pad(mutual, ((0, share * groups - len(pairs)), (0, 0)))
    own = lax.dynamic_slice_in_dim(mutual, share * lax.axis_index("group"), share, 0)
    primal, sums = gather_back(near_by(returned), kept(place.T), basis, own, spread)
    everyone = to_all(sums, AXES, devices)
    return finish(everyone, primal, basis, groups, rows_dev * devices)


def solution(mesh):
    both = ("branch", "group")
    return jax.shard_map(
        body,
        mesh=mesh,
        in_specs=(
            P(None, both, None),
            P(both, None),
            P(both, None),
            P(both, None),
            P(both, None, None),
            P(both, None, None, None),
            P(both, None),
            P(both, None, None),
            P(both, None, None, None),
            P(both, None),
            P(both, None, None),
            P(both, None, None),
            P("group", None),
        ),
        out_specs=(P(both, None), P()),
        check_vma=False,
    )
```
